32 devices in a mesh: dp: 2 (over core), ctx: 4 (over y, x), hd: 4 (over z).
Axes of the slice: x: 2, y: 2, z: 4, core: 2. Of those that a mesh axis runs over, the one named last changes fastest.
Arguments:
- tokens_in: bfloat16 [4, 2048, 1536], P('dp', ('ctx', 'hd')), may hold values from -6 to 6
- seg_ids: int32 [4, 2048], P('dp'), may hold values from 0 to 7, never falling along the last dimension, each value on 1 to 512 neighbouring positions
- in_norm: float32 [1536], replicated, may hold values from 0.5 to 1.5
- z_proj: bfloat16 [1536, 3072], P(('dp', 'ctx', 'hd')), may hold values from -0.15625 to 0.15625
- xbc_proj: bfloat16 [1536, 3328], P(('dp', 'ctx', 'hd')), may hold values from -0.15625 to 0.15625
- dt_proj: bfloat16 [1536, 48], P(('dp', 'ctx', 'hd')), may hold values from -0.0390625 to 0.0390625
- conv_taps: float32 [4, 3328], replicated, may hold values from -3 to 3
- conv_bias: float32 [3328], replicated, may hold values from -2 to 2
- dt_bias: float32 [48], replicated, may hold values from -9 to -2
- a_log: float32 [48], replicated, may hold values from 0 to 2.77
- d_skip: float32 [48], replicated, may hold values from 0.5 to 2
- gate_norm: float32 [3072], replicated, may hold values from 0.5 to 1.5
- out_proj: bfloat16 [3072, 1536], P(('dp', 'ctx', 'hd')), may hold values from -0.109375 to 0.109375
- out_cotangent: bfloat16 [4, 2048, 1536], P('dp', ('ctx', 'hd')), may hold values from -6 to 6
Outputs:
- layer_out: bfloat16 [4, 2048, 1536], P('dp', ('ctx', 'hd'))
- tokens_grad: float32 [4, 2048, 1536], P('dp', ('ctx', 'hd'))
- in_norm_grad: float32 [1536], replicated
- z_proj_grad: float32 [1536, 3072], P(('dp', 'ctx', 'hd'))
- xbc_proj_grad: float32 [1536, 3328], P(('dp', 'ctx', 'hd'))
- dt_proj_grad: float32 [1536, 48], P(('dp', 'ctx', 'hd'))
- conv_taps_grad: float32 [4, 3328], replicated
- conv_bias_grad: float32 [3328], replicated
- dt_bias_grad: float32 [48], replicated
- a_log_grad: float32 [48], replicated
- d_skip_grad: float32 [48], replicated
- gate_norm_grad: float32 [3072], replicated
- out_proj_grad: float32 [3072, 1536], P(('dp', 'ctx', 'hd'))
The draws below stay inside these ranges and needn't reach their ends.
Inputs may be any that keep to these rules, and one draw needn't show every extreme that they name: `seg_ids`: along each sequence the document numbers never fall; each document has 1 to 512 tokens and one has exactly that many.
All inputs are finite; a program needn't handle non-finite values.
Results may differ from the reference program's by a relative error of at most 0.0097.
Values may be sent and summed in bfloat16 or wider, within the bound.
No kernel may reach another device: no remote copies, remote signals or barrier semaphores. Data moves between devices by JAX's collectives and lax.ppermute only.
A program may use at most 320 MiB of HBM per device.

```python
import math
from functools import partial
import jax
import jax.numpy as jnp
import numpy as np
from jax import lax

D = 1536
H = 48
P_SIZE = 64
N = 128
KW = 4
Q = 256
DI = 3072
L = 2048
SEQS = 4


def level_of(rng, dims, split, smallest, largest):
    def one(axis_at, shards_of):
        heights = jax.random.uniform(jax.random.fold_in(jax.random.fold_in(rng, 6), axis_at), (shards_of,), jnp.float32, smallest / len(split), largest / len(split))
        return jnp.repeat(jnp.exp(heights), dims[axis_at] // shards_of).reshape((-1,) + (1,) * (len(dims) - axis_at - 1))

    loudness = one(*split[0])
    for cut in split[1:]:
        loudness = loudness * one(*cut)
    return loudness


def profile(amount, total, bound, skew):
    weights = [(1 << 20) // math.isqrt(standing ** skew) + 1 for standing in range(2, amount + 1)]
    spare, counts = total - bound - (amount - 1), [1] * (amount - 1)
    while spare > 0:
        movable = [i for i in range(amount - 1) if counts[i] < bound]
        whole, remaining = sum([weights[i] for i in movable]), spare
        for i in movable:
            extra = min(bound - counts[i], max(1, remaining * weights[i] // whole), spare)
            counts[i] = counts[i] + extra
            spare = spare - extra
    return np.array([bound] + counts)


def ragged_sizes(own_key, amount, total, limit, skew):
    if amount == 2:
        one = jax.random.randint(own_key, (), max(1, total - limit), min(limit, total - 1) + 1)
        return jnp.stack([one, total - one])
    tallies = jnp.asarray(profile(amount, total, limit, skew), jnp.int32)
    pairs = (amount - 1) // 2
    giver, taker = tallies[1:1 + 2 * pairs:2], tallies[2:2 + 2 * pairs:2]
    slack = jnp.minimum(giver - 1, limit - taker)
    passed = jax.random.randint(jax.random.fold_in(own_key, 1), (pairs,), 0, 1 << 20) % (slack + 1)
    tallies = tallies.at[1:1 + 2 * pairs:2].set(giver - passed).at[2:2 + 2 * pairs:2].set(taker + passed)
    return tallies[jax.random.permutation(jax.random.fold_in(own_key, 2), amount)]


def noise(stream_key, dims, scale, bound, shards=(), held_as=jnp.bfloat16):
    values = jax.random.normal(stream_key, dims, jnp.float32) * scale
    if len(shards) > 0:
        values = level_of(stream_key, dims, shards, -0.22, 0.18) * values
    return jnp.clip(values, min=-bound, max=bound).astype(held_as)


def setup_inputs(seed: int = 0) -> dict:
    keys = jax.random.split(jax.random.key(seed), 15)
    tokens_in = noise(keys[0], (SEQS, L, D), 1.0, 6.0, ((0, 2), (1, 16)))
    seg_ids = jax.vmap(lambda own: jnp.searchsorted(jnp.cumsum(ragged_sizes(own, max(L // 256, 8), L, L // 4, 2)), jnp.arange(L), side="right"))(jax.random.split(keys[1], SEQS)).reshape((SEQS, L)).astype(jnp.int32)
    in_norm = jnp.clip(1.0 + 0.1 * jax.random.normal(keys[2], (D,), jnp.float32), 0.5, 1.5)
    z_proj = noise(keys[3], (D, DI), D ** -0.5, 0.15625, ((0, 32),))
    xbc_proj = noise(keys[4], (D, DI + 2 * N), D ** -0.5, 0.15625, ((0, 32),))
    dt_proj = noise(keys[5], (D, H), (16 * D) ** -0.5, 0.0390625, ((0, 32),))
    conv_taps = noise(keys[6], (KW, DI + 2 * N), 0.5, 3.0, (), jnp.float32)
    conv_bias = noise(keys[7], (DI + 2 * N,), 0.3, 2.0, (), jnp.float32)
    dt_bias = jnp.clip(jax.random.uniform(keys[8], (H,), jnp.float32, -9.0, -2.0), -9.0, -2.0)
    a_log = jnp.clip(jax.random.uniform(keys[9], (H,), jnp.float32, 0.0, 2.77), 0.0, 2.77)
    d_skip = jnp.clip(jnp.exp(jax.random.uniform(keys[10], (H,), jnp.float32, math.log(0.5), math.log(2.0))), 0.5, 2.0)
    gate_norm = jnp.clip(1.0 + 0.1 * jax.random.normal(keys[11], (DI,), jnp.float32), 0.5, 1.5)
    out_proj = noise(keys[12], (DI, D), DI ** -0.5, 0.109375, ((0, 32),))
    out_cotangent = noise(keys[13], (SEQS, L, D), 1.0, 6.0, ((0, 2), (1, 16)))
    return dict(tokens_in=tokens_in, seg_ids=seg_ids, in_norm=in_norm, z_proj=z_proj, xbc_proj=xbc_proj, dt_proj=dt_proj, conv_taps=conv_taps, conv_bias=conv_bias, dt_bias=dt_bias, a_log=a_log, d_skip=d_skip, gate_norm=gate_norm, out_proj=out_proj, out_cotangent=out_cotangent)


HIGH = lax.Precision.HIGHEST
EPS = 1e-05

@jax.custom_vjp
def low(v):
    return lax.optimization_barrier(v.astype(jnp.bfloat16)).astype(jnp.float32)

@jax.custom_vjp
def low_back(v):
    return v

def low_keep(v):
    return (low(v), None)

def low_pass(kept, grad):
    return (grad,)

def back_keep(v):
    return (v, None)

def back_low(kept, grad):
    return (low(grad),)
low.defvjp(low_keep, low_pass)
low_back.defvjp(back_keep, back_low)

def norm_rows(values, gain):
    return values * lax.rsqrt(lax.optimization_barrier(jnp.mean(values * values, axis=-1, keepdims=True)) + EPS) * gain

def group_step(neg_rate, carry, piece):
    state, seg_last = carry
    x_group, dt_group, b_group, c_group, seg_group = piece
    cumul = jnp.cumsum(dt_group * neg_rate, axis=0)
    order = jnp.arange(seg_group.shape[0])
    mask = (seg_group[:, None] == seg_group[None, :]) & (order[:, None] >= order[None, :])
    gaps = cumul[:, None, :] - cumul[None, :, :]
    decay = jnp.exp(jnp.where(mask[:, :, None], gaps, 0.0)) * mask[:, :, None].astype(jnp.float32)
    scores = jnp.dot(c_group, b_group.T, precision=HIGH)
    mix_w = scores[:, :, None] * decay * dt_group[None, :, :]
    y_part = jnp.einsum('tsh,shp->thp', mix_w, x_group, precision=HIGH)
    keep = (seg_group == seg_last).astype(jnp.float32)
    lead = jnp.exp(cumul) * keep[:, None]
    y_part = y_part + lead[:, :, None] * jnp.einsum('tn,hpn->thp', c_group, state, precision=HIGH)
    tail = jnp.exp(cumul[-1][None, :] - cumul) * (seg_group == seg_group[-1]).astype(jnp.float32)[:, None] * dt_group
    new_state = state * lead[-1][:, None, None] + jnp.einsum('sh,shp,sn->hpn', tail, x_group, b_group, precision=HIGH)
    return ((new_state, seg_group[-1]), y_part)

def mixer(x_heads, rates, b_part, c_part, seg_row, neg_rate):
    length = x_heads.shape[0]
    count = length // Q
    stepper = jax.checkpoint(partial(group_step, neg_rate))
    start = (jnp.zeros((H, P_SIZE, N), jnp.float32), seg_row[0])
    pieces = (x_heads.reshape(count, Q, H, P_SIZE), rates.reshape(count, Q, H), b_part.reshape(count, Q, N), c_part.reshape(count, Q, N), seg_row.reshape(count, Q))
    unused, outputs = lax.scan(stepper, start, pieces)
    return outputs.reshape(length, H, P_SIZE)

def forward(source, seg_row, in_norm, z_proj, xbc_proj, dt_proj, conv_taps, conv_bias, dt_bias, a_log, d_skip, gate_norm, out_proj):
    length = source.shape[0]
    normed = low(norm_rows(source, in_norm))
    gate_in = low_back(jnp.dot(normed, z_proj, precision=HIGH))
    raw_xbc = low(low_back(jnp.dot(normed, xbc_proj, precision=HIGH)))
    rate_raw = low(low_back(jnp.dot(normed, dt_proj, precision=HIGH)))
    padded = jnp.concatenate([jnp.zeros((KW - 1, raw_xbc.shape[1]), jnp.float32), raw_xbc], 0)
    seg_pad = jnp.concatenate([jnp.full((KW - 1,), -1, jnp.int32), seg_row.astype(jnp.int32)], 0)
    mixed = conv_bias
    for tap in range(KW):
        same = (seg_pad[tap:tap + length] == seg_row).astype(jnp.float32)
        mixed = mixed + conv_taps[tap] * padded[tap:tap + length] * same[:, None]
    active = jax.nn.silu(mixed)
    x_part = low(low_back(active[:, :DI]))
    b_part = low(active[:, DI:DI + N])
    c_part = low(active[:, DI + N:])
    rates = jax.nn.softplus(rate_raw + dt_bias)
    x_heads = x_part.reshape(length, H, P_SIZE)
    mixer_out = mixer(x_heads, rates, b_part, c_part, seg_row, -jnp.exp(a_log))
    mixer_out = mixer_out + d_skip[:, None] * x_heads
    mixer_low = low(low_back(mixer_out.reshape(length, DI)))
    gated = low(norm_rows(mixer_low * jax.nn.silu(gate_in), gate_norm))
    return source + jnp.dot(gated, out_proj, precision=HIGH)

def reference(tokens_in, seg_ids, in_norm, z_proj, xbc_proj, dt_proj, conv_taps, conv_bias, dt_bias, a_log, d_skip, gate_norm, out_proj, out_cotangent):
    params = tuple((w.astype(jnp.float32) for w in (in_norm, z_proj, xbc_proj, dt_proj, conv_taps, conv_bias, dt_bias, a_log, d_skip, gate_norm, out_proj)))
    outputs = []
    input_grads = []
    totals = tuple((jnp.zeros(w.shape, jnp.float32) for w in params))
    for sequence in range(tokens_in.shape[0]):
        seg_row = seg_ids[sequence]

        def single(source, *weights):
            return forward(source, seg_row, *weights)
        result, pull = jax.vjp(single, tokens_in[sequence].astype(jnp.float32), *params)
        grads = pull(out_cotangent[sequence].astype(jnp.float32))
        outputs.append(result.astype(jnp.bfloat16))
        input_grads.append(grads[0])
        totals = tuple((a + b for a, b in zip(totals, grads[1:])))
    return (jnp.stack(outputs), jnp.stack(input_grads), totals[0], totals[1], totals[2], totals[3], totals[4], totals[5], totals[6], totals[7], totals[8], totals[9], totals[10])
```

```python
import jax
import jax.numpy as jnp
from jax import lax
from jax.experimental import pallas as pl
from jax.experimental.pallas import tpu as pltpu
from jax.sharding import Mesh, PartitionSpec as P

H = 48
PS = 64
N = 128
KW = 4
DI = 3072
GROUP = 4
HG = H // GROUP
XW = HG * PS
CW = XW + 2 * N
AW = CW + 128
QC = 128
EPS = 1e-05
NEG = -1e30
BF = jnp.bfloat16
F4 = jnp.float32
HIGH = lax.Precision.HIGHEST
LIMIT = 48 * 1024 * 1024
SUMS = ("dp", "ctx", "hh")
EVERY = ("dp", "ctx", "hh", "hl")


def swap(part, axis, k):
    count = lax.axis_size(axis)
    return lax.ppermute(part, axis, [(i, i ^ k) for i in range(count)])


def shift(part, axes, by):
    count = 1
    for axis in axes:
        count = count * lax.axis_size(axis)
    pairs = [(i, i + by) for i in range(count) if 0 <= i + by < count]
    return lax.ppermute(part, axes, pairs)


def mm(a, b):
    return jnp.dot(a, b, preferred_element_type=F4)


def mm_nt(a, b):
    return lax.dot_general(a, b, (((1,), (1,)), ((), ())), preferred_element_type=F4)


def mm_tn(a, b):
    return lax.dot_general(a, b, (((0,), (0,)), ((), ())), preferred_element_type=F4)


def spread(v, e):
    hi = v.astype(BF)
    lo = (v - hi.astype(F4)).astype(BF)
    return mm(hi, e) + mm(lo, e)


def gather_heads(w, e):
    hi = w.astype(BF)
    lo = (w - hi.astype(F4)).astype(BF)
    return mm_nt(hi, e) + mm_nt(lo, e)


def sigmoid(v):
    return 1.0 / (1.0 + jnp.exp(-v))


def tri():
    r = lax.broadcasted_iota(jnp.int32, (QC, QC), 0)
    c = lax.broadcasted_iota(jnp.int32, (QC, QC), 1)
    return r, c


def col_of(row):
    return jnp.transpose(jnp.broadcast_to(row, (QC, QC)))


def wide(col):
    return jnp.concatenate([col] * (XW // 128), axis=1)


def order_kernel(norm, place, own, r1, r2, r3, gain, out):
    here = place[0]
    for k, ref in enumerate((own, r1, r2, r3)):
        slot = jnp.bitwise_xor(here, k)
        rows = ref.shape[0]
        at = pl.ds(pl.multiple_of(slot * rows, rows), rows)
        if norm:
            v = ref[...].astype(F4)
            scale = lax.rsqrt(jnp.mean(v * v, axis=-1, keepdims=True) + EPS)
            out[at, :] = (v * scale * gain[...]).astype(BF)
        else:
            out[at, :] = ref[...]


def ordered(norm, place, pieces, gain):
    rows, width = pieces[0].shape
    vm = pl.BlockSpec(memory_space=pltpu.VMEM)
    return pl.pallas_call(
        lambda *refs: order_kernel(norm, *refs),
        out_shape=jax.ShapeDtypeStruct((GROUP * rows, width), BF),
        in_specs=[pl.BlockSpec(memory_space=pltpu.SMEM)] + [vm] * 5,
        out_specs=vm,
        compiler_params=pltpu.CompilerParams(vmem_limit_bytes=LIMIT),
        name="order_norm" if norm else "order_copy",
    )(place, *pieces, gain)


def rows_of(width):
    return pl.BlockSpec((QC, width), lambda i: (i, 0))


def fixed(*shape):
    return pl.BlockSpec(shape, lambda i: (0,) * len(shape))


META = pl.BlockSpec((1, 8, 128), lambda i: (i, 0, 0))


def front_kernel(raw, halo, meta, taps, hp, e, x_o, bc_o, cum_o, dt_o, st_o, dec_o, buf, act, st, dec):
    i = pl.program_id(0)

    @pl.when(i == 0)
    def _():
        buf[0:8, :] = halo[...].astype(F4)
        st[...] = jnp.zeros_like(st)
        dec[...] = jnp.ones_like(dec)

    @pl.when(i > 0)
    def _():
        buf[0:8, :] = buf[QC : QC + 8, :]

    buf[8 : QC + 8, :] = raw[:, :CW].astype(F4)
    mt = meta[0]
    masks = [col_of(mt[3 + k : 4 + k, :]) for k in range(3)]
    for j in range(CW // 128):
        c = slice(j * 128, j * 128 + 128)
        mixed = taps[4:5, c] + taps[3:4, c] * buf[8 : QC + 8, c]
        for k in range(3):
            mixed = mixed + taps[k : k + 1, c] * buf[5 + k : 5 + k + QC, c] * masks[k]
        act[:, c] = (mixed * sigmoid(mixed)).astype(BF)
    x = act[:, :XW]
    x_o[...] = x
    bc_o[...] = act[:, XW:]
    v = raw[:, CW:].astype(F4) + hp[0:1, :]
    dt = jnp.maximum(v, 0.0) + jnp.log1p(jnp.exp(-jnp.abs(v)))
    la = dt * hp[1:2, :]
    r, c = tri()
    cum = jnp.dot((r >= c).astype(F4), la, precision=HIGH, preferred_element_type=F4)
    cum_o[...] = cum
    dt_o[...] = dt
    same_last = col_of((mt[0:1, :] == mt[2:3, :]).astype(F4))
    last = cum[QC - 1 : QC, :]
    tail = jnp.exp(last - cum) * same_last * dt
    lead_last = jnp.exp(last) * (mt[1:2, :] == mt[2:3, :]).astype(F4)
    xw = (x.astype(F4) * spread(tail, e[...])).astype(BF)
    grow = spread(jnp.broadcast_to(lead_last, (8, 128)), e[...])[0:1, :]
    st[...] = st[...] * grow + mm_tn(act[:, XW : XW + N], xw)
    dec[...] = dec[...] * lead_last
    st_o[...] = st[...].astype(BF)
    dec_o[...] = dec[...]


def front(raw, halo, meta, taps, hp, e):
    length = raw.shape[0]
    sd = jax.ShapeDtypeStruct
    return pl.pallas_call(
        front_kernel,
        grid=(length // QC,),
        in_specs=[rows_of(AW), fixed(8, CW), META, fixed(8, CW), fixed(8, 128), fixed(128, XW)],
        out_specs=[rows_of(XW), rows_of(2 * N), rows_of(128), rows_of(128), fixed(N, XW), fixed(8, 128)],
        out_shape=[
            sd((length, XW), BF),
            sd((length, 2 * N), BF),
            sd((length, 128), F4),
            sd((length, 128), F4),
            sd((N, XW), BF),
            sd((8, 128), F4),
        ],
        scratch_shapes=[
            pltpu.VMEM((QC + 8, CW), F4),
            pltpu.VMEM((QC, CW), BF),
            pltpu.VMEM((N, XW), F4),
            pltpu.VMEM((8, 128), F4),
        ],
        compiler_params=pltpu.CompilerParams(vmem_limit_bytes=LIMIT),
        name="conv_state",
    )(raw, halo, meta, taps, hp, e)


def scan_kernel(x_r, bc, cum_r, dt_r, meta, s_in, z_r, dg_r, skip, gain, e, y_o, ent_o, sum_o, st, y_s):
    i = pl.program_id(0)

    @pl.when(i == 0)
    def _():
        st[...] = s_in[...].astype(F4)

    mt = meta[0]
    x = x_r[...]
    b = bc[:, :N]
    c = bc[:, N:]
    cum = cum_r[...]
    dt = dt_r[...]
    r, q = tri()
    keep = col_of((mt[0:1, :] == mt[1:2, :]).astype(F4))
    inside = (col_of(mt[0:1, :]) == mt[0:1, :]) & (r >= q)
    scores = mm_nt(c, b)
    before = st[...].astype(BF)
    ent_o[0] = before
    lead = jnp.exp(cum) * keep
    y_s[...] = spread(lead, e[...]) * mm(c, before) + skip[...] * x.astype(F4)
    cum_t = jnp.transpose(cum)
    dt_t = jnp.transpose(dt)
    lane = lax.broadcasted_iota(jnp.int32, (1, 128), 1)
    halves = [(lane < PS).astype(BF), (lane >= PS).astype(BF)]
    for j in range(HG // 2):
        at = slice(j * 128, j * 128 + 128)
        xp = x[:, at]
        part = jnp.zeros((QC, 128), F4)
        for half in range(2):
            h = 2 * j + half
            gap = jnp.where(inside, cum[:, h : h + 1] - cum_t[h : h + 1, :], NEG)
            w = (scores * jnp.exp(gap) * dt_t[h : h + 1, :]).astype(BF)
            part = part + mm(w, xp * halves[half])
        y_s[:, at] = y_s[:, at] + part
    same_last = col_of((mt[0:1, :] == mt[2:3, :]).astype(F4))
    last = cum[QC - 1 : QC, :]
    tail = jnp.exp(last - cum) * same_last * dt
    lead_last = jnp.exp(last) * (mt[1:2, :] == mt[2:3, :]).astype(F4)
    xw = (x.astype(F4) * spread(tail, e[...])).astype(BF)
    grow = spread(jnp.broadcast_to(lead_last, (8, 128)), e[...])[0:1, :]
    st[...] = st[...] * grow + mm_tn(b, xw)
    squares = jnp.zeros((QC, 128), F4)
    along = jnp.zeros((QC, 128), F4)
    for j in range(XW // 128):
        at = slice(j * 128, j * 128 + 128)
        low = y_s[:, at].astype(BF)
        y_o[:, at] = low
        z = z_r[:, at]
        s = low.astype(F4) * z * sigmoid(z)
        squares = squares + s * s
        along = along + s * gain[:, at] * dg_r[:, at]
    sum_o[0] = jnp.concatenate(
        [
            jnp.sum(jnp.transpose(squares), axis=0, keepdims=True),
            jnp.sum(jnp.transpose(along), axis=0, keepdims=True),
            jnp.zeros((6, QC), F4),
        ],
        axis=0,
    )


def scan(x, bc, cum, dt, meta, s_in, z, dg, skip, gain, e):
    length = x.shape[0]
    chunks = length // QC
    sd = jax.ShapeDtypeStruct
    return pl.pallas_call(
        scan_kernel,
        grid=(chunks,),
        in_specs=[
            rows_of(XW),
            rows_of(2 * N),
            rows_of(128),
            rows_of(128),
            META,
            fixed(N, XW),
            rows_of(XW),
            rows_of(XW),
            fixed(1, XW),
            fixed(1, XW),
            fixed(128, XW),
        ],
        out_specs=[rows_of(XW), pl.BlockSpec((1, N, XW), lambda i: (i, 0, 0)), META],
        out_shape=[sd((length, XW), BF), sd((chunks, N, XW), BF), sd((chunks, 8, 128), F4)],
        scratch_shapes=[pltpu.VMEM((N, XW), F4), pltpu.VMEM((QC, XW), F4)],
        compiler_params=pltpu.CompilerParams(vmem_limit_bytes=LIMIT),
        name="scan_gate",
    )(x, bc, cum, dt, meta, s_in, z, dg, skip, gain, e)


def gate_kernel(y_r, z_r, dg_r, tot, bc, cum_r, meta, gain, e, gated_o, dy_o, dz_o, gg_o, ds_o, ds, gg):
    i = pl.program_id(0)

    @pl.when(i == 0)
    def _():
        ds[...] = jnp.zeros_like(ds)
        gg[...] = jnp.zeros_like(gg)

    mt = meta[0]
    cum = cum_r[...]
    rstd = col_of(lax.rsqrt(tot[0, 0:1, :] * (1.0 / DI) + EPS))
    pull = col_of(tot[0, 1:2, :]) * (rstd * rstd * rstd) * (1.0 / DI)
    keep = col_of((mt[0:1, :] == mt[1:2, :]).astype(F4))
    lead = spread(jnp.exp(cum) * keep, e[...])
    for j in range(XW // 128):
        at = slice(j * 128, j * 128 + 128)
        y = y_r[:, at].astype(F4)
        z = z_r[:, at]
        sig = sigmoid(z)
        act = z * sig
        s = y * act
        n = s * rstd
        g = gain[:, at]
        dg = dg_r[:, at]
        gated_o[:, at] = (n * g).astype(BF)
        gg[0:1, at] = gg[0:1, at] + jnp.sum(dg * n, axis=0, keepdims=True)
        d_s = rstd * dg * g - s * pull
        dy_o[:, at] = (d_s * act).astype(BF)
        dz_o[:, at] = (d_s * y * sig * (1.0 + z * (1.0 - sig))).astype(BF)
    last = cum[QC - 1 : QC, :]
    lead_last = jnp.exp(last) * (mt[1:2, :] == mt[2:3, :]).astype(F4)
    grow = spread(jnp.broadcast_to(lead_last, (8, 128)), e[...])[0:1, :]
    led = (dy_o[...].astype(F4) * lead).astype(BF)
    ds[...] = ds[...] * grow + mm_tn(bc[:, N:], led)
    ds_o[...] = ds[...].astype(BF)
    gg_o[...] = gg[...]


def gate(y, z, dg, tot, bc, cum, meta, gain, e):
    length = y.shape[0]
    n = length // QC
    sd = jax.ShapeDtypeStruct

    def back(width):
        return pl.BlockSpec((QC, width), lambda i: (n - 1 - i, 0))

    bmeta = pl.BlockSpec((1, 8, 128), lambda i: (n - 1 - i, 0, 0))
    return pl.pallas_call(
        gate_kernel,
        grid=(n,),
        in_specs=[
            back(XW),
            back(XW),
            back(XW),
            bmeta,
            back(2 * N),
            back(128),
            bmeta,
            fixed(1, XW),
            fixed(128, XW),
        ],
        out_specs=[back(XW), back(XW), back(XW), fixed(8, XW), fixed(N, XW)],
        out_shape=[
            sd((length, XW), BF),
            sd((length, XW), BF),
            sd((length, XW), BF),
            sd((8, XW), F4),
            sd((N, XW), BF),
        ],
        scratch_shapes=[pltpu.VMEM((N, XW), F4), pltpu.VMEM((8, XW), F4)],
        compiler_params=pltpu.CompilerParams(vmem_limit_bytes=LIMIT),
        name="gate_back",
    )(y, z, dg, tot, bc, cum, meta, gain, e)


def back_kernel(
    x_r, bc, cum_r, dt_r, meta, ent, dy_r, d_end, raw, raw_before, halo, taps, hp, skip, e,
    draw_o, rim_o, cg_o, hg_o,
    ds, dx_s, act, buf, ebuf, carry, rowbuf, cg, hg,
):
    i = pl.program_id(0)
    n = pl.num_programs(0)
    first = i == n - 1

    @pl.when(i == 0)
    def _():
        ds[...] = d_end[...].astype(F4)
        carry[...] = jnp.zeros_like(carry)
        cg[...] = jnp.zeros_like(cg)
        hg[...] = jnp.zeros_like(hg)
        rowbuf[...] = jnp.zeros_like(rowbuf)

    mt = meta[0]
    ev = e[...]
    x = x_r[...]
    dy = dy_r[...]
    xf = x.astype(F4)
    dyf = dy.astype(F4)
    b = bc[:, :N]
    c = bc[:, N:]
    cum = cum_r[...]
    dt = dt_r[...]
    r, q = tri()
    keep = col_of((mt[0:1, :] == mt[1:2, :]).astype(F4))
    same_last = col_of((mt[0:1, :] == mt[2:3, :]).astype(F4))
    inside = (col_of(mt[0:1, :]) == mt[0:1, :]) & (r >= q)
    scores = mm_nt(c, b)
    before = ent[0]
    after = ds[...].astype(BF)
    last = cum[QC - 1 : QC, :]
    lead = spread(jnp.exp(cum) * keep, ev)
    tail0 = spread(jnp.exp(last - cum) * same_last, ev)
    dtw = spread(dt, ev)
    lead_last = jnp.exp(last) * (mt[1:2, :] == mt[2:3, :]).astype(F4)
    u = tail0 * mm(b, after)
    led = dyf * lead
    tq0 = gather_heads(xf * u, ev)
    lv = gather_heads(led * mm(c, before), ev)
    dx_s[...] = dtw * u + skip[...] * dyf
    xw = (xf * tail0 * dtw).astype(BF)
    ledb = led.astype(BF)
    d_b = mm_nt(xw, after)
    d_c = mm_nt(ledb, before)
    flow = jnp.sum(ds[...] * before.astype(F4), axis=0, keepdims=True)
    passed = jnp.sum(dyf * xf, axis=0, keepdims=True)
    heads2 = gather_heads(jnp.concatenate([flow, passed, jnp.zeros((6, XW), F4)], axis=0), ev)
    grow = spread(jnp.broadcast_to(lead_last, (8, 128)), ev)[0:1, :]
    ds[...] = ds[...] * grow + mm_tn(c, ledb)
    cum_t = jnp.transpose(cum)
    dt_t = jnp.transpose(dt)
    lane = lax.broadcasted_iota(jnp.int32, (1, 128), 1)
    halves = [(lane < PS).astype(BF), (lane >= PS).astype(BF)]
    d_sc = jnp.zeros((QC, QC), F4)
    rows = jnp.zeros((QC, 128), F4)
    for j in range(HG // 2):
        at = slice(j * 128, j * 128 + 128)
        xp = x[:, at]
        dyp = dy[:, at]
        part = jnp.zeros((QC, 128), F4)
        for half in range(2):
            h = 2 * j + half
            gap = jnp.where(inside, cum[:, h : h + 1] - cum_t[h : h + 1, :], NEG)
            dec = jnp.exp(gap)
            dtr = dt_t[h : h + 1, :]
            sl = scores * dec
            d_m = mm_nt(dyp, xp * halves[half])
            g = d_m * sl
            rowbuf[h : h + 1, :] = jnp.sum(g, axis=0, keepdims=True)
            rows = rows + jnp.where(lane == h, jnp.sum(g * dtr, axis=1, keepdims=True), 0.0)
            d_sc = d_sc + d_m * dec * dtr
            part = part + mm_tn((sl * dtr).astype(BF), dyp * halves[half])
        dx_s[:, at] = dx_s[:, at] + part
    d_scb = d_sc.astype(BF)
    d_c = d_c + mm(d_scb, b)
    d_b = d_b + mm_tn(d_scb, c)
    ecol = jnp.transpose(rowbuf[...])
    tq = tq0 * dt
    at_end = jnp.sum(tq, axis=0, keepdims=True) + lead_last * heads2[0:1, :]
    token = lax.broadcasted_iota(jnp.int32, (QC, 128), 0)
    d_cum = rows - dt * ecol - tq + lv + jnp.where(token == QC - 1, at_end, 0.0)
    d_la = jnp.dot((r <= q).astype(F4), d_cum, precision=HIGH, preferred_element_type=F4)
    neg = hp[1:2, :]
    v = raw[:, CW:].astype(F4) + hp[0:1, :]
    d_rate = (ecol + tq0 + d_la * neg) * sigmoid(v)
    draw_o[:, CW:] = d_rate.astype(BF)
    hg[0:1, :] = hg[0:1, :] + jnp.sum(d_rate, axis=0, keepdims=True)
    hg[1:2, :] = hg[1:2, :] + jnp.sum(d_la * dt * neg, axis=0, keepdims=True)
    hg[2:3, :] = hg[2:3, :] + heads2[1:2, :]
    act[:, :XW] = dx_s[...].astype(BF).astype(F4)
    act[:, XW : XW + N] = d_b
    act[:, XW + N :] = d_c

    @pl.when(first)
    def _():
        buf[0:8, :] = halo[...].astype(F4)

    @pl.when(jnp.logical_not(first))
    def _():
        buf[0:8, :] = raw_before[QC - 8 : QC, :CW].astype(F4)

    buf[8 : QC + 8, :] = raw[:, :CW].astype(F4)
    masks = [col_of(mt[3 + k : 4 + k, :]) for k in range(3)]
    ebuf[0:8, :] = jnp.zeros((8, 128), F4)
    for j in range(CW // 128):
        at = slice(j * 128, j * 128 + 128)
        own = buf[8 : QC + 8, at]
        shifted = [buf[5 + k : 5 + k + QC, at] * masks[k] for k in range(3)]
        mixed = taps[4:5, at] + taps[3:4, at] * own
        for k in range(3):
            mixed = mixed + taps[k : k + 1, at] * shifted[k]
        sig = sigmoid(mixed)
        dm = act[:, at] * (sig * (1.0 + mixed * (1.0 - sig)))
        sums = [jnp.sum(dm * s, axis=0, keepdims=True) for s in (*shifted, own)]
        sums.append(jnp.sum(dm, axis=0, keepdims=True))
        cg[0:5, at] = cg[0:5, at] + jnp.concatenate(sums, axis=0)
        d_raw = taps[3:4, at] * dm
        rim = jnp.zeros((8, 128), F4)
        for k in range(3):
            ek = taps[k : k + 1, at] * dm * masks[k]
            ebuf[8 : QC + 8, :] = ek
            ebuf[QC + 8 : QC + 16, :] = carry[8 * k : 8 * k + 8, at]
            d_raw = d_raw + ebuf[11 - k : 11 - k + QC, :]
            rim = rim + ebuf[3 - k : 11 - k, :]
            carry[8 * k : 8 * k + 8, at] = ek[0:8, :]
        draw_o[:, at] = d_raw.astype(BF)
        rim_o[:, at] = rim.astype(BF)
    cg_o[...] = cg[...]
    hg_o[...] = hg[...]


def scan_back(x, bc, cum, dt, meta, ent, dy, d_end, raw, halo, taps, hp, skip, e):
    length = x.shape[0]
    n = length // QC
    sd = jax.ShapeDtypeStruct

    def back(width):
        return pl.BlockSpec((QC, width), lambda i: (n - 1 - i, 0))

    bmeta = pl.BlockSpec((1, 8, 128), lambda i: (n - 1 - i, 0, 0))
    return pl.pallas_call(
        back_kernel,
        grid=(n,),
        in_specs=[
            back(XW),
            back(2 * N),
            back(128),
            back(128),
            bmeta,
            pl.BlockSpec((1, N, XW), lambda i: (n - 1 - i, 0, 0)),
            back(XW),
            fixed(N, XW),
            back(AW),
            pl.BlockSpec((QC, AW), lambda i: (jnp.maximum(n - 2 - i, 0), 0)),
            fixed(8, CW),
            fixed(8, CW),
            fixed(8, 128),
            fixed(1, XW),
            fixed(128, XW),
        ],
        out_specs=[back(AW), fixed(8, CW), fixed(8, CW), fixed(8, 128)],
        out_shape=[sd((length, AW), BF), sd((8, CW), BF), sd((8, CW), F4), sd((8, 128), F4)],
        scratch_shapes=[
            pltpu.VMEM((N, XW), F4),
            pltpu.VMEM((QC, XW), F4),
            pltpu.VMEM((QC, CW), F4),
            pltpu.VMEM((QC + 8, CW), F4),
            pltpu.VMEM((QC + 16, 128), F4),
            pltpu.VMEM((24, CW), F4),
            pltpu.VMEM((128, 128), F4),
            pltpu.VMEM((8, CW), F4),
            pltpu.VMEM((8, 128), F4),
        ],
        compiler_params=pltpu.CompilerParams(vmem_limit_bytes=LIMIT),
        name="scan_back",
    )(x, bc, cum, dt, meta, ent, dy, d_end, raw, raw, halo, taps, hp, skip, e)


def pad_lanes(v, width):
    return jnp.pad(v, [(0, 0)] * (v.ndim - 1) + [(0, width - v.shape[-1])])


def carried(state, decay, hops, by):
    chain = ("ctx", "hh")
    total = shift(state, chain, by)
    if hops == 1:
        return total
    far, fade = state, decay
    total, product = jnp.zeros(state.shape, F4), jnp.ones(decay.shape, F4)
    for _ in range(hops):
        far = shift(far, chain, by)
        total = total + product * far.astype(F4)
        fade = shift(fade, chain, by)
        product = product * fade
    return total.astype(BF)


def shards(
    tokens_in, seg_ids, in_norm, z_proj, xbc_proj, dt_proj, conv_taps, conv_bias,
    dt_bias, a_log, d_skip, gate_norm, out_proj, out_cotangent,
):
    seqs, rows, width = tokens_in.shape
    length = seg_ids.shape[1]
    block = rows * GROUP
    chunks = block // QC
    chain = ("ctx", "hh")
    n_blocks = length // block
    hops = min(-(-(length // 4 - 1) // block), n_blocks - 1)
    n_sums = lax.axis_size("dp") * n_blocks
    hl = lax.axis_index("hl")
    place = hl.astype(jnp.int32).reshape(1)
    own_rows = z_proj.shape[0]

    def quarters(w):
        return w.reshape(w.shape[0], GROUP, -1).transpose(1, 0, 2)

    bc_cols = jnp.broadcast_to(xbc_proj[None, :, DI:], (GROUP, own_rows, 2 * N))
    wx_parts = jnp.concatenate(
        [quarters(xbc_proj[:, :DI]), bc_cols, pad_lanes(quarters(dt_proj), 128)], axis=-1
    )
    wx_mine = lax.all_to_all(wx_parts, "hl", 0, 0, tiled=True).reshape(GROUP * own_rows, AW)
    wx = lax.all_gather(wx_mine, SUMS, axis=0, tiled=True)
    wz_mine = lax.all_to_all(quarters(z_proj), "hl", 0, 0, tiled=True).reshape(GROUP * own_rows, XW)
    wz = lax.all_gather(wz_mine, SUMS, axis=0, tiled=True)
    pairs = [(f, (f % n_sums) * GROUP + f // n_sums) for f in range(GROUP * n_sums)]
    wo_mine = lax.ppermute(out_proj, EVERY, pairs)
    wo = lax.all_gather(wo_mine, SUMS, axis=0, tiled=True)

    def mine(v, size):
        return lax.dynamic_slice_in_dim(v, hl * size, size, axis=-1)

    taps = jnp.concatenate([conv_taps, conv_bias[None]], axis=0)
    taps = jnp.concatenate([mine(taps[:, :DI], XW), taps[:, DI:]], axis=1)
    taps = jnp.pad(taps, ((0, 3), (0, 0)))
    hp = jnp.stack([mine(dt_bias, HG), -jnp.exp(mine(a_log, HG))])
    hp = jnp.pad(hp, ((0, 6), (0, 128 - HG)))
    skip = jnp.repeat(mine(d_skip, HG), PS)[None]
    gain = mine(gate_norm, XW)[None]
    e = (jnp.arange(128)[:, None] == jnp.arange(XW)[None, :] // PS).astype(BF)
    in_gain = in_norm[None]

    start = lax.axis_index(chain) * block
    seg_pad = jnp.concatenate([jnp.full((seqs, 8), -1, jnp.int32), seg_ids], axis=1)
    near = lax.dynamic_slice_in_dim(seg_pad, start, block + 8, axis=1)
    seg = near[:, 8:].reshape(seqs, chunks, QC)
    lines = [seg, jnp.broadcast_to(near[:, 7 : 7 + block : QC][:, :, None], seg.shape)]
    lines.append(jnp.broadcast_to(seg[:, :, QC - 1 :], seg.shape))
    for k in range(KW - 1):
        lines.append((near[:, 5 + k : 5 + k + block].reshape(seg.shape) == seg).astype(jnp.int32))
    lines.extend([jnp.zeros_like(seg)] * 2)
    meta = jnp.stack(lines, axis=2).astype(F4)

    def collected(part, norm):
        others = [swap(part, "hl", k) for k in range(1, GROUP)]
        return ordered(norm, place, [part, *others], in_gain)

    def spread_sum(part):
        def piece(k):
            at = jnp.bitwise_xor(hl, k) * rows
            return lax.dynamic_slice_in_dim(part, at, rows)

        total = piece(0).astype(F4)
        for k in range(1, GROUP):
            total = total + swap(piece(k), "hl", k).astype(F4)
        return total

    normed = [collected(tokens_in[s], True) for s in range(seqs)]
    cot = [collected(out_cotangent[s], False) for s in range(seqs)]
    kept = []
    for s in range(seqs):
        raw = mm(normed[s], wx).astype(BF)
        halo = shift(raw[block - 8 :, :CW], chain, 1)
        x, bc, cum, dt, state, decay = front(raw, halo, meta[s], taps, hp, e)
        decay_row = jnp.repeat(decay[0, :HG], PS)[None]
        kept.append((raw, halo, x, bc, cum, dt, carried(state, decay_row, hops, 1), decay_row))
    gates = [mm(normed[s], wz) for s in range(seqs)]
    d_gated = [mm_nt(cot[s], wo) for s in range(seqs)]
    outs = []
    middle = []
    out_grad = 0.0
    gate_total = 0.0
    for s in range(seqs):
        raw, halo, x, bc, cum, dt, s_in, decay_row = kept[s]
        y, ent, sums = scan(x, bc, cum, dt, meta[s], s_in, gates[s], d_gated[s], skip, gain, e)
        tot = sums
        for k in range(1, GROUP):
            tot = tot + swap(sums, "hl", k)
        gated, dy, dz, gg, d_state = gate(y, gates[s], d_gated[s], tot, bc, cum, meta[s], gain, e)
        d_end = carried(d_state, decay_row, hops, -1)
        gate_total = gate_total + gg[0]
        out_grad = out_grad + mm_tn(gated, cot[s])
        summed = spread_sum(mm(gated, wo).astype(BF))
        outs.append((tokens_in[s].astype(F4) + summed).astype(BF))
        middle.append((ent, dy, dz, d_end))
    out_part = lax.psum_scatter(out_grad.astype(BF), SUMS, scatter_dimension=0, tiled=True)
    back_pairs = [(b, a) for a, b in pairs]
    out_proj_grad = lax.ppermute(out_part, EVERY, back_pairs).astype(F4)
    z_grad = 0.0
    for s in range(seqs):
        z_grad = z_grad + mm_tn(normed[s], middle[s][2])

    def columns(grad, n_cols):
        part = lax.psum_scatter(grad.astype(BF), SUMS, scatter_dimension=0, tiled=True)
        parts = part.reshape(GROUP, own_rows, n_cols)
        return lax.all_to_all(parts, "hl", 0, 0, tiled=True).astype(F4)

    z_parts = columns(z_grad, XW)
    z_proj_grad = z_parts.transpose(1, 0, 2).reshape(own_rows, DI)
    x_grad = 0.0
    conv_total = 0.0
    head_total = 0.0
    norm_total = 0.0
    grads_tok = []
    for s in range(seqs):
        raw, halo, x, bc, cum, dt, _, _ = kept[s]
        ent, dy, dz, d_end = middle[s]
        draw, rim, cg, hg = scan_back(
            x, bc, cum, dt, meta[s], ent, dy, d_end, raw, halo, taps, hp, skip, e
        )
        conv_total = conv_total + cg
        head_total = head_total + hg
        rim = shift(rim, chain, -1)
        draw = draw.at[block - 8 :, :CW].add(rim)
        x_grad = x_grad + mm_tn(normed[s], draw)
        d_normed = mm_nt(dz, wz) + mm_nt(draw, wx)
        norm_total = norm_total + jnp.sum(d_normed * normed[s].astype(F4), axis=0)
        summed = spread_sum(d_normed.astype(BF))
        u = tokens_in[s].astype(F4)
        scale = lax.rsqrt(jnp.mean(u * u, axis=-1, keepdims=True) + EPS)
        hat = u * scale
        dh = summed * in_norm
        d_u = scale * (dh - hat * jnp.mean(dh * hat, axis=-1, keepdims=True))
        grads_tok.append(d_u + out_cotangent[s].astype(F4))
    x_parts = columns(x_grad, AW)
    xs = x_parts[:, :, :XW].transpose(1, 0, 2).reshape(own_rows, DI)
    xbc_proj_grad = jnp.concatenate([xs, jnp.sum(x_parts[:, :, XW:CW], axis=0)], axis=1)
    dt_proj_grad = x_parts[:, :, CW : CW + HG].transpose(1, 0, 2).reshape(own_rows, H)

    pieces = [
        conv_total[:5, :XW].reshape(-1),
        gate_total,
        head_total[:3].reshape(-1),
        conv_total[:5, XW:].reshape(-1),
        norm_total / in_norm,
    ]
    sizes = [p.shape[0] for p in pieces]
    pack = jnp.concatenate(pieces)
    lines_n = -(-pack.shape[0] // 1024) * 8
    pack = jnp.pad(pack, (0, lines_n * 128 - pack.shape[0])).reshape(lines_n, 128)
    for axis in SUMS:
        k = 1
        while k < lax.axis_size(axis):
            pack = pack + swap(pack, axis, k)
            k = 2 * k
    got = [pack] + [swap(pack, "hl", k) for k in range(1, GROUP)]
    for bit in (1, 2):
        odd = (hl & bit) > 0
        got = [jnp.where(odd, got[j ^ bit], got[j]) for j in range(GROUP)]
    flat = jnp.stack(got).reshape(GROUP, -1)
    cuts = []
    low = 0
    for size in sizes:
        cuts.append(flat[:, low : low + size])
        low = low + size
    conv_x = cuts[0].reshape(GROUP, 5, XW).transpose(1, 0, 2).reshape(5, DI)
    conv_all = jnp.concatenate([conv_x, jnp.sum(cuts[3], axis=0).reshape(5, 2 * N)], axis=1)
    per_head = cuts[2].reshape(GROUP, 3, 128)[:, :, :HG].transpose(1, 0, 2).reshape(3, H)
    return (
        jnp.stack(outs),
        jnp.stack(grads_tok),
        jnp.sum(cuts[4], axis=0),
        z_proj_grad,
        xbc_proj_grad,
        dt_proj_grad,
        conv_all[:4],
        conv_all[4],
        per_head[0],
        per_head[1],
        per_head[2],
        cuts[1].reshape(DI),
        out_proj_grad,
    )


def solution(mesh):
    sizes = dict(mesh.shape)
    grid = mesh.devices.reshape(sizes["dp"], sizes["ctx"], sizes["hd"] // GROUP, GROUP)
    fine = Mesh(grid, ("dp", "ctx", "hh", "hl"))
    tok = P("dp", ("ctx", "hh", "hl"), None)
    wgt = P(("dp", "ctx", "hh", "hl"), None)
    in_specs = (tok, P("dp", None), P(), wgt, wgt, wgt, P(), P(), P(), P(), P(), P(), wgt, tok)
    out_specs = (tok, tok, P(), wgt, wgt, wgt, P(), P(), P(), P(), P(), P(), wgt)
    return jax.shard_map(shards, mesh=fine, in_specs=in_specs, out_specs=out_specs, check_vma=False)
```

```python
import jax
import jax.numpy as jnp
from jax import lax
from jax.experimental import pallas as pl
from jax.experimental.pallas import tpu as pltpu
from jax.sharding import Mesh, PartitionSpec as P

H = 48
PS = 64
N = 128
KW = 4
DI = 3072
GROUP = 4
HG = H // GROUP
HP = 16
XW = HG * PS
CW = XW + 2 * N
AW = CW + 128
QC = 128
EPS = 1e-05
NEG = -1e30
BF = jnp.bfloat16
F4 = jnp.float32
LIMIT = 48 * 1024 * 1024
SUMS = ("dp", "ctx", "hh")
CHAIN = ("ctx", "hh")
EVERY = ("dp", "ctx", "hh", "hl")


def swap(part, axis, k):
    count = lax.axis_size(axis)
    return lax.ppermute(part, axis, [(i, i ^ k) for i in range(count)])


def shift(part, axes, by):
    count = 1
    for axis in axes:
        count = count * lax.axis_size(axis)
    pairs = [(i, i + by) for i in range(count) if 0 <= i + by < count]
    return lax.ppermute(part, axes, pairs)


def mm(a, b):
    return jnp.dot(a, b, preferred_element_type=F4)


def mm_nt(a, b):
    return lax.dot_general(a, b, (((1,), (1,)), ((), ())), preferred_element_type=F4)


def mm_tn(a, b):
    return lax.dot_general(a, b, (((0,), (0,)), ((), ())), preferred_element_type=F4)


def spread(v, e):
    return mm_tn(v.astype(BF), e)


def spread_fine(v, e):
    hi = v.astype(BF)
    lo = (v - hi.astype(F4)).astype(BF)
    return mm_tn(hi, e) + mm_tn(lo, e)


def gather_heads(w, e):
    return mm_nt(e, w.astype(BF))


def gather_fine(w, e):
    hi = w.astype(BF)
    lo = (w - hi.astype(F4)).astype(BF)
    return mm_nt(e, hi) + mm_nt(e, lo)


def sigmoid(v):
    return 0.5 * jnp.tanh(0.5 * v) + 0.5


def norm_rows(values, gain):
    return values * lax.rsqrt(jnp.mean(values * values, axis=-1, keepdims=True) + EPS) * gain


def running(v, back):
    r = lax.broadcasted_iota(jnp.int32, (QC, QC), 0)
    q = lax.broadcasted_iota(jnp.int32, (QC, QC), 1)
    ones = ((r >= q) if back else (r <= q)).astype(BF)
    hi = v.astype(BF)
    rest = v - hi.astype(F4)
    mid = rest.astype(BF)
    lo = (rest - mid.astype(F4)).astype(BF)
    got = mm(jnp.concatenate([hi, mid, lo], axis=0), ones)
    n = v.shape[0]
    return got[:n] + got[n : 2 * n] + got[2 * n :]


def lines_of(mt):
    return jnp.transpose(jnp.concatenate([mt, jnp.zeros((QC - 8, QC), F4)], axis=0))


def tiles(count):
    return [slice(j * 128, j * 128 + 128) for j in range(count)]


def col_of(row):
    return jnp.transpose(jnp.broadcast_to(row, (QC, QC)))


def cols_of(v):
    return jnp.transpose(jnp.concatenate([v, jnp.zeros((QC - HP, QC), F4)], axis=0))


def place_kernel(place, *refs):
    out = refs[-1]
    rows = refs[0].shape[0]
    for k, ref in enumerate(refs[:-1]):
        slot = jnp.bitwise_xor(place[0], k)
        out[pl.ds(pl.multiple_of(slot * rows, rows), rows), :] = ref[...]


def placed(place, pieces):
    rows, width = pieces[0].shape
    vm = pl.BlockSpec(memory_space=pltpu.VMEM)
    return pl.pallas_call(
        place_kernel,
        out_shape=jax.ShapeDtypeStruct((len(pieces) * rows, width), BF),
        in_specs=[pl.BlockSpec(memory_space=pltpu.SMEM)] + [vm] * len(pieces),
        out_specs=vm,
        compiler_params=pltpu.CompilerParams(vmem_limit_bytes=LIMIT),
        name="place_rows",
    )(place, *pieces)


def joined(cur, got, side):
    low = jnp.where(side == 0, cur, got)
    high = jnp.where(side == 0, got, cur)
    return jnp.concatenate([low, high], axis=0)


def sums_gather(mine, cuts):
    rows = mine.shape[0]
    if lax.axis_size("hh") > 1 or rows % 16:
        whole = lax.all_gather(mine, SUMS, axis=0, tiled=True)
        return [whole[:, a:b] for a, b in cuts]
    place = lax.axis_index("ctx").astype(jnp.int32).reshape(1)
    others = [swap(mine, "ctx", k) for k in range(1, lax.axis_size("ctx"))]
    stack = placed(place, [mine, *others])
    got = swap(stack, "dp", 1)
    side = lax.axis_index("dp")
    return [joined(stack[:, a:b], got[:, a:b], side) for a, b in cuts]


def team_halves(total):
    if lax.axis_size("hh") > 1:
        return total
    parts = total.reshape(2, -1, total.shape[1])
    dp = lax.axis_index("dp")
    give = lax.dynamic_index_in_dim(parts, 1 - dp, 0, keepdims=False)
    keep = lax.dynamic_index_in_dim(parts, dp, 0, keepdims=False)
    return (keep.astype(F4) + swap(give, "dp", 1).astype(F4)).astype(BF)


def chain_sum(cur):
    if lax.axis_size("hh") > 1:
        return lax.psum_scatter(cur, SUMS, scatter_dimension=0, tiled=True).astype(BF)
    count = lax.axis_size("ctx")
    parts = cur.reshape(count, -1, cur.shape[1])
    ctx = lax.axis_index("ctx")

    def piece(k):
        return lax.dynamic_index_in_dim(parts, jnp.bitwise_xor(ctx, k), 0, keepdims=False)

    out = piece(0).astype(F4)
    for k in range(1, count):
        out = out + swap(piece(k), "ctx", k).astype(F4)
    return out.astype(BF)


def work(length, us):
    flops = int(us * 1e9) * length // 1024
    return pl.CostEstimate(flops=flops, transcendentals=0, bytes_accessed=length * 8192)


def fixed(*shape):
    return pl.BlockSpec(shape, lambda i: (0,) * len(shape))


def ahead(rows, width, at=0):
    return pl.BlockSpec((rows, width), lambda i: (i, at))


def ahead3(seqs, *shape):
    return pl.BlockSpec((seqs, *shape), lambda i: (i, 0, 0))


def behind(n, rows, width, at=0):
    return pl.BlockSpec((rows, width), lambda i: (n - 1 - i, at))


def behind3(n, seqs, *shape):
    return pl.BlockSpec((seqs, *shape), lambda i: (n - 1 - i, 0, 0))


def decays(cum, mt):
    last = cum[:, QC - 1 : QC]
    same_last = (mt[0:1, :] == mt[2:3, :]).astype(F4)
    follows = (mt[1:2, :] == mt[2:3, :]).astype(F4)
    tail0 = jnp.exp(last - cum) * same_last
    lead_last = jnp.exp(last) * follows
    return tail0, lead_last


def front_kernel(
    xr, br, rr, halo, meta, taps, hp, e, x_o, bc_o, sl_o, sc_o, st_o, dec_o, buf, st, dec
):
    i = pl.program_id(0)
    seqs = halo.shape[0]

    @pl.when(i == 0)
    def _():
        buf[:, 0:8, :] = halo[...].astype(F4)
        st[...] = jnp.zeros_like(st)
        dec[...] = jnp.ones_like(dec)

    @pl.when(i > 0)
    def _():
        buf[:, 0:8, :] = buf[:, QC : QC + 8, :]

    every = range(seqs)
    rows = [slice(s * QC, s * QC + QC) for s in every]
    tails, lasts = [], []
    for s in every:
        v = jnp.transpose(rr[rows[s], :].astype(F4))[:HP] + hp[0]
        dt = jnp.maximum(v, 0.0) + jnp.log1p(jnp.exp(-jnp.abs(v)))
        cum = running(dt * hp[1], False)
        sc_o[s, 0:HP, :] = cum
        sc_o[s, HP:, :] = dt
        tail0, lead_last = decays(cum, meta[s])
        dec[s] = dec[s] * lead_last
        tails.append((tail0 * dt).astype(BF))
        lasts.append(lead_last[:, :8])
    order = tiles(CW // 128)
    n_x = XW // 128
    for s in every:
        turned = lines_of(meta[s])
        for j in [*range(n_x, len(order)), *range(n_x)]:
            c = order[j]
            if j < n_x:
                own = xr[rows[s], c].astype(F4)
            else:
                own = br[rows[s], j * 128 - XW : j * 128 - XW + 128].astype(F4)
            buf[s, 8 : QC + 8, c] = own
            mixed = taps[4:5, c] + taps[3:4, c] * own
            for k in range(3):
                mixed = mixed + taps[k : k + 1, c] * (
                    buf[s, 5 + k : 5 + k + QC, c] * turned[:, 3 + k : 4 + k]
                )
            sig = sigmoid(mixed)
            act = (mixed * sig).astype(BF)
            sl_o[rows[s], c] = (sig + mixed * sig * (1.0 - sig)).astype(BF)
            if j < n_x:
                x_o[rows[s], c] = act
                xw = (act.astype(F4) * spread(tails[s], e[:, c])).astype(BF)
                grow = spread_fine(lasts[s], e[:, c])[0:1, :]
                st[s, :, c] = st[s, :, c] * grow + mm_tn(bc_o[rows[s], :N], xw)
            else:
                bc_o[rows[s], j * 128 - XW : j * 128 - XW + 128] = act
    st_o[...] = st[...].astype(BF)
    dec_o[...] = dec[...]


def front(seqs, raw, halo, meta, taps, hp, e):
    length = raw.shape[0]
    span = seqs * QC
    sd = jax.ShapeDtypeStruct
    return pl.pallas_call(
        front_kernel,
        grid=(length // span,),
        in_specs=[
            ahead(span, XW),
            ahead(span, 2 * N, XW // (2 * N)),
            ahead(span, 128, CW // 128),
            fixed(seqs, 8, CW),
            ahead3(seqs, 8, 128),
            fixed(8, CW),
            fixed(2, HP, 128),
            fixed(HP, XW),
        ],
        out_specs=[
            ahead(span, XW),
            ahead(span, 2 * N),
            ahead(span, CW),
            ahead3(seqs, 2 * HP, 128),
            fixed(seqs, N, XW),
            fixed(seqs, HP, 128),
        ],
        out_shape=[
            sd((length, XW), BF),
            sd((length, 2 * N), BF),
            sd((length, CW), BF),
            sd((length // QC, 2 * HP, 128), F4),
            sd((seqs, N, XW), BF),
            sd((seqs, HP, 128), F4),
        ],
        scratch_shapes=[
            pltpu.VMEM((seqs, QC + 8, CW), F4),
            pltpu.VMEM((seqs, N, XW), F4),
            pltpu.VMEM((seqs, HP, 128), F4),
        ],
        compiler_params=pltpu.CompilerParams(vmem_limit_bytes=LIMIT),
        cost_estimate=work(length, 1),
        name="conv_state",
    )(raw, raw, raw, halo, meta, taps, hp, e)


def lane_halves():
    lane = lax.broadcasted_iota(jnp.int32, (1, 128), 1)
    return [(lane < PS).astype(BF), (lane >= PS).astype(BF)]


def inside_of(mt):
    r = lax.broadcasted_iota(jnp.int32, (QC, QC), 0)
    q = lax.broadcasted_iota(jnp.int32, (QC, QC), 1)
    return (col_of(mt[0:1, :]) == mt[0:1, :]) & (r >= q)


def scan_kernel(x_r, bc, sc, meta, s_in, z_r, skip, e, y_o, ent_o, sum_o, st):
    i = pl.program_id(0)
    seqs = s_in.shape[0]
    every = range(seqs)
    rows = [slice(s * QC, s * QC + QC) for s in every]

    @pl.when(i == 0)
    def _():
        st[...] = s_in[...].astype(F4)

    halves = lane_halves()
    for s in every:
        mt = meta[s]
        cum, dt = sc[s, 0:HP, :], sc[s, HP:, :]
        b, c = bc[rows[s], :N], bc[rows[s], N:]
        lead = (jnp.exp(cum) * (mt[0:1, :] == mt[1:2, :]).astype(F4)).astype(BF)
        tail0, lead_last = decays(cum, mt)
        tail = (tail0 * dt).astype(BF)
        scores = mm_nt(c, b)
        inside = inside_of(mt)
        cum_cols = cols_of(cum)
        squares = jnp.zeros((QC, 128), F4)
        for j, at in enumerate(tiles(XW // 128)):
            ej = e[:, at]
            xp = x_r[rows[s], at]
            xf = xp.astype(F4)
            now = st[s, :, at]
            before = now.astype(BF)
            ent_o[s, :, at] = before
            y = spread(lead, ej) * mm(c, before) + skip[:, at] * xf
            xw = (xf * spread(tail, ej)).astype(BF)
            st[s, :, at] = now * spread_fine(lead_last[:, :8], ej)[0:1, :] + mm_tn(b, xw)
            for half in range(2):
                h = 2 * j + half
                gap = jnp.where(inside, cum_cols[:, h : h + 1] - sc[s, h : h + 1, :], NEG)
                w = (scores * jnp.exp(gap) * sc[s, HP + h : HP + h + 1, :]).astype(BF)
                y = y + mm(w, xp * halves[half])
            low = y.astype(BF)
            y_o[rows[s], at] = low
            z = z_r[rows[s], at]
            v = low.astype(F4) * z * sigmoid(z)
            squares = squares + v * v
        sum_o[s] = jnp.sum(jnp.transpose(squares), axis=0, keepdims=True)


def scan(seqs, x, bc, sc, meta, s_in, z, skip, e):
    length = x.shape[0]
    span = seqs * QC
    chunks = length // QC
    sd = jax.ShapeDtypeStruct
    return pl.pallas_call(
        scan_kernel,
        grid=(length // span,),
        in_specs=[
            ahead(span, XW),
            ahead(span, 2 * N),
            ahead3(seqs, 2 * HP, 128),
            ahead3(seqs, 8, 128),
            fixed(seqs, N, XW),
            ahead(span, XW),
            fixed(1, XW),
            fixed(HP, XW),
        ],
        out_specs=[ahead(span, XW), ahead3(seqs, N, XW), ahead3(seqs, 1, QC)],
        out_shape=[sd((length, XW), BF), sd((chunks, N, XW), BF), sd((chunks, 1, QC), F4)],
        scratch_shapes=[pltpu.VMEM((seqs, N, XW), F4)],
        compiler_params=pltpu.CompilerParams(vmem_limit_bytes=LIMIT),
        cost_estimate=work(length, 1),
        name="scan_gate",
    )(x, bc, sc, meta, s_in, z, skip, e)


def gate_kernel(y_r, z_r, dg_r, sq, al, bc, sc, meta, gain, e, dy_o, dz_o, gg_o, ds_o, ds, gg):
    i = pl.program_id(0)
    seqs = ds.shape[0]
    every = range(seqs)
    rows = [slice(s * QC, s * QC + QC) for s in every]

    @pl.when(i == 0)
    def _():
        gg[...] = jnp.zeros_like(gg)
        ds[...] = jnp.zeros_like(ds)

    for s in every:
        mt = meta[s]
        cum = sc[s, 0:HP, :]
        c = bc[rows[s], N:]
        scale = lax.rsqrt(sq[s] * (1.0 / DI) + EPS)
        rstd = col_of(scale)
        pull = col_of(al[s] * (scale * scale * scale) * (1.0 / DI))
        lead = (jnp.exp(cum) * (mt[0:1, :] == mt[1:2, :]).astype(F4)).astype(BF)
        _, lead_last = decays(cum, mt)
        for at in tiles(XW // 128):
            ej = e[:, at]
            y = y_r[rows[s], at].astype(F4)
            z = z_r[rows[s], at]
            sig = sigmoid(z)
            act = z * sig
            v = y * act
            dg = dg_r[rows[s], at] * rstd
            gg[0:1, at] = gg[0:1, at] + jnp.sum(dg * v, axis=0, keepdims=True)
            d_v = dg * gain[:, at] - v * pull
            dy = (d_v * act).astype(BF)
            dy_o[rows[s], at] = dy
            dz_o[rows[s], at] = (d_v * y * (sig + act * (1.0 - sig))).astype(BF)
            led = (dy.astype(F4) * spread(lead, ej)).astype(BF)
            grow = spread_fine(lead_last[:, :8], ej)[0:1, :]
            ds[s, :, at] = ds[s, :, at] * grow + mm_tn(c, led)
    ds_o[...] = ds[...].astype(BF)
    gg_o[...] = gg[...]


def gate(seqs, y, z, dg, sq, al, bc, sc, meta, gain, e):
    length = y.shape[0]
    span = seqs * QC
    n = length // span
    sd = jax.ShapeDtypeStruct
    wide = behind(n, span, XW)
    line = behind3(n, seqs, 1, QC)
    return pl.pallas_call(
        gate_kernel,
        grid=(n,),
        in_specs=[
            wide,
            wide,
            wide,
            line,
            line,
            behind(n, span, 2 * N),
            behind3(n, seqs, 2 * HP, 128),
            behind3(n, seqs, 8, 128),
            fixed(1, XW),
            fixed(HP, XW),
        ],
        out_specs=[wide, wide, fixed(8, XW), fixed(seqs, N, XW)],
        out_shape=[
            sd((length, XW), BF),
            sd((length, XW), BF),
            sd((8, XW), F4),
            sd((seqs, N, XW), BF),
        ],
        scratch_shapes=[pltpu.VMEM((seqs, N, XW), F4), pltpu.VMEM((8, XW), F4)],
        compiler_params=pltpu.CompilerParams(vmem_limit_bytes=LIMIT),
        cost_estimate=work(length, 1),
        name="gate_back",
    )(y, z, dg, sq, al, bc, sc, meta, gain, e)


def back_kernel(
    x_r, bc, sl, sc, meta, ent, dy_r, d_end, xr, br, rr, halo, taps, hp, skip, e,
    draw_o, rim_o, cg_o, hg_o,
    ds, carry, colbuf, rowbuf, cg, hg,
):
    i = pl.program_id(0)
    seqs = ds.shape[0]
    every = range(seqs)
    rows = [slice(s * QC, s * QC + QC) for s in every]
    first = (i == pl.num_programs(0) - 1).astype(F4)

    @pl.when(i == 0)
    def _():
        ds[...] = d_end[...].astype(F4)
        carry[...] = jnp.zeros_like(carry)
        cg[...] = jnp.zeros_like(cg)
        hg[...] = jnp.zeros_like(hg)
        colbuf[...] = jnp.zeros_like(colbuf)
        rowbuf[...] = jnp.zeros_like(rowbuf)

    halves = lane_halves()
    lane = lax.broadcasted_iota(jnp.int32, (1, 128), 1)
    token = lax.broadcasted_iota(jnp.int32, (QC, 128), 0)
    edge = lax.broadcasted_iota(jnp.int32, (8, 128), 0)
    place = lax.broadcasted_iota(jnp.int32, (HP, QC), 1)

    def conv_back(s, c, own, d_act, turned):
        dm = d_act * sl[rows[s], c].astype(F4)
        near = turned[:, 5:6]
        shifted = [dm]
        for k in range(3):
            ready = shifted[-1] * near
            moved = pltpu.roll(ready, QC - 1, 0)
            shifted.append(jnp.where(token == QC - 1, carry[s, k : k + 1, c], moved))
            carry[s, k : k + 1, c] = ready[0:1, :]
        d_raw = taps[3:4, c] * shifted[0]
        for k in range(3):
            d_raw = d_raw + taps[2 - k : 3 - k, c] * shifted[k + 1]
        draw_o[rows[s], c] = d_raw.astype(BF)
        parts = [jnp.sum(own * v, axis=0, keepdims=True) for v in shifted[::-1]]
        parts.append(jnp.sum(dm, axis=0, keepdims=True))
        head = dm[0:8, :]
        outside = halo[s, :, c].astype(F4) * first
        rim = jnp.zeros((8, 128), F4)
        for k in range(3):
            held = jnp.where(edge < 3 - k, head * turned[0:8, 3 + k : 4 + k], 0.0)
            held = pltpu.roll(held, 5 + k, 0)
            rim = rim + taps[k : k + 1, c] * held
            parts[k] = parts[k] + jnp.sum(outside * held, axis=0, keepdims=True)
        rim_o[s, :, c] = rim.astype(BF)
        cg[0:5, c] = cg[0:5, c] + jnp.concatenate(parts, axis=0)

    for s in every:
        mt = meta[s]
        turned = lines_of(mt)
        cum, dt = sc[s, 0:HP, :], sc[s, HP:, :]
        b, c = bc[rows[s], :N], bc[rows[s], N:]
        lead = (jnp.exp(cum) * (mt[0:1, :] == mt[1:2, :]).astype(F4)).astype(BF)
        tail0, lead_last = decays(cum, mt)
        tail = (tail0 * dt).astype(BF)
        scores = mm_nt(c, b)
        inside = inside_of(mt)
        cum_cols = cols_of(cum)
        d_sc = jnp.zeros((QC, QC), F4)
        sums = jnp.zeros((QC, 128), F4)
        tq = jnp.zeros((HP, QC), F4)
        lv = jnp.zeros((HP, QC), F4)
        d_b = jnp.zeros((QC, N), F4)
        d_c = jnp.zeros((QC, N), F4)
        for j, at in enumerate(tiles(XW // 128)):
            ej = e[:, at]
            xp = x_r[rows[s], at]
            dyp = dy_r[rows[s], at]
            xf = xp.astype(F4)
            dyf = dyp.astype(F4)
            before = ent[s, :, at]
            now = ds[s, :, at]
            after = now.astype(BF)
            tailj = spread(tail, ej)
            u = tailj * mm(b, after)
            led = dyf * spread(lead, ej)
            tq = tq + gather_heads(xf * u, ej)
            lv = lv + gather_heads(led * mm(c, before), ej)
            ledb = led.astype(BF)
            d_b = d_b + mm_nt((xf * tailj).astype(BF), after)
            d_c = d_c + mm_nt(ledb, before)
            colbuf[s, 0:1, at] = jnp.sum(now * before.astype(F4), axis=0, keepdims=True)
            colbuf[s, 1:2, at] = jnp.sum(dyf * xf, axis=0, keepdims=True)
            ds[s, :, at] = now * spread_fine(lead_last[:, :8], ej)[0:1, :] + mm_tn(c, ledb)
            dx = u + skip[:, at] * dyf
            for half in range(2):
                h = 2 * j + half
                gap = jnp.where(inside, cum_cols[:, h : h + 1] - sc[s, h : h + 1, :], NEG)
                dec = jnp.exp(gap)
                dtr = sc[s, HP + h : HP + h + 1, :]
                sl_h = scores * dec
                d_m = mm_nt(dyp, xp * halves[half])
                g = d_m * sl_h
                rowbuf[s, h : h + 1, :] = jnp.sum(g, axis=0, keepdims=True)
                sums = jnp.where(lane == h, jnp.sum(g * dtr, axis=1, keepdims=True), sums)
                d_sc = d_sc + d_m * (dec * dtr)
                dx = dx + mm_tn((sl_h * dtr).astype(BF), dyp * halves[half])
            conv_back(s, at, xr[rows[s], at].astype(F4), dx.astype(BF).astype(F4), turned)
        d_scb = d_sc.astype(BF)
        d_b = d_b + mm_tn(d_scb, c)
        d_c = d_c + mm(d_scb, b)
        conv_back(s, slice(XW, XW + N), br[rows[s], :N].astype(F4), d_b, turned)
        conv_back(s, slice(XW + N, CW), br[rows[s], N:].astype(F4), d_c, turned)
        ecol = rowbuf[s]
        both = gather_fine(colbuf[s], e[...])
        at_end = jnp.sum(tq, axis=1, keepdims=True) + lead_last * both[:, 0:1]
        d_cum = jnp.transpose(sums)[:HP] - dt * ecol - tq + lv
        d_la = running(d_cum + jnp.where(place == QC - 1, at_end, 0.0), True)
        v = jnp.transpose(rr[rows[s], :].astype(F4))[:HP] + hp[0]
        d_rate = (ecol + tq / jnp.maximum(dt, 1e-30) + d_la * hp[1]) * sigmoid(v)
        draw_o[rows[s], CW:] = cols_of(d_rate).astype(BF)
        hg[0] = hg[0] + d_rate
        hg[1] = hg[1] + d_la * dt * hp[1]
        hg[2] = hg[2] + jnp.where(place == 0, both[:, 1:2], 0.0)
    cg_o[...] = cg[...]
    hg_o[...] = hg[...]


def scan_back(seqs, x, bc, sl, sc, meta, ent, dy, d_end, raw, halo, taps, hp, skip, e):
    length = x.shape[0]
    span = seqs * QC
    n = length // span
    sd = jax.ShapeDtypeStruct
    return pl.pallas_call(
        back_kernel,
        grid=(n,),
        in_specs=[
            behind(n, span, XW),
            behind(n, span, 2 * N),
            behind(n, span, CW),
            behind3(n, seqs, 2 * HP, 128),
            behind3(n, seqs, 8, 128),
            behind3(n, seqs, N, XW),
            behind(n, span, XW),
            fixed(seqs, N, XW),
            behind(n, span, XW),
            behind(n, span, 2 * N, XW // (2 * N)),
            behind(n, span, 128, CW // 128),
            fixed(seqs, 8, CW),
            fixed(8, CW),
            fixed(2, HP, 128),
            fixed(1, XW),
            fixed(HP, XW),
        ],
        out_specs=[behind(n, span, AW), fixed(seqs, 8, CW), fixed(8, CW), fixed(3, HP, 128)],
        out_shape=[
            sd((length, AW), BF),
            sd((seqs, 8, CW), BF),
            sd((8, CW), F4),
            sd((3, HP, 128), F4),
        ],
        scratch_shapes=[
            pltpu.VMEM((seqs, N, XW), F4),
            pltpu.VMEM((seqs, 8, CW), F4),
            pltpu.VMEM((seqs, 8, XW), F4),
            pltpu.VMEM((seqs, HP, 128), F4),
            pltpu.VMEM((8, CW), F4),
            pltpu.VMEM((3, HP, 128), F4),
        ],
        compiler_params=pltpu.CompilerParams(vmem_limit_bytes=LIMIT),
        cost_estimate=work(length, 2),
        name="scan_back",
    )(x, bc, sl, sc, meta, ent, dy, d_end, raw, raw, raw, halo, taps, hp, skip, e)


def pad_lanes(v, width):
    return jnp.pad(v, [(0, 0)] * (v.ndim - 1) + [(0, width - v.shape[-1])])


def carried(state, decay, hops, by):
    total = shift(state, CHAIN, by)
    if hops == 1:
        return total
    total, product = total.astype(F4), 1.0
    for j in range(2, hops + 1):
        product = product * shift(decay, CHAIN, by * (j - 1))
        total = total + product * shift(state, CHAIN, by * j).astype(F4)
    return total.astype(BF)


def shards(
    tokens_in, seg_ids, in_norm, z_proj, xbc_proj, dt_proj, conv_taps, conv_bias,
    dt_bias, a_log, d_skip, gate_norm, out_proj, out_cotangent,
):
    seqs, rows, width = tokens_in.shape
    length = seg_ids.shape[1]
    block = rows * GROUP
    n_blocks = length // block
    hops = min(-(-(length // 4 - 1) // block), n_blocks - 1)
    n_sums = lax.axis_size("dp") * n_blocks
    hl = lax.axis_index("hl")
    own_rows = z_proj.shape[0]

    def collected(part):
        return lax.all_gather(part, "hl", axis=0).reshape(GROUP * seqs * rows, width)

    def quarters(w):
        return w.reshape(w.shape[0], GROUP, -1).transpose(1, 0, 2)

    bc_cols = jnp.broadcast_to(xbc_proj[None, :, DI:], (GROUP, own_rows, 2 * N))
    parts = [quarters(xbc_proj[:, :DI]), bc_cols, pad_lanes(quarters(dt_proj), 128), quarters(z_proj)]
    in_mine = lax.all_to_all(jnp.concatenate(parts, axis=-1), "hl", 0, 0, tiled=True)
    in_mine = in_mine.reshape(GROUP * own_rows, AW + XW)
    pairs = [(f, (f % n_sums) * GROUP + f // n_sums) for f in range(GROUP * n_sums)]
    wo_mine = lax.ppermute(out_proj, EVERY, pairs)
    in_mine, wo_mine, tokens_now = lax.optimization_barrier((in_mine, wo_mine, tokens_in))
    tokens = collected(tokens_now)
    cot = collected(out_cotangent)
    wx, wz = sums_gather(in_mine, [(0, AW), (AW, AW + XW)])
    [wo] = sums_gather(wo_mine, [(0, width)])

    def mine(v, size):
        return lax.dynamic_slice_in_dim(v, hl * size, size, axis=-1)

    taps = jnp.concatenate([conv_taps, conv_bias[None]], axis=0)
    taps = jnp.concatenate([mine(taps[:, :DI], XW), taps[:, DI:]], axis=1)
    taps = jnp.pad(taps, ((0, 3), (0, 0)))
    hp = jnp.stack([mine(dt_bias, HG), -jnp.exp(mine(a_log, HG))])
    hp = jnp.broadcast_to(jnp.pad(hp, ((0, 0), (0, HP - HG)))[:, :, None], (2, HP, 128))
    skip = jnp.repeat(mine(d_skip, HG), PS)[None]
    gain = mine(gate_norm, XW)[None]
    e = (jnp.arange(HP)[:, None] == jnp.arange(XW)[None, :] // PS).astype(BF)

    start = lax.axis_index(CHAIN) * block
    seg_pad = jnp.concatenate([jnp.full((seqs, 8), -1, jnp.int32), seg_ids], axis=1)
    near = lax.dynamic_slice_in_dim(seg_pad, start, block + 8, axis=1)
    seg = near[:, 8:].reshape(seqs, GROUP, QC)
    lines = [seg, jnp.broadcast_to(near[:, 7 : 7 + block : QC][:, :, None], seg.shape)]
    lines.append(jnp.broadcast_to(seg[:, :, QC - 1 :], seg.shape))
    for k in range(KW - 1):
        lines.append((near[:, 5 + k : 5 + k + block].reshape(seg.shape) == seg).astype(jnp.int32))
    lines.extend([jnp.zeros_like(seg)] * 2)
    meta = jnp.stack(lines, axis=2).astype(F4)
    meta = meta.transpose(1, 0, 2, 3).reshape(GROUP * seqs, 8, QC)

    tokens, wx, wz, wo, meta, taps, hp, skip, gain, e = lax.optimization_barrier(
        (tokens, wx, wz, wo, meta, taps, hp, skip, gain, e)
    )
    normed = norm_rows(tokens.astype(F4), in_norm).astype(BF)
    raw = mm(normed, wx).astype(BF)
    last = raw.reshape(GROUP, seqs, rows, AW)[GROUP - 1, :, rows - 8 :, :CW]
    halo = shift(last, CHAIN, 1)
    x, bc, sl, sc, state, decay = front(seqs, raw, halo, meta, taps, hp, e)
    decay_row = jnp.repeat(decay[:, :HG, 0], PS, axis=-1)[:, None]
    s_in = carried(state, decay_row, hops, 1)
    gates = mm(normed, wz)
    y, ent, squares = scan(seqs, x, bc, sc, meta, s_in, gates, skip, e)

    def team_sum(part):
        total = part
        for k in range(1, GROUP):
            total = total + swap(part, "hl", k)
        return total

    def spread_sum(part):
        total = lax.psum_scatter(part, "hl", scatter_dimension=0, tiled=True)
        return total.reshape(seqs, rows, width).astype(F4)

    squares = team_sum(squares)
    scale = lax.rsqrt(squares.reshape(-1, 1) * (1.0 / DI) + EPS)
    s_val = y.astype(F4) * jax.nn.silu(gates)
    gated = (s_val * scale * gain).astype(BF)
    out_rows = mm(gated, wo).astype(BF)
    cot, out_rows = lax.optimization_barrier((cot, out_rows))
    d_gated = mm_nt(cot, wo)
    along = team_sum(jnp.sum(d_gated * gain * s_val, axis=1).reshape(squares.shape))
    out_sum = spread_sum(out_rows)
    o_grad = mm_tn(gated, cot).astype(BF)
    dy, dz, gg, d_state = gate(seqs, y, gates, d_gated, squares, along, bc, sc, meta, gain, e)
    d_end = carried(d_state, decay_row, hops, -1)
    z_grad = mm_tn(normed, dz).astype(BF)
    from_z = mm_nt(dz, wz)
    dy, o_grad, z_grad, from_z = lax.optimization_barrier((dy, o_grad, z_grad, from_z))
    draw, rim, conv_total, head_total = scan_back(
        seqs, x, bc, sl, sc, meta, ent, dy, d_end, raw, halo, taps, hp, skip, e
    )
    rim = shift(rim, CHAIN, -1)
    o_half = team_halves(o_grad)
    z_half = team_halves(z_grad)
    rim, o_half, z_half, out_sum = lax.optimization_barrier((rim, o_half, z_half, out_sum))
    for s in range(seqs):
        at = ((GROUP - 1) * seqs + s) * rows + rows - 8
        edge = draw[at : at + 8, :CW].astype(F4) + rim[s].astype(F4)
        draw = lax.dynamic_update_slice(draw, edge.astype(BF), (at, 0))
    d_low = (from_z + mm_nt(draw, wx)).astype(BF)
    d_low, o_half, z_half, draw = lax.optimization_barrier((d_low, o_half, z_half, draw))
    d_sum = spread_sum(d_low)
    x_grad = mm_tn(normed, draw).astype(BF)
    norm_total = jnp.sum(x_grad.astype(F4) * wx.astype(F4), axis=1)
    norm_total = norm_total + jnp.sum(z_grad.astype(F4) * wz.astype(F4), axis=1)
    x_own = chain_sum(team_halves(x_grad)).reshape(GROUP, own_rows, AW)
    z_own = chain_sum(z_half).reshape(GROUP, own_rows, XW)
    o_own = chain_sum(o_half)
    out_proj_grad = lax.ppermute(o_own, EVERY, [(b, a) for a, b in pairs]).astype(F4)
    z_all = lax.all_to_all(z_own, "hl", 0, 0, tiled=True)

    pieces = [
        conv_total[:5, :XW].reshape(-1),
        gg[0],
        jnp.sum(head_total, axis=2).reshape(-1),
        conv_total[:5, XW:].reshape(-1),
        norm_total / in_norm,
    ]
    sizes = [p.shape[0] for p in pieces]
    pack = jnp.concatenate(pieces)
    lines_n = -(-pack.shape[0] // 1024) * 8
    total = lines_n * 128
    pack = jnp.pad(pack, (0, total - pack.shape[0])).reshape(lines_n, 128)
    for axis in SUMS:
        pack = pack + sum(swap(pack, axis, k) for k in range(1, lax.axis_size(axis)))
    high = pack.astype(BF)
    rest = (pack - high.astype(F4)).astype(BF)
    extra = -(-2 * total // (AW * 16)) * 16
    small = jnp.concatenate([high.reshape(-1), rest.reshape(-1)])
    small = jnp.pad(small, (0, extra * AW - 2 * total)).reshape(1, extra, AW)
    x_own = jnp.concatenate([x_own, jnp.broadcast_to(small, (GROUP, extra, AW))], axis=1)
    x_all = lax.all_to_all(x_own, "hl", 0, 0, tiled=True)
    x_all, d_sum = lax.optimization_barrier((x_all, d_sum))

    u = tokens_in.astype(F4)
    scale = lax.rsqrt(jnp.mean(u * u, axis=-1, keepdims=True) + EPS)
    hat = u * scale
    dh = d_sum * in_norm
    d_u = scale * (dh - hat * jnp.mean(dh * hat, axis=-1, keepdims=True))
    tokens_grad = d_u + out_cotangent.astype(F4)
    layer_out = (tokens_in.astype(F4) + out_sum).astype(BF)
    z_proj_grad = z_all.transpose(1, 0, 2).reshape(own_rows, DI).astype(F4)
    x_parts = x_all[:, :own_rows]
    xs = x_parts[:, :, :XW].transpose(1, 0, 2).reshape(own_rows, DI).astype(F4)
    bc_grad = jnp.sum(x_parts[:, :, XW:CW].astype(F4), axis=0)
    xbc_proj_grad = jnp.concatenate([xs, bc_grad], axis=1)
    dt_parts = x_parts[:, :, CW : CW + HG].transpose(1, 0, 2)
    dt_proj_grad = dt_parts.reshape(own_rows, H).astype(F4)
    got = x_all[:, own_rows:].astype(F4).reshape(GROUP, -1)
    flat = got[:, :total] + got[:, total : 2 * total]
    cuts = []
    low = 0
    for size in sizes:
        cuts.append(flat[:, low : low + size])
        low = low + size
    conv_x = cuts[0].reshape(GROUP, 5, XW).transpose(1, 0, 2).reshape(5, DI)
    conv_all = jnp.concatenate([conv_x, jnp.sum(cuts[3], axis=0).reshape(5, 2 * N)], axis=1)
    per_head = cuts[2].reshape(GROUP, 3, HP)[:, :, :HG].transpose(1, 0, 2).reshape(3, H)
    return (
        layer_out,
        tokens_grad,
        jnp.sum(cuts[4], axis=0),
        z_proj_grad,
        xbc_proj_grad,
        dt_proj_grad,
        conv_all[:4],
        conv_all[4],
        per_head[0],
        per_head[1],
        per_head[2],
        cuts[1].reshape(DI),
        out_proj_grad,
    )


def solution(mesh):
    sizes = dict(mesh.shape)
    grid = mesh.devices.reshape(sizes["dp"], sizes["ctx"], sizes["hd"] // GROUP, GROUP)
    fine = Mesh(grid, ("dp", "ctx", "hh", "hl"))
    tok = P("dp", ("ctx", "hh", "hl"), None)
    wgt = P(("dp", "ctx", "hh", "hl"), None)
    in_specs = (tok, P("dp", None), P(), wgt, wgt, wgt, P(), P(), P(), P(), P(), P(), wgt, tok)
    out_specs = (tok, tok, P(), wgt, wgt, wgt, P(), P(), P(), P(), P(), P(), wgt)
    return jax.shard_map(shards, mesh=fine, in_specs=in_specs, out_specs=out_specs, check_vma=False)
```

```python
import jax
import jax.numpy as jnp
from jax import lax
from jax.experimental import pallas as pl
from jax.experimental.pallas import tpu as pltpu
from jax.sharding import Mesh, PartitionSpec as P

H = 48
PS = 64
N = 128
KW = 4
DI = 3072
GROUP = 4
HG = H // GROUP
HP = 16
XW = HG * PS
CW = XW + 2 * N
AW = CW + 128
QC = 128
EPS = 1e-05
NEG = -1e30
BF = jnp.bfloat16
F4 = jnp.float32
LIMIT = 48 * 1024 * 1024
SUMS = ("dp", "ctx", "hh")
CHAIN = ("ctx", "hh")
EVERY = ("dp", "ctx", "hh", "hl")


def swap(part, axis, k):
    count = lax.axis_size(axis)
    return lax.ppermute(part, axis, [(i, i ^ k) for i in range(count)])


def shift(part, axes, by):
    count = 1
    for axis in axes:
        count = count * lax.axis_size(axis)
    pairs = [(i, i + by) for i in range(count) if 0 <= i + by < count]
    return lax.ppermute(part, axes, pairs)


def mm(a, b):
    return jnp.dot(a, b, preferred_element_type=F4)


def mm_nt(a, b):
    return lax.dot_general(a, b, (((1,), (1,)), ((), ())), preferred_element_type=F4)


def mm_tn(a, b):
    return lax.dot_general(a, b, (((0,), (0,)), ((), ())), preferred_element_type=F4)


def grown(lead_last, e):
    v = lead_last[:, :8]
    hi = v.astype(BF)
    lo = (v - hi.astype(F4)).astype(BF)
    return (mm_tn(hi, e[:HP, :]) + mm_tn(lo, e[:HP, :]))[0:1, :]


def gather_heads(w, e):
    return mm_nt(e, w.astype(BF))


def gather_fine(w, e):
    hi = w.astype(BF)
    lo = (w - hi.astype(F4)).astype(BF)
    return mm_nt(e, hi) + mm_nt(e, lo)


def turn(v):
    return jnp.transpose(v.astype(F4)).astype(BF)


def sigmoid(v):
    return 0.5 * jnp.tanh(0.5 * v) + 0.5


def norm_rows(values, gain):
    return values * lax.rsqrt(jnp.mean(values * values, axis=-1, keepdims=True) + EPS) * gain


def running(v, back):
    r = lax.broadcasted_iota(jnp.int32, (QC, QC), 0)
    q = lax.broadcasted_iota(jnp.int32, (QC, QC), 1)
    ones = ((r >= q) if back else (r <= q)).astype(BF)
    hi = v.astype(BF)
    rest = v - hi.astype(F4)
    mid = rest.astype(BF)
    lo = (rest - mid.astype(F4)).astype(BF)
    got = mm(jnp.concatenate([hi, mid, lo], axis=0), ones)
    n = v.shape[0]
    return got[:n] + got[n : 2 * n] + got[2 * n :]


def lines_of(mt):
    return jnp.transpose(jnp.concatenate([mt, jnp.zeros((QC - 8, QC), F4)], axis=0))


def full(col):
    return jnp.broadcast_to(col, (QC, 128))


def tiles(count, width=128):
    return [slice(j * width, j * width + width) for j in range(count)]


WIDE = 256


def stacked(v, halves):
    return jnp.concatenate([v * halves[0], v * halves[1]], axis=0)


def col_of(row):
    return jnp.transpose(jnp.broadcast_to(row, (QC, QC)))


def cols_of(v):
    return jnp.transpose(jnp.concatenate([v, jnp.zeros((QC - HP, QC), F4)], axis=0))


def place_kernel(place, *refs):
    out = refs[-1]
    rows = refs[0].shape[0]
    for k, ref in enumerate(refs[:-1]):
        slot = jnp.bitwise_xor(place[0], k)
        out[pl.ds(pl.multiple_of(slot * rows, rows), rows), :] = ref[...]


def placed(place, pieces):
    rows, width = pieces[0].shape
    vm = pl.BlockSpec(memory_space=pltpu.VMEM)
    return pl.pallas_call(
        place_kernel,
        out_shape=jax.ShapeDtypeStruct((len(pieces) * rows, width), BF),
        in_specs=[pl.BlockSpec(memory_space=pltpu.SMEM)] + [vm] * len(pieces),
        out_specs=vm,
        compiler_params=pltpu.CompilerParams(vmem_limit_bytes=LIMIT),
        name="place_rows",
    )(place, *pieces)


def joined(cur, got, side):
    low = jnp.where(side == 0, cur, got)
    high = jnp.where(side == 0, got, cur)
    return jnp.concatenate([low, high], axis=0)


def plain():
    return lax.axis_size("hh") == 1


def near_rows(mine):
    if not plain() or mine.shape[0] % 16:
        return [mine]
    return [mine] + [swap(mine, "ctx", k) for k in range(1, lax.axis_size("ctx"))]


def all_rows(pieces, cuts):
    if len(pieces) == 1:
        whole = lax.all_gather(pieces[0], SUMS, axis=0, tiled=True)
        return [whole[:, a:b] for a, b in cuts]
    stack = placed(lax.axis_index("ctx").astype(jnp.int32).reshape(1), pieces)
    got = swap(stack, "dp", 1)
    side = lax.axis_index("dp")
    return [joined(stack[:, a:b], got[:, a:b], side) for a, b in cuts]


def half_of(v, side):
    return lax.dynamic_slice_in_dim(v, side * (v.shape[1] // 2), v.shape[1] // 2, axis=1)


def chain_pieces(keep, got):
    count = lax.axis_size("ctx")
    ctx = lax.axis_index("ctx")
    keep = keep.reshape(count, -1, keep.shape[-1])
    got = got.reshape(keep.shape)
    pieces = []
    for k in range(count):
        at = jnp.bitwise_xor(ctx, k)
        parts = [lax.dynamic_index_in_dim(v, at, 0, keepdims=False) for v in (keep, got)]
        pieces.append((parts[0].astype(F4) + parts[1].astype(F4)).astype(BF))
    return pieces


def chain_sum(pieces):
    out = pieces[0].astype(F4)
    for k in range(1, len(pieces)):
        out = out + swap(pieces[k], "ctx", k).astype(F4)
    return out.astype(BF)


def work(length, us):
    flops = int(us * 1e9) * length // 1024
    return pl.CostEstimate(flops=flops, transcendentals=0, bytes_accessed=length * 8192)


def fixed(*shape):
    return pl.BlockSpec(shape, lambda i: (0,) * len(shape))


def ahead(rows, width, at=0):
    return pl.BlockSpec((rows, width), lambda i: (i, at))


def ahead3(seqs, *shape):
    return pl.BlockSpec((seqs, *shape), lambda i: (i, 0, 0))


def behind(n, rows, width, at=0):
    return pl.BlockSpec((rows, width), lambda i: (n - 1 - i, at))


def behind3(n, seqs, *shape):
    return pl.BlockSpec((seqs, *shape), lambda i: (n - 1 - i, 0, 0))


def decays(cum, mt):
    last = cum[:, QC - 1 : QC]
    same_last = (mt[0:1, :] == mt[2:3, :]).astype(F4)
    follows = (mt[1:2, :] == mt[2:3, :]).astype(F4)
    tail0 = jnp.exp(last - cum) * same_last
    lead_last = jnp.exp(last) * follows
    return tail0, lead_last


def front_kernel(
    xr, br, rr, halo, meta, taps, hp, e, x_o, bc_o, sl_o, sc_o, st_o, dec_o, buf, st, dec
):
    i = pl.program_id(0)
    seqs = halo.shape[0]

    @pl.when(i == 0)
    def _():
        buf[:, 0:8, :] = halo[...].astype(F4)
        st[...] = jnp.zeros_like(st)
        dec[...] = jnp.ones_like(dec)

    @pl.when(i > 0)
    def _():
        buf[:, 0:8, :] = buf[:, QC : QC + 8, :]

    every = range(seqs)
    rows = [slice(s * QC, s * QC + QC) for s in every]
    tails, lasts = [], []
    for s in every:
        v = jnp.transpose(rr[rows[s], :].astype(F4))[:HP] + hp[0]
        dt = jnp.maximum(v, 0.0) + jnp.log1p(jnp.exp(-jnp.abs(v)))
        cum = running(dt * hp[1], False)
        sc_o[s, 0:HP, :] = cum
        sc_o[s, HP:, :] = dt
        tail0, lead_last = decays(cum, meta[s])
        dec[s] = dec[s] * lead_last
        tails.append(cols_of(tail0 * dt).astype(BF))
        lasts.append(grown(lead_last, e))
    order = tiles(CW // 128)
    n_x = XW // 128
    for s in every:
        turned = lines_of(meta[s])
        masks = [full(turned[:, 3 + k : 4 + k]) for k in range(3)]
        for j in [*range(n_x, len(order)), *range(n_x)]:
            c = order[j]
            if j < n_x:
                own = xr[rows[s], c].astype(F4)
            else:
                own = br[rows[s], j * 128 - XW : j * 128 - XW + 128].astype(F4)
            buf[s, 8 : QC + 8, c] = own
            mixed = taps[4:5, c] + taps[3:4, c] * own
            for k in range(3):
                mixed = mixed + taps[k : k + 1, c] * (
                    buf[s, 5 + k : 5 + k + QC, c] * masks[k]
                )
            sig = sigmoid(mixed)
            act = (mixed * sig).astype(BF)
            sl_o[rows[s], c] = (sig + mixed * sig * (1.0 - sig)).astype(BF)
            if j < n_x:
                x_o[rows[s], c] = act
                if j % 2:
                    c2 = slice(j * 128 - 128, j * 128 + 128)
                    pair = jnp.concatenate([held, act], axis=1).astype(F4)
                    xw = (pair * mm(tails[s], e[:, c2])).astype(BF)
                    st[s, :, c2] = st[s, :, c2] * lasts[s][:, c2] + mm(b_t, xw)
                held = act
            else:
                bc_o[rows[s], j * 128 - XW : j * 128 - XW + 128] = act
                if j == n_x:
                    b_t = turn(act)
    st_o[...] = st[...].astype(BF)
    dec_o[...] = dec[...]


def front(seqs, raw, halo, meta, taps, hp, e):
    length = raw.shape[0]
    span = seqs * QC
    sd = jax.ShapeDtypeStruct
    return pl.pallas_call(
        front_kernel,
        grid=(length // span,),
        in_specs=[
            ahead(span, XW),
            ahead(span, 2 * N, XW // (2 * N)),
            ahead(span, 128, CW // 128),
            fixed(seqs, 8, CW),
            ahead3(seqs, 8, 128),
            fixed(8, CW),
            fixed(2, HP, 128),
            fixed(128, XW),
        ],
        out_specs=[
            ahead(span, XW),
            ahead(span, 2 * N),
            ahead(span, CW),
            ahead3(seqs, 2 * HP, 128),
            fixed(seqs, N, XW),
            fixed(seqs, HP, 128),
        ],
        out_shape=[
            sd((length, XW), BF),
            sd((length, 2 * N), BF),
            sd((length, CW), BF),
            sd((length // QC, 2 * HP, 128), F4),
            sd((seqs, N, XW), BF),
            sd((seqs, HP, 128), F4),
        ],
        scratch_shapes=[
            pltpu.VMEM((seqs, QC + 8, CW), F4),
            pltpu.VMEM((seqs, N, XW), F4),
            pltpu.VMEM((seqs, HP, 128), F4),
        ],
        compiler_params=pltpu.CompilerParams(vmem_limit_bytes=LIMIT),
        cost_estimate=work(length, 1),
        name="conv_state",
    )(raw, raw, raw, halo, meta, taps, hp, e)


def lane_halves():
    lane = lax.broadcasted_iota(jnp.int32, (1, 128), 1)
    return [(lane < PS).astype(BF), (lane >= PS).astype(BF)]


def inside_of(mt):
    r = lax.broadcasted_iota(jnp.int32, (QC, QC), 0)
    q = lax.broadcasted_iota(jnp.int32, (QC, QC), 1)
    return (col_of(mt[0:1, :]) == mt[0:1, :]) & (r >= q)


def scan_kernel(x_r, bc, sc, meta, s_in, z_r, skip, gain, e, y_o, sg_o, ent_o, sum_o, st):
    i = pl.program_id(0)
    seqs = s_in.shape[0]
    every = range(seqs)
    rows = [slice(s * QC, s * QC + QC) for s in every]

    @pl.when(i == 0)
    def _():
        st[...] = s_in[...].astype(F4)

    halves = lane_halves()
    for s in every:
        mt = meta[s]
        cum, dt = sc[s, 0:HP, :], sc[s, HP:, :]
        b, c = bc[rows[s], :N], bc[rows[s], N:]
        lead = cols_of(jnp.exp(cum) * (mt[0:1, :] == mt[1:2, :]).astype(F4)).astype(BF)
        tail0, lead_last = decays(cum, mt)
        tail = cols_of(tail0 * dt).astype(BF)
        b_t = turn(b)
        scores = mm_nt(c, b)
        inside = inside_of(mt)
        cum_cols = cols_of(cum)
        squares = jnp.zeros((QC, 128), F4)
        grow = grown(lead_last, e)
        for j, at in enumerate(tiles(XW // WIDE, WIDE)):
            ej = e[:, at]
            xf = x_r[rows[s], at].astype(F4)
            now = st[s, :, at]
            before = now.astype(BF)
            ent_o[s, :, at] = before
            wide = mm(lead, ej) * mm(c, before) + skip[:, at] * xf
            xw = (xf * mm(tail, ej)).astype(BF)
            st[s, :, at] = now * grow[:, at] + mm(b_t, xw)
            for k in range(WIDE // 128):
                here = slice(j * WIDE + k * 128, j * WIDE + k * 128 + 128)
                xp = x_r[rows[s], here]
                ws = []
                for half in range(2):
                    h = (j * WIDE + k * 128) // PS + half
                    gap = jnp.where(inside, cum_cols[:, h : h + 1] - sc[s, h : h + 1, :], NEG)
                    ws.append((scores * jnp.exp(gap) * sc[s, HP + h : HP + h + 1, :]).astype(BF))
                y = wide[:, k * 128 : k * 128 + 128] + mm(jnp.concatenate(ws, axis=1), stacked(xp, halves))
                low = y.astype(BF)
                y_o[rows[s], here] = low
                z = z_r[rows[s], here]
                v = low.astype(F4) * z * sigmoid(z)
                squares = squares + v * v
                sg_o[rows[s], here] = (v * gain[:, here]).astype(BF)
        sum_o[s] = jnp.sum(jnp.transpose(squares), axis=0, keepdims=True)


def scan(seqs, x, bc, sc, meta, s_in, z, skip, gain, e):
    length = x.shape[0]
    span = seqs * QC
    chunks = length // QC
    sd = jax.ShapeDtypeStruct
    return pl.pallas_call(
        scan_kernel,
        grid=(length // span,),
        in_specs=[
            ahead(span, XW),
            ahead(span, 2 * N),
            ahead3(seqs, 2 * HP, 128),
            ahead3(seqs, 8, 128),
            fixed(seqs, N, XW),
            ahead(span, XW),
            fixed(1, XW),
            fixed(1, XW),
            fixed(128, XW),
        ],
        out_specs=[ahead(span, XW), ahead(span, XW), ahead3(seqs, N, XW), ahead3(seqs, 1, QC)],
        out_shape=[
            sd((length, XW), BF),
            sd((length, XW), BF),
            sd((chunks, N, XW), BF),
            sd((chunks, 1, QC), F4),
        ],
        scratch_shapes=[pltpu.VMEM((seqs, N, XW), F4)],
        compiler_params=pltpu.CompilerParams(vmem_limit_bytes=LIMIT),
        cost_estimate=work(length, 1),
        name="scan_gate",
    )(x, bc, sc, meta, s_in, z, skip, gain, e)


def gate_kernel(y_r, z_r, dg_r, sq, al, bc, sc, meta, gain, e, dy_o, dz_o, gg_o, ds_o, ds, gg):
    i = pl.program_id(0)
    seqs = ds.shape[0]
    every = range(seqs)
    rows = [slice(s * QC, s * QC + QC) for s in every]

    @pl.when(i == 0)
    def _():
        gg[...] = jnp.zeros_like(gg)
        ds[...] = jnp.zeros_like(ds)

    for s in every:
        mt = meta[s]
        cum = sc[s, 0:HP, :]
        c = bc[rows[s], N:]
        scale = lax.rsqrt(sq[s] * (1.0 / DI) + EPS)
        rstd = jnp.concatenate([col_of(scale)] * (WIDE // 128), axis=1)
        pull = col_of(al[s] * (scale * scale * scale) * (1.0 / DI))
        pull = jnp.concatenate([pull] * (WIDE // 128), axis=1)
        lead = cols_of(jnp.exp(cum) * (mt[0:1, :] == mt[1:2, :]).astype(F4)).astype(BF)
        _, lead_last = decays(cum, mt)
        c_t = turn(c)
        grow = grown(lead_last, e)
        for at in tiles(XW // WIDE, WIDE):
            ej = e[:, at]
            y = y_r[rows[s], at].astype(F4)
            z = z_r[rows[s], at]
            sig = sigmoid(z)
            act = z * sig
            v = y * act
            dg = dg_r[rows[s], at] * rstd
            gg[0:1, at] = gg[0:1, at] + jnp.sum(dg * v, axis=0, keepdims=True)
            d_v = dg * gain[:, at] - v * pull
            dy = (d_v * act).astype(BF)
            dy_o[rows[s], at] = dy
            dz_o[rows[s], at] = (d_v * y * (sig + act * (1.0 - sig))).astype(BF)
            led = (dy.astype(F4) * mm(lead, ej)).astype(BF)
            ds[s, :, at] = ds[s, :, at] * grow[:, at] + mm(c_t, led)
    ds_o[...] = ds[...].astype(BF)
    gg_o[...] = gg[...]


def gate(seqs, y, z, dg, sq, al, bc, sc, meta, gain, e):
    length = y.shape[0]
    span = seqs * QC
    n = length // span
    sd = jax.ShapeDtypeStruct
    wide = behind(n, span, XW)
    line = behind3(n, seqs, 1, QC)
    return pl.pallas_call(
        gate_kernel,
        grid=(n,),
        in_specs=[
            wide,
            wide,
            wide,
            line,
            line,
            behind(n, span, 2 * N),
            behind3(n, seqs, 2 * HP, 128),
            behind3(n, seqs, 8, 128),
            fixed(1, XW),
            fixed(128, XW),
        ],
        out_specs=[wide, wide, fixed(8, XW), fixed(seqs, N, XW)],
        out_shape=[
            sd((length, XW), BF),
            sd((length, XW), BF),
            sd((8, XW), F4),
            sd((seqs, N, XW), BF),
        ],
        scratch_shapes=[pltpu.VMEM((seqs, N, XW), F4), pltpu.VMEM((8, XW), F4)],
        compiler_params=pltpu.CompilerParams(vmem_limit_bytes=LIMIT),
        cost_estimate=work(length, 1),
        name="gate_back",
    )(y, z, dg, sq, al, bc, sc, meta, gain, e)


def back_kernel(
    x_r, bc, sl, sc, meta, ent, dy_r, d_end, xr, br, rr, halo, taps, hp, skip, e,
    draw_o, rim_o, cg_o, hg_o,
    ds, carry, colbuf, rowbuf, cg, hg,
):
    i = pl.program_id(0)
    seqs = ds.shape[0]
    every = range(seqs)
    rows = [slice(s * QC, s * QC + QC) for s in every]
    first = (i == pl.num_programs(0) - 1).astype(F4)

    @pl.when(i == 0)
    def _():
        ds[...] = d_end[...].astype(F4)
        carry[...] = jnp.zeros_like(carry)
        cg[...] = jnp.zeros_like(cg)
        hg[...] = jnp.zeros_like(hg)
        colbuf[...] = jnp.zeros_like(colbuf)
        rowbuf[...] = jnp.zeros_like(rowbuf)

    halves = lane_halves()
    lane = lax.broadcasted_iota(jnp.int32, (1, 128), 1)
    token = lax.broadcasted_iota(jnp.int32, (QC, 128), 0)
    edge = lax.broadcasted_iota(jnp.int32, (8, 128), 0)
    place = lax.broadcasted_iota(jnp.int32, (HP, QC), 1)

    near_of = {}

    def conv_back(s, c, own, d_act, turned):
        dm = d_act * sl[rows[s], c].astype(F4)
        near = near_of[s]
        shifted = [dm]
        for k in range(3):
            ready = shifted[-1] * near
            moved = pltpu.roll(ready, QC - 1, 0)
            shifted.append(jnp.where(token == QC - 1, carry[s, k : k + 1, c], moved))
            carry[s, k : k + 1, c] = ready[0:1, :]
        d_raw = taps[3:4, c] * shifted[0]
        for k in range(3):
            d_raw = d_raw + taps[2 - k : 3 - k, c] * shifted[k + 1]
        draw_o[rows[s], c] = d_raw.astype(BF)
        parts = [jnp.sum(own * v, axis=0, keepdims=True) for v in shifted[::-1]]
        parts.append(jnp.sum(dm, axis=0, keepdims=True))
        head = dm[0:8, :]
        outside = halo[s, :, c].astype(F4) * first
        rim = jnp.zeros((8, 128), F4)
        for k in range(3):
            held = jnp.where(edge < 3 - k, head * turned[0:8, 3 + k : 4 + k], 0.0)
            held = pltpu.roll(held, 5 + k, 0)
            rim = rim + taps[k : k + 1, c] * held
            parts[k] = parts[k] + jnp.sum(outside * held, axis=0, keepdims=True)
        rim_o[s, :, c] = rim.astype(BF)
        cg[0:5, c] = cg[0:5, c] + jnp.concatenate(parts, axis=0)

    for s in every:
        mt = meta[s]
        turned = lines_of(mt)
        near_of[s] = full(turned[:, 5:6])
        cum, dt = sc[s, 0:HP, :], sc[s, HP:, :]
        b, c = bc[rows[s], :N], bc[rows[s], N:]
        lead = cols_of(jnp.exp(cum) * (mt[0:1, :] == mt[1:2, :]).astype(F4)).astype(BF)
        tail0, lead_last = decays(cum, mt)
        tail = cols_of(tail0 * dt).astype(BF)
        c_t = turn(c)
        scores = mm_nt(c, b)
        inside = inside_of(mt)
        cum_cols = cols_of(cum)
        d_sc = jnp.zeros((QC, QC), F4)
        sums = jnp.zeros((QC, 128), F4)
        tq = jnp.zeros((HP, QC), F4)
        lv = jnp.zeros((HP, QC), F4)
        d_b = jnp.zeros((QC, N), F4)
        d_c = jnp.zeros((QC, N), F4)
        grow = grown(lead_last, e)
        for j, at in enumerate(tiles(XW // WIDE, WIDE)):
            ej = e[:, at]
            xf = x_r[rows[s], at].astype(F4)
            dyf = dy_r[rows[s], at].astype(F4)
            before = ent[s, :, at]
            now = ds[s, :, at]
            after = now.astype(BF)
            tailj = mm(tail, ej)
            u = tailj * mm(b, after)
            led = dyf * mm(lead, ej)
            ledb = led.astype(BF)
            both = jnp.concatenate([xf * u, led * mm(c, before)], axis=0)
            got = gather_heads(both, ej[:HP])
            tq = tq + got[:, :QC]
            lv = lv + got[:, QC:]
            d_b = d_b + mm_nt((xf * tailj).astype(BF), after)
            d_c = d_c + mm_nt(ledb, before)
            colbuf[s, 0:1, at] = jnp.sum(now * before.astype(F4), axis=0, keepdims=True)
            colbuf[s, 1:2, at] = jnp.sum(dyf * xf, axis=0, keepdims=True)
            ds[s, :, at] = now * grow[:, at] + mm(c_t, ledb)
            wide = u + skip[:, at] * dyf
            for k in range(WIDE // 128):
                here = slice(j * WIDE + k * 128, j * WIDE + k * 128 + 128)
                dyp = dy_r[rows[s], here]
                d_ms = mm_nt(dyp, stacked(x_r[rows[s], here], halves))
                ws = []
                for half in range(2):
                    h = (j * WIDE + k * 128) // PS + half
                    gap = jnp.where(inside, cum_cols[:, h : h + 1] - sc[s, h : h + 1, :], NEG)
                    dec = jnp.exp(gap)
                    dtr = sc[s, HP + h : HP + h + 1, :]
                    sl_h = scores * dec
                    d_m = d_ms[:, half * QC : half * QC + QC]
                    g = d_m * sl_h
                    rowbuf[s, h : h + 1, :] = jnp.sum(g, axis=0, keepdims=True)
                    sums = jnp.where(lane == h, jnp.sum(g * dtr, axis=1, keepdims=True), sums)
                    d_sc = d_sc + d_m * (dec * dtr)
                    ws.append((sl_h * dtr).astype(BF))
                dx = wide[:, k * 128 : k * 128 + 128] + mm_tn(
                    jnp.concatenate(ws, axis=0), stacked(dyp, halves)
                )
                conv_back(s, here, xr[rows[s], here].astype(F4), dx.astype(BF).astype(F4), turned)
        d_scb = d_sc.astype(BF)
        d_b = d_b + mm_tn(d_scb, c)
        d_c = d_c + mm(d_scb, b)
        conv_back(s, slice(XW, XW + N), br[rows[s], :N].astype(F4), d_b, turned)
        conv_back(s, slice(XW + N, CW), br[rows[s], N:].astype(F4), d_c, turned)
        ecol = rowbuf[s]
        both = gather_fine(colbuf[s], e[:HP, :])
        at_end = jnp.sum(tq, axis=1, keepdims=True) + lead_last * both[:, 0:1]
        d_cum = jnp.transpose(sums)[:HP] - dt * ecol - tq + lv
        d_la = running(d_cum + jnp.where(place == QC - 1, at_end, 0.0), True)
        v = jnp.transpose(rr[rows[s], :].astype(F4))[:HP] + hp[0]
        d_rate = (ecol + tq / jnp.maximum(dt, 1e-30) + d_la * hp[1]) * sigmoid(v)
        draw_o[rows[s], CW:] = cols_of(d_rate).astype(BF)
        hg[0] = hg[0] + d_rate
        hg[1] = hg[1] + d_la * dt * hp[1]
        hg[2] = hg[2] + jnp.where(place == 0, both[:, 1:2], 0.0)
    cg_o[...] = cg[...]
    hg_o[...] = hg[...]


def scan_back(seqs, x, bc, sl, sc, meta, ent, dy, d_end, raw, halo, taps, hp, skip, e):
    length = x.shape[0]
    span = seqs * QC
    n = length // span
    sd = jax.ShapeDtypeStruct
    return pl.pallas_call(
        back_kernel,
        grid=(n,),
        in_specs=[
            behind(n, span, XW),
            behind(n, span, 2 * N),
            behind(n, span, CW),
            behind3(n, seqs, 2 * HP, 128),
            behind3(n, seqs, 8, 128),
            behind3(n, seqs, N, XW),
            behind(n, span, XW),
            fixed(seqs, N, XW),
            behind(n, span, XW),
            behind(n, span, 2 * N, XW // (2 * N)),
            behind(n, span, 128, CW // 128),
            fixed(seqs, 8, CW),
            fixed(8, CW),
            fixed(2, HP, 128),
            fixed(1, XW),
            fixed(128, XW),
        ],
        out_specs=[behind(n, span, AW), fixed(seqs, 8, CW), fixed(8, CW), fixed(3, HP, 128)],
        out_shape=[
            sd((length, AW), BF),
            sd((seqs, 8, CW), BF),
            sd((8, CW), F4),
            sd((3, HP, 128), F4),
        ],
        scratch_shapes=[
            pltpu.VMEM((seqs, N, XW), F4),
            pltpu.VMEM((seqs, 8, CW), F4),
            pltpu.VMEM((seqs, 8, XW), F4),
            pltpu.VMEM((seqs, HP, 128), F4),
            pltpu.VMEM((8, CW), F4),
            pltpu.VMEM((3, HP, 128), F4),
        ],
        compiler_params=pltpu.CompilerParams(vmem_limit_bytes=LIMIT),
        cost_estimate=work(length, 2),
        name="scan_back",
    )(x, bc, sl, sc, meta, ent, dy, d_end, raw, raw, raw, halo, taps, hp, skip, e)


def last_kernel(x_r, xbc_o, dt_o, taps_o, bias_o, gate_o, norm_o, h0_o, h1_o, h2_o):
    own = xbc_o.shape[0]
    r = lax.broadcasted_iota(jnp.int32, (128, 128), 0)
    c = lax.broadcasted_iota(jnp.int32, (128, 128), 1)
    bc = jnp.zeros((own, 2 * N), F4)
    dt = jnp.zeros((own, 128), F4)
    shared = jnp.zeros((8, AW), F4)
    heads = [jnp.zeros((16, 128), F4) for _ in range(3)]
    for g in range(GROUP):
        at = slice(g * XW, g * XW + XW)
        xbc_o[:, at] = x_r[g, :own, :XW].astype(F4)
        bc = bc + x_r[g, :own, XW:CW].astype(F4)
        move = ((c == r + HG * g) & (r < HG)).astype(BF)
        dt = dt + mm(x_r[g, :own, CW:], move)
        tail = x_r[g, own:, :].astype(F4)
        both = tail[:8] + tail[8:]
        taps_o[:, at] = both[:4, :XW]
        bias_o[:, at] = both[4:5, :XW]
        gate_o[:, at] = both[5:6, :XW]
        shared = shared + both
        for p in range(3):
            move = ((c - HG * g == r - HP * p) & (r >= HP * p) & (r < HP * p + HG)).astype(BF)
            heads[p] = heads[p] + mm(tail[:, XW : XW + 128].astype(BF), move)
    xbc_o[:, DI:] = bc
    dt_o[...] = dt[:, :H]
    taps_o[:, DI:] = shared[:4, XW:CW]
    bias_o[:, DI:] = shared[4:5, XW:CW]
    norm_o[:, :AW] = shared[6:7, :]
    norm_o[:, AW:] = shared[7:8, : norm_o.shape[1] - AW]
    for p, ref in enumerate((h0_o, h1_o, h2_o)):
        ref[...] = heads[p][5:6, :H] + heads[p][13:14, :H]


def last_outputs(x_all, own, width):
    sd = jax.ShapeDtypeStruct
    vm = pl.BlockSpec(memory_space=pltpu.VMEM)
    shapes = [(own, DI + 2 * N), (own, H), (4, DI + 2 * N), (1, DI + 2 * N), (1, DI), (1, width)]
    shapes.extend([(1, H)] * 3)
    return pl.pallas_call(
        last_kernel,
        out_shape=[sd(shape, F4) for shape in shapes],
        in_specs=[vm],
        out_specs=[vm] * len(shapes),
        compiler_params=pltpu.CompilerParams(vmem_limit_bytes=LIMIT),
        name="last_outputs",
    )(x_all)


def pad_lanes(v, width):
    return jnp.pad(v, [(0, 0)] * (v.ndim - 1) + [(0, width - v.shape[-1])])


def carried(state, decay, hops, by):
    total = shift(state, CHAIN, by)
    if hops == 1:
        return total
    total, product = total.astype(F4), 1.0
    for j in range(2, hops + 1):
        product = product * shift(decay, CHAIN, by * (j - 1))
        total = total + product * shift(state, CHAIN, by * j).astype(F4)
    return total.astype(BF)


def shards(
    tokens_in, seg_ids, in_norm, z_proj, xbc_proj, dt_proj, conv_taps, conv_bias,
    dt_bias, a_log, d_skip, gate_norm, out_proj, out_cotangent,
):
    seqs, rows, width = tokens_in.shape
    length = seg_ids.shape[1]
    block = rows * GROUP
    n_blocks = length // block
    hops = min(-(-(length // 4 - 1) // block), n_blocks - 1)
    n_sums = lax.axis_size("dp") * n_blocks
    hl = lax.axis_index("hl")
    own_rows = z_proj.shape[0]

    def collected(part):
        return lax.all_gather(part, "hl", axis=0).reshape(GROUP * seqs * rows, width)

    def quarters(w):
        return w.reshape(w.shape[0], GROUP, -1).transpose(1, 0, 2)

    bc_cols = jnp.broadcast_to(xbc_proj[None, :, DI:], (GROUP, own_rows, 2 * N))
    parts = [quarters(xbc_proj[:, :DI]), bc_cols, pad_lanes(quarters(dt_proj), 128), quarters(z_proj)]
    in_mine = lax.all_to_all(jnp.concatenate(parts, axis=-1), "hl", 0, 0, tiled=True)
    in_mine = in_mine.reshape(GROUP * own_rows, AW + XW)
    pairs = [(f, (f % n_sums) * GROUP + f // n_sums) for f in range(GROUP * n_sums)]
    wo_mine = lax.ppermute(out_proj, EVERY, pairs)
    in_mine, wo_mine, tokens_now = lax.optimization_barrier((in_mine, wo_mine, tokens_in))
    tokens = collected(tokens_now)
    cot = collected(out_cotangent)
    wx, wz = all_rows(near_rows(in_mine), [(0, AW), (AW, AW + XW)])
    wx, wz, wo_mine = lax.optimization_barrier((wx, wz, wo_mine))
    wo_near = near_rows(wo_mine)

    def mine(v, size):
        return lax.dynamic_slice_in_dim(v, hl * size, size, axis=-1)

    taps = jnp.concatenate([conv_taps, conv_bias[None]], axis=0)
    taps = jnp.concatenate([mine(taps[:, :DI], XW), taps[:, DI:]], axis=1)
    taps = jnp.pad(taps, ((0, 3), (0, 0)))
    hp = jnp.stack([mine(dt_bias, HG), -jnp.exp(mine(a_log, HG))])
    hp = jnp.broadcast_to(jnp.pad(hp, ((0, 0), (0, HP - HG)))[:, :, None], (2, HP, 128))
    skip = jnp.repeat(mine(d_skip, HG), PS)[None]
    gain = mine(gate_norm, XW)[None]
    e = (jnp.arange(128)[:, None] == jnp.arange(XW)[None, :] // PS).astype(BF)

    start = lax.axis_index(CHAIN) * block
    seg_pad = jnp.concatenate([jnp.full((seqs, 8), -1, jnp.int32), seg_ids], axis=1)
    near = lax.dynamic_slice_in_dim(seg_pad, start, block + 8, axis=1)
    seg = near[:, 8:].reshape(seqs, GROUP, QC)
    lines = [seg, jnp.broadcast_to(near[:, 7 : 7 + block : QC][:, :, None], seg.shape)]
    lines.append(jnp.broadcast_to(seg[:, :, QC - 1 :], seg.shape))
    for k in range(KW - 1):
        lines.append((near[:, 5 + k : 5 + k + block].reshape(seg.shape) == seg).astype(jnp.int32))
    lines.extend([jnp.zeros_like(seg)] * 2)
    meta = jnp.stack(lines, axis=2).astype(F4)
    meta = meta.transpose(1, 0, 2, 3).reshape(GROUP * seqs, 8, QC)

    tokens, wx, wz, meta, taps, hp, skip, gain, e = lax.optimization_barrier(
        (tokens, wx, wz, meta, taps, hp, skip, gain, e)
    )
    normed = norm_rows(tokens.astype(F4), in_norm).astype(BF)
    raw = mm(normed, wx).astype(BF)
    raw, *wo_near = lax.optimization_barrier((raw, *wo_near))
    [wo] = all_rows(wo_near, [(0, width)])
    last = raw.reshape(GROUP, seqs, rows, AW)[GROUP - 1, :, rows - 8 :, :CW]
    halo = shift(last, CHAIN, 1)
    x, bc, sl, sc, state, decay = front(seqs, raw, halo, meta, taps, hp, e)
    decay_row = jnp.repeat(decay[:, :HG, 0], PS, axis=-1)[:, None]
    state, z_normed = lax.optimization_barrier((state, normed))
    s_in = carried(state, decay_row, hops, 1)
    gates = mm(z_normed, wz)
    s_in, wo = lax.optimization_barrier((s_in, wo))
    y, sg, ent, squares = scan(seqs, x, bc, sc, meta, s_in, gates, skip, gain, e)

    def team_sum(part):
        total = part
        for k in range(1, GROUP):
            total = total + swap(part, "hl", k)
        return total

    def spread_sum(part):
        total = lax.psum_scatter(part, "hl", scatter_dimension=0, tiled=True)
        return total.reshape(seqs, rows, width)

    out_rows = mm(sg, wo).astype(BF)
    squares = team_sum(squares)
    cot, out_rows, squares = lax.optimization_barrier((cot, out_rows, squares))
    d_gated = mm_nt(cot, wo)
    row_scale = lax.rsqrt(squares * (1.0 / DI) + EPS)
    gated = (sg.astype(F4) * row_scale.reshape(-1, 1)).astype(BF)
    along = team_sum(jnp.sum(d_gated * sg.astype(F4), axis=1).reshape(squares.shape))
    out_sum = spread_sum(out_rows)
    dp = lax.axis_index("dp")
    if plain():
        o_give, o_keep = (mm_tn(half_of(gated, at), cot).astype(BF) for at in (1 - dp, dp))
    dy, dz, gg, d_state = gate(seqs, y, gates, d_gated, squares, along, bc, sc, meta, gain, e)
    d_end = carried(d_state, decay_row, hops, -1)
    if plain():
        n_give, n_keep = (half_of(normed, at) for at in (1 - dp, dp))
        z_give, z_keep = (mm_tn(v, dz).astype(BF) for v in (n_give, n_keep))
        dy, z_give, z_keep = lax.optimization_barrier((dy, z_give, z_keep))
        z_got, o_got = swap(z_give, "dp", 1), swap(o_give, "dp", 1)
        early = []
        for z_part, o_part in zip(chain_pieces(z_keep, z_got), chain_pieces(o_keep, o_got)):
            early.append(jnp.concatenate([z_part, o_part[:, : width // 2], o_part[:, width // 2 :]]))
        dy, *early = lax.optimization_barrier((dy, *early))
        early = chain_sum(early)
    draw, rim, conv_total, head_total = scan_back(
        seqs, x, bc, sl, sc, meta, ent, dy, d_end, raw, halo, taps, hp, skip, e
    )
    rim = shift(rim, CHAIN, -1)
    from_z = mm_nt(dz, wz).astype(BF)
    if plain():
        rim, from_z, out_sum, early = lax.optimization_barrier((rim, from_z, out_sum, early))
    draw = draw.reshape(GROUP, seqs, rows, AW)
    edge = draw[GROUP - 1 :, :, rows - 8 :, :CW].astype(F4) + rim.astype(F4)
    draw = lax.dynamic_update_slice(draw, edge.astype(BF), (GROUP - 1, 0, rows - 8, 0))
    draw = draw.reshape(GROUP * seqs * rows, AW)

    def row_dots(grad, w):
        return jnp.sum(grad.astype(F4) * w.astype(F4), axis=1)

    if plain():
        z_rows = GROUP * own_rows
        o_rows = (early.shape[0] - z_rows) // 2
        z_own = early[:z_rows].reshape(GROUP, own_rows, XW)
        z_all = lax.all_to_all(z_own, "hl", 0, 0, tiled=True)
        o_own = jnp.concatenate([early[z_rows : z_rows + o_rows], early[z_rows + o_rows :]], axis=1)
        d_low = (from_z.astype(F4) + mm_nt(draw, wx)).astype(BF)
        d_low, draw, z_all = lax.optimization_barrier((d_low, draw, z_all))
        x_give = mm_tn(n_give, draw).astype(BF)
        x_give, draw = lax.optimization_barrier((x_give, draw))
        x_got = swap(x_give, "dp", 1)
        x_keep = mm_tn(n_keep, draw).astype(BF)
        x_pieces = chain_pieces(x_keep, x_got)
        x_give, x_keep, *x_pieces = lax.optimization_barrier((x_give, x_keep, *x_pieces))
        x_own = chain_sum(x_pieces)
        norm_parts = []
        for at, xg, zg in ((1 - dp, x_give, z_give), (dp, x_keep, z_keep)):
            half = [lax.dynamic_slice_in_dim(w, at * (width // 2), width // 2) for w in (wx, wz)]
            norm_parts.append(row_dots(xg, half[0]) + row_dots(zg, half[1]))
        norm_total = joined(norm_parts[1], norm_parts[0], dp)
    else:
        grads = [mm_tn(normed, dz), mm_tn(gated, cot), mm_tn(normed, draw)]
        grads = [g.astype(BF) for g in grads]
        d_low = (from_z.astype(F4) + mm_nt(draw, wx)).astype(BF)
        norm_total = row_dots(grads[0], wz) + row_dots(grads[2], wx)
        z_own, o_own, x_own = (
            lax.psum_scatter(g, SUMS, scatter_dimension=0, tiled=True) for g in grads
        )
    d_sum = spread_sum(d_low)
    out_proj_grad = lax.ppermute(o_own, EVERY, [(b, a) for a, b in pairs]).astype(F4)

    heads = jnp.sum(head_total, axis=2).reshape(1, -1)
    norm_rows_2 = jnp.pad(norm_total / in_norm, (0, 2 * AW - width)).reshape(2, AW)
    pack = jnp.concatenate(
        [
            pad_lanes(conv_total[:5], AW),
            pad_lanes(jnp.concatenate([gg[:1], heads], axis=1), AW),
            norm_rows_2,
        ],
        axis=0,
    )
    for axis in SUMS:
        pack = pack + sum(swap(pack, axis, k) for k in range(1, lax.axis_size(axis)))
    high = pack.astype(BF)
    small = jnp.concatenate([high, (pack - high.astype(F4)).astype(BF)], axis=0)
    small = jnp.broadcast_to(small[None], (GROUP, 16, AW))
    x_own = jnp.concatenate([x_own.reshape(GROUP, own_rows, AW), small], axis=1)
    if not plain():
        z_all = lax.all_to_all(z_own.reshape(GROUP, own_rows, XW), "hl", 0, 0, tiled=True)
    x_all = lax.all_to_all(x_own, "hl", 0, 0, tiled=True)

    u = tokens_in.astype(F4)
    scale = lax.rsqrt(jnp.mean(u * u, axis=-1, keepdims=True) + EPS)
    hat = u * scale
    dh = d_sum.astype(F4) * in_norm
    along = jnp.mean(dh * hat, axis=-1, keepdims=True)
    x_all, along = lax.optimization_barrier((x_all, along))
    d_u = scale * (dh - hat * along)
    tokens_grad = d_u + out_cotangent.astype(F4)
    own_scale = lax.dynamic_index_in_dim(row_scale.reshape(GROUP, seqs, rows, 1), hl, 0, keepdims=False)
    layer_out = (tokens_in.astype(F4) + own_scale * out_sum.astype(F4)).astype(BF)
    z_proj_grad = z_all.transpose(1, 0, 2).reshape(own_rows, DI).astype(F4)
    if plain():
        outs = last_outputs(x_all, own_rows, width)
        xbc_proj_grad, dt_proj_grad, taps_grad = outs[:3]
        bias_grad, gate_grad, in_norm_grad = (v.reshape(-1) for v in outs[3:6])
        per_head = [v.reshape(-1) for v in outs[6:]]
    else:
        x_parts = x_all[:, :own_rows]
        xs = x_parts[:, :, :XW].transpose(1, 0, 2).reshape(own_rows, DI).astype(F4)
        bc_grad = jnp.sum(x_parts[:, :, XW:CW].astype(F4), axis=0)
        xbc_proj_grad = jnp.concatenate([xs, bc_grad], axis=1)
        dt_parts = x_parts[:, :, CW : CW + HG].transpose(1, 0, 2)
        dt_proj_grad = dt_parts.reshape(own_rows, H).astype(F4)
        got = x_all[:, own_rows:, :AW].astype(F4)
        got = got[:, :8] + got[:, 8:]
        conv_x = got[:, :5, :XW].transpose(1, 0, 2).reshape(5, DI)
        conv_all = jnp.concatenate([conv_x, jnp.sum(got[:, :5, XW:CW], axis=0)], axis=1)
        per_head = got[:, 5, XW : XW + 3 * HP].reshape(GROUP, 3, HP)[:, :, :HG]
        per_head = per_head.transpose(1, 0, 2).reshape(3, H)
        in_norm_grad = jnp.sum(got[:, 6:8], axis=0).reshape(-1)[:width]
        taps_grad, bias_grad, gate_grad = conv_all[:4], conv_all[4], got[:, 5, :XW].reshape(DI)
    return (
        layer_out,
        tokens_grad,
        in_norm_grad,
        z_proj_grad,
        xbc_proj_grad,
        dt_proj_grad,
        taps_grad,
        bias_grad,
        per_head[0],
        per_head[1],
        per_head[2],
        gate_grad,
        out_proj_grad,
    )


def solution(mesh):
    sizes = dict(mesh.shape)
    grid = mesh.devices.reshape(sizes["dp"], sizes["ctx"], sizes["hd"] // GROUP, GROUP)
    fine = Mesh(grid, ("dp", "ctx", "hh", "hl"))
    tok = P("dp", ("ctx", "hh", "hl"), None)
    wgt = P(("dp", "ctx", "hh", "hl"), None)
    in_specs = (tok, P("dp", None), P(), wgt, wgt, wgt, P(), P(), P(), P(), P(), P(), wgt, tok)
    out_specs = (tok, tok, P(), wgt, wgt, wgt, P(), P(), P(), P(), P(), P(), wgt)
    return jax.shard_map(shards, mesh=fine, in_specs=in_specs, out_specs=out_specs, check_vma=False)
```

```python
import jax
import jax.numpy as jnp
from jax import lax
from jax.experimental import pallas as pl
from jax.experimental.pallas import tpu as pltpu
from jax.sharding import Mesh, PartitionSpec as P

H = 48
PS = 64
N = 128
KW = 4
DI = 3072
GROUP = 4
HG = H // GROUP
HP = 16
XW = HG * PS
CW = XW + 2 * N
AW = CW + 128
QC = 128
EPS = 1e-05
NEG = -1e30
BF = jnp.bfloat16
F4 = jnp.float32
LIMIT = 48 * 1024 * 1024
SUMS = ("dp", "ctx", "hh")
CHAIN = ("ctx", "hh")
EVERY = ("dp", "ctx", "hh", "hl")


def swap(part, axis, k):
    count = lax.axis_size(axis)
    return lax.ppermute(part, axis, [(i, i ^ k) for i in range(count)])


def shift(part, axes, by):
    count = 1
    for axis in axes:
        count = count * lax.axis_size(axis)
    pairs = [(i, i + by) for i in range(count) if 0 <= i + by < count]
    return lax.ppermute(part, axes, pairs)


def mm(a, b):
    return jnp.dot(a, b, preferred_element_type=F4)


def mm_nt(a, b):
    return lax.dot_general(a, b, (((1,), (1,)), ((), ())), preferred_element_type=F4)


def mm_tn(a, b):
    return lax.dot_general(a, b, (((0,), (0,)), ((), ())), preferred_element_type=F4)


def grown(lead_last, e):
    v = lead_last[:, :8]
    hi = v.astype(BF)
    lo = (v - hi.astype(F4)).astype(BF)
    return (mm_tn(hi, e[:HP, :]) + mm_tn(lo, e[:HP, :]))[0:1, :]


def gather_heads(w, e):
    return mm_nt(e, w.astype(BF))


def gather_fine(w, e):
    hi = w.astype(BF)
    lo = (w - hi.astype(F4)).astype(BF)
    return mm_nt(e, hi) + mm_nt(e, lo)


def turn(v):
    return jnp.transpose(v.astype(F4)).astype(BF)


def sigmoid(v):
    return 0.5 * jnp.tanh(0.5 * v) + 0.5


def norm_rows(values, gain):
    return values * lax.rsqrt(jnp.mean(values * values, axis=-1, keepdims=True) + EPS) * gain


def running(v, back):
    r = lax.broadcasted_iota(jnp.int32, (QC, QC), 0)
    q = lax.broadcasted_iota(jnp.int32, (QC, QC), 1)
    ones = ((r >= q) if back else (r <= q)).astype(BF)
    hi = v.astype(BF)
    rest = v - hi.astype(F4)
    mid = rest.astype(BF)
    lo = (rest - mid.astype(F4)).astype(BF)
    got = mm(jnp.concatenate([hi, mid, lo], axis=0), ones)
    n = v.shape[0]
    return got[:n] + got[n : 2 * n] + got[2 * n :]


def lines_of(mt):
    return jnp.transpose(jnp.concatenate([mt, jnp.zeros((QC - 8, QC), F4)], axis=0))


def full(col):
    return jnp.broadcast_to(col, (QC, 128))


def tiles(count, width=128):
    return [slice(j * width, j * width + width) for j in range(count)]


WIDE = 256


def stacked(v, halves):
    return jnp.concatenate([v * halves[0], v * halves[1]], axis=0)


def col_of(row):
    return jnp.transpose(jnp.broadcast_to(row, (QC, QC)))


def cols_of(v):
    return jnp.transpose(jnp.concatenate([v, jnp.zeros((QC - HP, QC), F4)], axis=0))


def place_kernel(place, *refs):
    out = refs[-1]
    rows = refs[0].shape[0]
    for k, ref in enumerate(refs[:-1]):
        slot = jnp.bitwise_xor(place[0], k)
        out[pl.ds(pl.multiple_of(slot * rows, rows), rows), :] = ref[...]


def placed(place, pieces):
    rows, width = pieces[0].shape
    vm = pl.BlockSpec(memory_space=pltpu.VMEM)
    return pl.pallas_call(
        place_kernel,
        out_shape=jax.ShapeDtypeStruct((len(pieces) * rows, width), BF),
        in_specs=[pl.BlockSpec(memory_space=pltpu.SMEM)] + [vm] * len(pieces),
        out_specs=vm,
        compiler_params=pltpu.CompilerParams(vmem_limit_bytes=LIMIT),
        name="place_rows",
    )(place, *pieces)


def joined(cur, got, side):
    low = jnp.where(side == 0, cur, got)
    high = jnp.where(side == 0, got, cur)
    return jnp.concatenate([low, high], axis=0)


def plain():
    return lax.axis_size("hh") == 1


def near_rows(mine):
    if not plain() or mine.shape[0] % 16:
        return [mine]
    return [mine] + [swap(mine, "ctx", k) for k in range(1, lax.axis_size("ctx"))]


def all_rows(pieces, cuts):
    if len(pieces) == 1:
        whole = lax.all_gather(pieces[0], SUMS, axis=0, tiled=True)
        return [whole[:, a:b] for a, b in cuts]
    stack = placed(lax.axis_index("ctx").astype(jnp.int32).reshape(1), pieces)
    got = swap(stack, "dp", 1)
    side = lax.axis_index("dp")
    return [joined(stack[:, a:b], got[:, a:b], side) for a, b in cuts]


def half_of(v, side):
    return lax.dynamic_slice_in_dim(v, side * (v.shape[1] // 2), v.shape[1] // 2, axis=1)


def chain_pieces(keep, got):
    count = lax.axis_size("ctx")
    ctx = lax.axis_index("ctx")
    keep = keep.reshape(count, -1, keep.shape[-1])
    got = got.reshape(keep.shape)
    pieces = []
    for k in range(count):
        at = jnp.bitwise_xor(ctx, k)
        parts = [lax.dynamic_index_in_dim(v, at, 0, keepdims=False) for v in (keep, got)]
        pieces.append((parts[0].astype(F4) + parts[1].astype(F4)).astype(BF))
    return pieces


def chain_sum(pieces):
    out = pieces[0].astype(F4)
    for k in range(1, len(pieces)):
        out = out + swap(pieces[k], "ctx", k).astype(F4)
    return out.astype(BF)


def work(length, us):
    flops = int(us * 1e9) * length // 1024
    return pl.CostEstimate(flops=flops, transcendentals=0, bytes_accessed=length * 8192)


def fixed(*shape):
    return pl.BlockSpec(shape, lambda i: (0,) * len(shape))


def ahead(rows, width, at=0):
    return pl.BlockSpec((rows, width), lambda i: (i, at))


def ahead3(seqs, *shape):
    return pl.BlockSpec((seqs, *shape), lambda i: (i, 0, 0))


def behind(n, rows, width, at=0):
    return pl.BlockSpec((rows, width), lambda i: (n - 1 - i, at))


def behind3(n, seqs, *shape):
    return pl.BlockSpec((seqs, *shape), lambda i: (n - 1 - i, 0, 0))


def decays(cum, mt):
    last = cum[:, QC - 1 : QC]
    same_last = (mt[0:1, :] == mt[2:3, :]).astype(F4)
    follows = (mt[1:2, :] == mt[2:3, :]).astype(F4)
    tail0 = jnp.exp(last - cum) * same_last
    lead_last = jnp.exp(last) * follows
    return tail0, lead_last


def front_kernel(
    xr, br, rr, halo, meta, taps, hp, e, x_o, bc_o, sl_o, sc_o, st_o, dec_o, buf, st, dec
):
    i = pl.program_id(0)
    seqs = halo.shape[0]

    @pl.when(i == 0)
    def _():
        buf[:, 0:8, :] = halo[...].astype(F4)
        st[...] = jnp.zeros_like(st)
        dec[...] = jnp.ones_like(dec)

    @pl.when(i > 0)
    def _():
        buf[:, 0:8, :] = buf[:, QC : QC + 8, :]

    every = range(seqs)
    rows = [slice(s * QC, s * QC + QC) for s in every]
    tails, lasts = [], []
    for s in every:
        v = jnp.transpose(rr[rows[s], :].astype(F4))[:HP] + hp[0]
        dt = jnp.maximum(v, 0.0) + jnp.log1p(jnp.exp(-jnp.abs(v)))
        cum = running(dt * hp[1], False)
        sc_o[s, 0:HP, :] = cum
        sc_o[s, HP:, :] = dt
        tail0, lead_last = decays(cum, meta[s])
        dec[s] = dec[s] * lead_last
        tails.append(cols_of(tail0 * dt).astype(BF))
        lasts.append(grown(lead_last, e))
    order = tiles(CW // 128)
    n_x = XW // 128
    for s in every:
        turned = lines_of(meta[s])
        masks = [full(turned[:, 3 + k : 4 + k]) for k in range(3)]
        for j in [*range(n_x, len(order)), *range(n_x)]:
            c = order[j]
            if j < n_x:
                own = xr[rows[s], c].astype(F4)
            else:
                own = br[rows[s], j * 128 - XW : j * 128 - XW + 128].astype(F4)
            buf[s, 8 : QC + 8, c] = own
            mixed = taps[4:5, c] + taps[3:4, c] * own
            for k in range(3):
                mixed = mixed + taps[k : k + 1, c] * (
                    buf[s, 5 + k : 5 + k + QC, c] * masks[k]
                )
            sig = sigmoid(mixed)
            act = (mixed * sig).astype(BF)
            sl_o[rows[s], c] = (sig + mixed * sig * (1.0 - sig)).astype(BF)
            if j < n_x:
                x_o[rows[s], c] = act
                if j % 2:
                    c2 = slice(j * 128 - 128, j * 128 + 128)
                    pair = jnp.concatenate([held, act], axis=1).astype(F4)
                    xw = (pair * mm(tails[s], e[:, c2])).astype(BF)
                    st[s, :, c2] = st[s, :, c2] * lasts[s][:, c2] + mm(b_t, xw)
                held = act
            else:
                bc_o[rows[s], j * 128 - XW : j * 128 - XW + 128] = act
                if j == n_x:
                    b_t = turn(act)
    st_o[...] = st[...].astype(BF)
    dec_o[...] = dec[...]


def front(seqs, raw, halo, meta, taps, hp, e):
    length = raw.shape[0]
    span = seqs * QC
    sd = jax.ShapeDtypeStruct
    return pl.pallas_call(
        front_kernel,
        grid=(length // span,),
        in_specs=[
            ahead(span, XW),
            ahead(span, 2 * N, XW // (2 * N)),
            ahead(span, 128, CW // 128),
            fixed(seqs, 8, CW),
            ahead3(seqs, 8, 128),
            fixed(8, CW),
            fixed(2, HP, 128),
            fixed(128, XW),
        ],
        out_specs=[
            ahead(span, XW),
            ahead(span, 2 * N),
            ahead(span, CW),
            ahead3(seqs, 2 * HP, 128),
            fixed(seqs, N, XW),
            fixed(seqs, HP, 128),
        ],
        out_shape=[
            sd((length, XW), BF),
            sd((length, 2 * N), BF),
            sd((length, CW), BF),
            sd((length // QC, 2 * HP, 128), F4),
            sd((seqs, N, XW), BF),
            sd((seqs, HP, 128), F4),
        ],
        scratch_shapes=[
            pltpu.VMEM((seqs, QC + 8, CW), F4),
            pltpu.VMEM((seqs, N, XW), F4),
            pltpu.VMEM((seqs, HP, 128), F4),
        ],
        compiler_params=pltpu.CompilerParams(vmem_limit_bytes=LIMIT),
        cost_estimate=work(length, 1),
        name="conv_state",
    )(raw, raw, raw, halo, meta, taps, hp, e)


def lane_halves():
    lane = lax.broadcasted_iota(jnp.int32, (1, 128), 1)
    return [(lane < PS).astype(BF), (lane >= PS).astype(BF)]


def inside_of(mt):
    r = lax.broadcasted_iota(jnp.int32, (QC, QC), 0)
    q = lax.broadcasted_iota(jnp.int32, (QC, QC), 1)
    return (col_of(mt[0:1, :]) == mt[0:1, :]) & (r >= q)


def scan_kernel(x_r, bc, sc, meta, s_in, z_r, skip, gain, e, y_o, sg_o, ent_o, sum_o, st):
    i = pl.program_id(0)
    seqs = s_in.shape[0]
    every = range(seqs)
    rows = [slice(s * QC, s * QC + QC) for s in every]

    @pl.when(i == 0)
    def _():
        st[...] = s_in[...].astype(F4)

    halves = lane_halves()
    for s in every:
        mt = meta[s]
        cum, dt = sc[s, 0:HP, :], sc[s, HP:, :]
        b, c = bc[rows[s], :N], bc[rows[s], N:]
        lead = cols_of(jnp.exp(cum) * (mt[0:1, :] == mt[1:2, :]).astype(F4)).astype(BF)
        tail0, lead_last = decays(cum, mt)
        tail = cols_of(tail0 * dt).astype(BF)
        b_t = turn(b)
        scores = mm_nt(c, b)
        inside = inside_of(mt)
        cum_cols = cols_of(cum)
        squares = jnp.zeros((QC, 128), F4)
        grow = grown(lead_last, e)
        for j, at in enumerate(tiles(XW // WIDE, WIDE)):
            ej = e[:, at]
            xf = x_r[rows[s], at].astype(F4)
            now = st[s, :, at]
            before = now.astype(BF)
            ent_o[s, :, at] = before
            wide = mm(lead, ej) * mm(c, before) + skip[:, at] * xf
            xw = (xf * mm(tail, ej)).astype(BF)
            st[s, :, at] = now * grow[:, at] + mm(b_t, xw)
            for k in range(WIDE // 128):
                here = slice(j * WIDE + k * 128, j * WIDE + k * 128 + 128)
                xp = x_r[rows[s], here]
                ws = []
                for half in range(2):
                    h = (j * WIDE + k * 128) // PS + half
                    gap = jnp.where(inside, cum_cols[:, h : h + 1] - sc[s, h : h + 1, :], NEG)
                    ws.append((scores * jnp.exp(gap) * sc[s, HP + h : HP + h + 1, :]).astype(BF))
                y = wide[:, k * 128 : k * 128 + 128] + mm(jnp.concatenate(ws, axis=1), stacked(xp, halves))
                low = y.astype(BF)
                y_o[rows[s], here] = low
                z = z_r[rows[s], here]
                v = low.astype(F4) * z * sigmoid(z)
                squares = squares + v * v
                sg_o[rows[s], here] = (v * gain[:, here]).astype(BF)
        sum_o[s] = jnp.sum(jnp.transpose(squares), axis=0, keepdims=True)


def scan(seqs, x, bc, sc, meta, s_in, z, skip, gain, e):
    length = x.shape[0]
    span = seqs * QC
    chunks = length // QC
    sd = jax.ShapeDtypeStruct
    return pl.pallas_call(
        scan_kernel,
        grid=(length // span,),
        in_specs=[
            ahead(span, XW),
            ahead(span, 2 * N),
            ahead3(seqs, 2 * HP, 128),
            ahead3(seqs, 8, 128),
            fixed(seqs, N, XW),
            ahead(span, XW),
            fixed(1, XW),
            fixed(1, XW),
            fixed(128, XW),
        ],
        out_specs=[ahead(span, XW), ahead(span, XW), ahead3(seqs, N, XW), ahead3(seqs, 1, QC)],
        out_shape=[
            sd((length, XW), BF),
            sd((length, XW), BF),
            sd((chunks, N, XW), BF),
            sd((chunks, 1, QC), F4),
        ],
        scratch_shapes=[pltpu.VMEM((seqs, N, XW), F4)],
        compiler_params=pltpu.CompilerParams(vmem_limit_bytes=LIMIT),
        cost_estimate=work(length, 1),
        name="scan_gate",
    )(x, bc, sc, meta, s_in, z, skip, gain, e)


def gate_kernel(y_r, z_r, dg_r, sq, al, bc, sc, meta, gain, e, dy_o, dz_o, gg_o, ds_o, ds, gg):
    i = pl.program_id(0)
    seqs = ds.shape[0]
    every = range(seqs)
    rows = [slice(s * QC, s * QC + QC) for s in every]

    @pl.when(i == 0)
    def _():
        gg[...] = jnp.zeros_like(gg)
        ds[...] = jnp.zeros_like(ds)

    for s in every:
        mt = meta[s]
        cum = sc[s, 0:HP, :]
        c = bc[rows[s], N:]
        scale = lax.rsqrt(sq[s] * (1.0 / DI) + EPS)
        rstd = jnp.concatenate([col_of(scale)] * (WIDE // 128), axis=1)
        pull = col_of(al[s] * (scale * scale * scale) * (1.0 / DI))
        pull = jnp.concatenate([pull] * (WIDE // 128), axis=1)
        lead = cols_of(jnp.exp(cum) * (mt[0:1, :] == mt[1:2, :]).astype(F4)).astype(BF)
        _, lead_last = decays(cum, mt)
        c_t = turn(c)
        grow = grown(lead_last, e)
        for at in tiles(XW // WIDE, WIDE):
            ej = e[:, at]
            y = y_r[rows[s], at].astype(F4)
            z = z_r[rows[s], at]
            sig = sigmoid(z)
            act = z * sig
            v = y * act
            dg = dg_r[rows[s], at] * rstd
            gg[0:1, at] = gg[0:1, at] + jnp.sum(dg * v, axis=0, keepdims=True)
            d_v = dg * gain[:, at] - v * pull
            dy = (d_v * act).astype(BF)
            dy_o[rows[s], at] = dy
            dz_o[rows[s], at] = (d_v * y * (sig + act * (1.0 - sig))).astype(BF)
            led = (dy.astype(F4) * mm(lead, ej)).astype(BF)
            ds[s, :, at] = ds[s, :, at] * grow[:, at] + mm(c_t, led)
    ds_o[...] = ds[...].astype(BF)
    gg_o[...] = gg[...]


def gate(seqs, y, z, dg, sq, al, bc, sc, meta, gain, e):
    length = y.shape[0]
    span = seqs * QC
    n = length // span
    sd = jax.ShapeDtypeStruct
    wide = behind(n, span, XW)
    line = behind3(n, seqs, 1, QC)
    return pl.pallas_call(
        gate_kernel,
        grid=(n,),
        in_specs=[
            wide,
            wide,
            wide,
            line,
            line,
            behind(n, span, 2 * N),
            behind3(n, seqs, 2 * HP, 128),
            behind3(n, seqs, 8, 128),
            fixed(1, XW),
            fixed(128, XW),
        ],
        out_specs=[wide, wide, fixed(8, XW), fixed(seqs, N, XW)],
        out_shape=[
            sd((length, XW), BF),
            sd((length, XW), BF),
            sd((8, XW), F4),
            sd((seqs, N, XW), BF),
        ],
        scratch_shapes=[pltpu.VMEM((seqs, N, XW), F4), pltpu.VMEM((8, XW), F4)],
        compiler_params=pltpu.CompilerParams(vmem_limit_bytes=LIMIT),
        cost_estimate=work(length, 1),
        name="gate_back",
    )(y, z, dg, sq, al, bc, sc, meta, gain, e)


def back_kernel(
    x_r, bc, sl, sc, meta, ent, dy_r, d_end, xr, br, rr, halo, taps, hp, skip, e,
    draw_o, rim_o, cg_o, hg_o,
    ds, carry, colbuf, rowbuf, cg, hg,
):
    i = pl.program_id(0)
    seqs = ds.shape[0]
    every = range(seqs)
    rows = [slice(s * QC, s * QC + QC) for s in every]
    first = (i == pl.num_programs(0) - 1).astype(F4)

    @pl.when(i == 0)
    def _():
        ds[...] = d_end[...].astype(F4)
        carry[...] = jnp.zeros_like(carry)
        cg[...] = jnp.zeros_like(cg)
        hg[...] = jnp.zeros_like(hg)
        colbuf[...] = jnp.zeros_like(colbuf)
        rowbuf[...] = jnp.zeros_like(rowbuf)

    halves = lane_halves()
    lane = lax.broadcasted_iota(jnp.int32, (1, 128), 1)
    token = lax.broadcasted_iota(jnp.int32, (QC, 128), 0)
    edge = lax.broadcasted_iota(jnp.int32, (8, 128), 0)
    place = lax.broadcasted_iota(jnp.int32, (HP, QC), 1)

    near_of = {}

    def conv_back(s, c, own, d_act, turned):
        dm = d_act * sl[rows[s], c].astype(F4)
        near = near_of[s]
        shifted = [dm]
        for k in range(3):
            ready = shifted[-1] * near
            moved = pltpu.roll(ready, QC - 1, 0)
            shifted.append(jnp.where(token == QC - 1, carry[s, k : k + 1, c], moved))
            carry[s, k : k + 1, c] = ready[0:1, :]
        d_raw = taps[3:4, c] * shifted[0]
        for k in range(3):
            d_raw = d_raw + taps[2 - k : 3 - k, c] * shifted[k + 1]
        draw_o[rows[s], c] = d_raw.astype(BF)
        parts = [jnp.sum(own * v, axis=0, keepdims=True) for v in shifted[::-1]]
        parts.append(jnp.sum(dm, axis=0, keepdims=True))
        head = dm[0:8, :]
        outside = halo[s, :, c].astype(F4) * first
        rim = jnp.zeros((8, 128), F4)
        for k in range(3):
            held = jnp.where(edge < 3 - k, head * turned[0:8, 3 + k : 4 + k], 0.0)
            held = pltpu.roll(held, 5 + k, 0)
            rim = rim + taps[k : k + 1, c] * held
            parts[k] = parts[k] + jnp.sum(outside * held, axis=0, keepdims=True)
        rim_o[s, :, c] = rim.astype(BF)
        cg[0:5, c] = cg[0:5, c] + jnp.concatenate(parts, axis=0)

    for s in every:
        mt = meta[s]
        turned = lines_of(mt)
        near_of[s] = full(turned[:, 5:6])
        cum, dt = sc[s, 0:HP, :], sc[s, HP:, :]
        b, c = bc[rows[s], :N], bc[rows[s], N:]
        lead = cols_of(jnp.exp(cum) * (mt[0:1, :] == mt[1:2, :]).astype(F4)).astype(BF)
        tail0, lead_last = decays(cum, mt)
        tail = cols_of(tail0 * dt).astype(BF)
        c_t = turn(c)
        scores = mm_nt(c, b)
        inside = inside_of(mt)
        cum_cols = cols_of(cum)
        d_sc = jnp.zeros((QC, QC), F4)
        sums = jnp.zeros((QC, 128), F4)
        tq = jnp.zeros((HP, QC), F4)
        lv = jnp.zeros((HP, QC), F4)
        d_b = jnp.zeros((QC, N), F4)
        d_c = jnp.zeros((QC, N), F4)
        grow = grown(lead_last, e)
        for j, at in enumerate(tiles(XW // WIDE, WIDE)):
            ej = e[:, at]
            xf = x_r[rows[s], at].astype(F4)
            dyf = dy_r[rows[s], at].astype(F4)
            before = ent[s, :, at]
            now = ds[s, :, at]
            after = now.astype(BF)
            tailj = mm(tail, ej)
            u = tailj * mm(b, after)
            led = dyf * mm(lead, ej)
            ledb = led.astype(BF)
            both = jnp.concatenate([xf * u, led * mm(c, before)], axis=0)
            got = gather_heads(both, ej[:HP])
            tq = tq + got[:, :QC]
            lv = lv + got[:, QC:]
            d_b = d_b + mm_nt((xf * tailj).astype(BF), after)
            d_c = d_c + mm_nt(ledb, before)
            colbuf[s, 0:1, at] = jnp.sum(now * before.astype(F4), axis=0, keepdims=True)
            colbuf[s, 1:2, at] = jnp.sum(dyf * xf, axis=0, keepdims=True)
            ds[s, :, at] = now * grow[:, at] + mm(c_t, ledb)
            wide = u + skip[:, at] * dyf
            for k in range(WIDE // 128):
                here = slice(j * WIDE + k * 128, j * WIDE + k * 128 + 128)
                dyp = dy_r[rows[s], here]
                d_ms = mm_nt(dyp, stacked(x_r[rows[s], here], halves))
                ws = []
                for half in range(2):
                    h = (j * WIDE + k * 128) // PS + half
                    gap = jnp.where(inside, cum_cols[:, h : h + 1] - sc[s, h : h + 1, :], NEG)
                    dec = jnp.exp(gap)
                    dtr = sc[s, HP + h : HP + h + 1, :]
                    sl_h = scores * dec
                    d_m = d_ms[:, half * QC : half * QC + QC]
                    g = d_m * sl_h
                    rowbuf[s, h : h + 1, :] = jnp.sum(g, axis=0, keepdims=True)
                    sums = jnp.where(lane == h, jnp.sum(g * dtr, axis=1, keepdims=True), sums)
                    d_sc = d_sc + d_m * (dec * dtr)
                    ws.append((sl_h * dtr).astype(BF))
                dx = wide[:, k * 128 : k * 128 + 128] + mm_tn(
                    jnp.concatenate(ws, axis=0), stacked(dyp, halves)
                )
                conv_back(s, here, xr[rows[s], here].astype(F4), dx.astype(BF).astype(F4), turned)
        d_scb = d_sc.astype(BF)
        d_b = d_b + mm_tn(d_scb, c)
        d_c = d_c + mm(d_scb, b)
        conv_back(s, slice(XW, XW + N), br[rows[s], :N].astype(F4), d_b, turned)
        conv_back(s, slice(XW + N, CW), br[rows[s], N:].astype(F4), d_c, turned)
        ecol = rowbuf[s]
        both = gather_fine(colbuf[s], e[:HP, :])
        at_end = jnp.sum(tq, axis=1, keepdims=True) + lead_last * both[:, 0:1]
        d_cum = jnp.transpose(sums)[:HP] - dt * ecol - tq + lv
        d_la = running(d_cum + jnp.where(place == QC - 1, at_end, 0.0), True)
        v = jnp.transpose(rr[rows[s], :].astype(F4))[:HP] + hp[0]
        d_rate = (ecol + tq / jnp.maximum(dt, 1e-30) + d_la * hp[1]) * sigmoid(v)
        draw_o[rows[s], CW:] = cols_of(d_rate).astype(BF)
        hg[0] = hg[0] + d_rate
        hg[1] = hg[1] + d_la * dt * hp[1]
        hg[2] = hg[2] + jnp.where(place == 0, both[:, 1:2], 0.0)
    cg_o[...] = cg[...]
    hg_o[...] = hg[...]


def scan_back(seqs, x, bc, sl, sc, meta, ent, dy, d_end, raw, halo, taps, hp, skip, e):
    length = x.shape[0]
    span = seqs * QC
    n = length // span
    sd = jax.ShapeDtypeStruct
    return pl.pallas_call(
        back_kernel,
        grid=(n,),
        in_specs=[
            behind(n, span, XW),
            behind(n, span, 2 * N),
            behind(n, span, CW),
            behind3(n, seqs, 2 * HP, 128),
            behind3(n, seqs, 8, 128),
            behind3(n, seqs, N, XW),
            behind(n, span, XW),
            fixed(seqs, N, XW),
            behind(n, span, XW),
            behind(n, span, 2 * N, XW // (2 * N)),
            behind(n, span, 128, CW // 128),
            fixed(seqs, 8, CW),
            fixed(8, CW),
            fixed(2, HP, 128),
            fixed(1, XW),
            fixed(128, XW),
        ],
        out_specs=[behind(n, span, AW), fixed(seqs, 8, CW), fixed(8, CW), fixed(3, HP, 128)],
        out_shape=[
            sd((length, AW), BF),
            sd((seqs, 8, CW), BF),
            sd((8, CW), F4),
            sd((3, HP, 128), F4),
        ],
        scratch_shapes=[
            pltpu.VMEM((seqs, N, XW), F4),
            pltpu.VMEM((seqs, 8, CW), F4),
            pltpu.VMEM((seqs, 8, XW), F4),
            pltpu.VMEM((seqs, HP, 128), F4),
            pltpu.VMEM((8, CW), F4),
            pltpu.VMEM((3, HP, 128), F4),
        ],
        compiler_params=pltpu.CompilerParams(vmem_limit_bytes=LIMIT),
        cost_estimate=work(length, 2),
        name="scan_back",
    )(x, bc, sl, sc, meta, ent, dy, d_end, raw, raw, raw, halo, taps, hp, skip, e)


def last_kernel(x_r, xbc_o, dt_o, taps_o, bias_o, gate_o, norm_o, h0_o, h1_o, h2_o):
    own = xbc_o.shape[0]
    r = lax.broadcasted_iota(jnp.int32, (128, 128), 0)
    c = lax.broadcasted_iota(jnp.int32, (128, 128), 1)
    bc = jnp.zeros((own, 2 * N), F4)
    dt = jnp.zeros((own, 128), F4)
    shared = jnp.zeros((8, AW), F4)
    heads = [jnp.zeros((16, 128), F4) for _ in range(3)]
    for g in range(GROUP):
        at = slice(g * XW, g * XW + XW)
        xbc_o[:, at] = x_r[g, :own, :XW].astype(F4)
        bc = bc + x_r[g, :own, XW:CW].astype(F4)
        move = ((c == r + HG * g) & (r < HG)).astype(BF)
        dt = dt + mm(x_r[g, :own, CW:], move)
        tail = x_r[g, own:, :].astype(F4)
        both = tail[:8] + tail[8:]
        taps_o[:, at] = both[:4, :XW]
        bias_o[:, at] = both[4:5, :XW]
        gate_o[:, at] = both[5:6, :XW]
        shared = shared + both
        for p in range(3):
            move = ((c - HG * g == r - HP * p) & (r >= HP * p) & (r < HP * p + HG)).astype(BF)
            heads[p] = heads[p] + mm(tail[:, XW : XW + 128].astype(BF), move)
    xbc_o[:, DI:] = bc
    dt_o[...] = dt[:, :H]
    taps_o[:, DI:] = shared[:4, XW:CW]
    bias_o[:, DI:] = shared[4:5, XW:CW]
    norm_o[:, :AW] = shared[6:7, :]
    norm_o[:, AW:] = shared[7:8, : norm_o.shape[1] - AW]
    for p, ref in enumerate((h0_o, h1_o, h2_o)):
        ref[...] = heads[p][5:6, :H] + heads[p][13:14, :H]


def last_outputs(x_all, own, width):
    sd = jax.ShapeDtypeStruct
    vm = pl.BlockSpec(memory_space=pltpu.VMEM)
    shapes = [(own, DI + 2 * N), (own, H), (4, DI + 2 * N), (1, DI + 2 * N), (1, DI), (1, width)]
    shapes.extend([(1, H)] * 3)
    return pl.pallas_call(
        last_kernel,
        out_shape=[sd(shape, F4) for shape in shapes],
        in_specs=[vm],
        out_specs=[vm] * len(shapes),
        compiler_params=pltpu.CompilerParams(vmem_limit_bytes=LIMIT),
        name="last_outputs",
    )(x_all)


def down_kernel(a, w, base, n, o, dots):
    v = mm_nt(a[...], w[...]) + base[...].astype(F4)
    o[...] = v.astype(BF)
    dots[...] = jnp.sum(v * n[...].astype(F4), axis=0, keepdims=True)


def down(a, w, base, normed):
    length, inner = a.shape
    width = w.shape[0]
    cols = 256
    return pl.pallas_call(
        down_kernel,
        grid=(width // cols,),
        in_specs=[
            fixed(length, inner),
            ahead(cols, inner),
            pl.BlockSpec((length, cols), lambda i: (0, i)),
            pl.BlockSpec((length, cols), lambda i: (0, i)),
        ],
        out_specs=[
            pl.BlockSpec((length, cols), lambda i: (0, i)),
            pl.BlockSpec((1, cols), lambda i: (0, i)),
        ],
        out_shape=[
            jax.ShapeDtypeStruct((length, width), BF),
            jax.ShapeDtypeStruct((1, width), F4),
        ],
        compiler_params=pltpu.CompilerParams(vmem_limit_bytes=LIMIT),
        name="down_proj",
    )(a, w, base, normed)


def pad_lanes(v, width):
    return jnp.pad(v, [(0, 0)] * (v.ndim - 1) + [(0, width - v.shape[-1])])


def carried(state, decay, hops, by):
    total = shift(state, CHAIN, by)
    if hops == 1:
        return total
    total, product = total.astype(F4), 1.0
    for j in range(2, hops + 1):
        product = product * shift(decay, CHAIN, by * (j - 1))
        total = total + product * shift(state, CHAIN, by * j).astype(F4)
    return total.astype(BF)


def shards(
    tokens_in, seg_ids, in_norm, z_proj, xbc_proj, dt_proj, conv_taps, conv_bias,
    dt_bias, a_log, d_skip, gate_norm, out_proj, out_cotangent,
):
    seqs, rows, width = tokens_in.shape
    length = seg_ids.shape[1]
    block = rows * GROUP
    n_blocks = length // block
    hops = min(-(-(length // 4 - 1) // block), n_blocks - 1)
    n_sums = lax.axis_size("dp") * n_blocks
    hl = lax.axis_index("hl")
    own_rows = z_proj.shape[0]

    def collected(part):
        return lax.all_gather(part, "hl", axis=0).reshape(GROUP * seqs * rows, width)

    def quarters(w):
        return w.reshape(w.shape[0], GROUP, -1).transpose(1, 0, 2)

    bc_cols = jnp.broadcast_to(xbc_proj[None, :, DI:], (GROUP, own_rows, 2 * N))
    parts = [quarters(xbc_proj[:, :DI]), bc_cols, pad_lanes(quarters(dt_proj), 128), quarters(z_proj)]
    parts = jnp.concatenate(parts, axis=-1)
    if plain():
        def part_of(k):
            return lax.dynamic_index_in_dim(parts, jnp.bitwise_xor(hl, k), 0, keepdims=False)

        near_parts = [part_of(0)] + [swap(part_of(k), "hl", k) for k in (3, 2, 1)][::-1]
        in_mine = placed(hl.astype(jnp.int32).reshape(1), near_parts)
    else:
        in_mine = lax.all_to_all(parts, "hl", 0, 0, tiled=True)
        in_mine = in_mine.reshape(GROUP * own_rows, AW + XW)
    pairs = [(f, (f % n_sums) * GROUP + f // n_sums) for f in range(GROUP * n_sums)]
    wo_mine = lax.ppermute(out_proj, EVERY, pairs)
    in_mine, wo_mine, tokens_now = lax.optimization_barrier((in_mine, wo_mine, tokens_in))
    tokens = collected(tokens_now)
    cot = collected(out_cotangent)
    wx, wz = all_rows(near_rows(in_mine), [(0, AW), (AW, AW + XW)])
    wx, wz, wo_mine = lax.optimization_barrier((wx, wz, wo_mine))
    wo_near = near_rows(wo_mine)

    def mine(v, size):
        return lax.dynamic_slice_in_dim(v, hl * size, size, axis=-1)

    taps = jnp.concatenate([conv_taps, conv_bias[None]], axis=0)
    taps = jnp.concatenate([mine(taps[:, :DI], XW), taps[:, DI:]], axis=1)
    taps = jnp.pad(taps, ((0, 3), (0, 0)))
    hp = jnp.stack([mine(dt_bias, HG), -jnp.exp(mine(a_log, HG))])
    hp = jnp.broadcast_to(jnp.pad(hp, ((0, 0), (0, HP - HG)))[:, :, None], (2, HP, 128))
    skip = jnp.repeat(mine(d_skip, HG), PS)[None]
    gain = mine(gate_norm, XW)[None]
    e = (jnp.arange(128)[:, None] == jnp.arange(XW)[None, :] // PS).astype(BF)

    start = lax.axis_index(CHAIN) * block
    seg_pad = jnp.concatenate([jnp.full((seqs, 8), -1, jnp.int32), seg_ids], axis=1)
    near = lax.dynamic_slice_in_dim(seg_pad, start, block + 8, axis=1)
    seg = near[:, 8:].reshape(seqs, GROUP, QC)
    lines = [seg, jnp.broadcast_to(near[:, 7 : 7 + block : QC][:, :, None], seg.shape)]
    lines.append(jnp.broadcast_to(seg[:, :, QC - 1 :], seg.shape))
    for k in range(KW - 1):
        lines.append((near[:, 5 + k : 5 + k + block].reshape(seg.shape) == seg).astype(jnp.int32))
    lines.extend([jnp.zeros_like(seg)] * 2)
    meta = jnp.stack(lines, axis=2).astype(F4)
    meta = meta.transpose(1, 0, 2, 3).reshape(GROUP * seqs, 8, QC)

    tokens, wx, wz, meta, taps, hp, skip, gain, e = lax.optimization_barrier(
        (tokens, wx, wz, meta, taps, hp, skip, gain, e)
    )
    normed = norm_rows(tokens.astype(F4), in_norm).astype(BF)
    raw = mm(normed, wx).astype(BF)
    raw, *wo_near = lax.optimization_barrier((raw, *wo_near))
    [wo] = all_rows(wo_near, [(0, width)])
    last = raw.reshape(GROUP, seqs, rows, AW)[GROUP - 1, :, rows - 8 :, :CW]
    halo = shift(last, CHAIN, 1)
    x, bc, sl, sc, state, decay = front(seqs, raw, halo, meta, taps, hp, e)
    decay_row = jnp.repeat(decay[:, :HG, 0], PS, axis=-1)[:, None]
    state, z_normed = lax.optimization_barrier((state, normed))
    s_in = carried(state, decay_row, hops, 1)
    gates = mm(z_normed, wz)
    s_in, wo = lax.optimization_barrier((s_in, wo))
    y, sg, ent, squares = scan(seqs, x, bc, sc, meta, s_in, gates, skip, gain, e)

    def team_sum(part):
        total = part
        for k in range(1, GROUP):
            total = total + swap(part, "hl", k)
        return total

    def spread_sum(part):
        total = lax.psum_scatter(part, "hl", scatter_dimension=0, tiled=True)
        return total.reshape(seqs, rows, width)

    out_rows = mm(sg, wo).astype(BF)
    squares = team_sum(squares)
    cot, out_rows, squares = lax.optimization_barrier((cot, out_rows, squares))
    d_gated = mm_nt(cot, wo)
    row_scale = lax.rsqrt(squares * (1.0 / DI) + EPS)
    gated = (sg.astype(F4) * row_scale.reshape(-1, 1)).astype(BF)
    along = team_sum(jnp.sum(d_gated * sg.astype(F4), axis=1).reshape(squares.shape))
    out_sum = spread_sum(out_rows)
    dp = lax.axis_index("dp")
    if plain():
        o_give, o_keep = (mm_tn(half_of(gated, at), cot).astype(BF) for at in (1 - dp, dp))
    dy, dz, gg, d_state = gate(seqs, y, gates, d_gated, squares, along, bc, sc, meta, gain, e)
    d_end = carried(d_state, decay_row, hops, -1)
    if plain():
        n_give, n_keep = (half_of(normed, at) for at in (1 - dp, dp))
        z_give, z_keep = (mm_tn(v, dz).astype(BF) for v in (n_give, n_keep))
        dy, z_give, z_keep = lax.optimization_barrier((dy, z_give, z_keep))
        z_got, o_got = swap(z_give, "dp", 1), swap(o_give, "dp", 1)
        early = []
        for z_part, o_part in zip(chain_pieces(z_keep, z_got), chain_pieces(o_keep, o_got)):
            early.append(jnp.concatenate([z_part, o_part[:, : width // 2], o_part[:, width // 2 :]]))
        dy, *early = lax.optimization_barrier((dy, *early))
        early = chain_sum(early)
    draw, rim, conv_total, head_total = scan_back(
        seqs, x, bc, sl, sc, meta, ent, dy, d_end, raw, halo, taps, hp, skip, e
    )
    rim = shift(rim, CHAIN, -1)
    from_z = mm_nt(dz, wz).astype(BF)
    if plain():
        rim, from_z, out_sum, early = lax.optimization_barrier((rim, from_z, out_sum, early))
    draw = draw.reshape(GROUP, seqs, rows, AW)
    edge = draw[GROUP - 1 :, :, rows - 8 :, :CW].astype(F4) + rim.astype(F4)
    draw = lax.dynamic_update_slice(draw, edge.astype(BF), (GROUP - 1, 0, rows - 8, 0))
    draw = draw.reshape(GROUP * seqs * rows, AW)

    if plain():
        z_rows = GROUP * own_rows
        o_rows = (early.shape[0] - z_rows) // 2
        z_own = early[:z_rows].reshape(GROUP, own_rows, XW)
        o_own = jnp.concatenate([early[z_rows : z_rows + o_rows], early[z_rows + o_rows :]], axis=1)
        o_back = lax.ppermute(o_own, EVERY, [(b, a) for a, b in pairs])
        z_all = lax.all_to_all(z_own, "hl", 0, 0, tiled=True)
        d_low, norm_total = down(draw, wx, from_z, normed)
        d_low, draw, z_all, o_back = lax.optimization_barrier((d_low, draw, z_all, o_back))
        out_proj_grad = o_back.astype(F4)
        x_give = mm_tn(n_give, draw).astype(BF)
        x_give, draw = lax.optimization_barrier((x_give, draw))
        x_got = swap(x_give, "dp", 1)
        x_keep = mm_tn(n_keep, draw).astype(BF)
        x_pieces = chain_pieces(x_keep, x_got)
        x_own = chain_sum(x_pieces)
    else:
        grads = [mm_tn(normed, dz), mm_tn(gated, cot), mm_tn(normed, draw)]
        grads = [g.astype(BF) for g in grads]
        d_low, norm_total = down(draw, wx, from_z, normed)
        z_own, o_own, x_own = (
            lax.psum_scatter(g, SUMS, scatter_dimension=0, tiled=True) for g in grads
        )
    d_sum = spread_sum(d_low)
    if not plain():
        out_proj_grad = lax.ppermute(o_own, EVERY, [(b, a) for a, b in pairs]).astype(F4)

    heads = jnp.sum(head_total, axis=2).reshape(1, -1)
    norm_grad = norm_total / in_norm[None]
    pack = jnp.concatenate(
        [
            pad_lanes(conv_total[:5], AW),
            pad_lanes(jnp.concatenate([gg[:1], heads], axis=1), AW),
            norm_grad[:, :AW],
            pad_lanes(norm_grad[:, AW:], AW),
        ],
        axis=0,
    )
    for axis in SUMS:
        pack = pack + sum(swap(pack, axis, k) for k in range(1, lax.axis_size(axis)))
    high = pack.astype(BF)
    small = jnp.concatenate([high, (pack - high.astype(F4)).astype(BF)], axis=0)
    small = jnp.broadcast_to(small[None], (GROUP, 16, AW))
    x_own = jnp.concatenate([x_own.reshape(GROUP, own_rows, AW), small], axis=1)
    if not plain():
        z_all = lax.all_to_all(z_own.reshape(GROUP, own_rows, XW), "hl", 0, 0, tiled=True)
    x_all = lax.all_to_all(x_own, "hl", 0, 0, tiled=True)

    u = tokens_in.astype(F4)
    scale = lax.rsqrt(jnp.mean(u * u, axis=-1, keepdims=True) + EPS)
    hat = u * scale
    dh = d_sum.astype(F4) * in_norm
    along = jnp.mean(dh * hat, axis=-1, keepdims=True)
    x_all, along = lax.optimization_barrier((x_all, along))
    d_u = scale * (dh - hat * along)
    tokens_grad = d_u + out_cotangent.astype(F4)
    own_scale = lax.dynamic_index_in_dim(row_scale.reshape(GROUP, seqs, rows, 1), hl, 0, keepdims=False)
    layer_out = (tokens_in.astype(F4) + own_scale * out_sum.astype(F4)).astype(BF)
    z_proj_grad = z_all.transpose(1, 0, 2).reshape(own_rows, DI).astype(F4)
    if plain():
        outs = last_outputs(x_all, own_rows, width)
        xbc_proj_grad, dt_proj_grad, taps_grad = outs[:3]
        bias_grad, gate_grad, in_norm_grad = (v.reshape(-1) for v in outs[3:6])
        per_head = [v.reshape(-1) for v in outs[6:]]
    else:
        x_parts = x_all[:, :own_rows]
        xs = x_parts[:, :, :XW].transpose(1, 0, 2).reshape(own_rows, DI).astype(F4)
        bc_grad = jnp.sum(x_parts[:, :, XW:CW].astype(F4), axis=0)
        xbc_proj_grad = jnp.concatenate([xs, bc_grad], axis=1)
        dt_parts = x_parts[:, :, CW : CW + HG].transpose(1, 0, 2)
        dt_proj_grad = dt_parts.reshape(own_rows, H).astype(F4)
        got = x_all[:, own_rows:, :AW].astype(F4)
        got = got[:, :8] + got[:, 8:]
        conv_x = got[:, :5, :XW].transpose(1, 0, 2).reshape(5, DI)
        conv_all = jnp.concatenate([conv_x, jnp.sum(got[:, :5, XW:CW], axis=0)], axis=1)
        per_head = got[:, 5, XW : XW + 3 * HP].reshape(GROUP, 3, HP)[:, :, :HG]
        per_head = per_head.transpose(1, 0, 2).reshape(3, H)
        in_norm_grad = jnp.sum(got[:, 6:8], axis=0).reshape(-1)[:width]
        taps_grad, bias_grad, gate_grad = conv_all[:4], conv_all[4], got[:, 5, :XW].reshape(DI)
    return (
        layer_out,
        tokens_grad,
        in_norm_grad,
        z_proj_grad,
        xbc_proj_grad,
        dt_proj_grad,
        taps_grad,
        bias_grad,
        per_head[0],
        per_head[1],
        per_head[2],
        gate_grad,
        out_proj_grad,
    )


def solution(mesh):
    sizes = dict(mesh.shape)
    grid = mesh.devices.reshape(sizes["dp"], sizes["ctx"], sizes["hd"] // GROUP, GROUP)
    fine = Mesh(grid, ("dp", "ctx", "hh", "hl"))
    tok = P("dp", ("ctx", "hh", "hl"), None)
    wgt = P(("dp", "ctx", "hh", "hl"), None)
    in_specs = (tok, P("dp", None), P(), wgt, wgt, wgt, P(), P(), P(), P(), P(), P(), wgt, tok)
    out_specs = (tok, tok, P(), wgt, wgt, wgt, P(), P(), P(), P(), P(), P(), wgt)
    return jax.shard_map(shards, mesh=fine, in_specs=in_specs, out_specs=out_specs, check_vma=False)
```

```python
import jax
import jax.numpy as jnp
from jax import lax
from jax.experimental import pallas as pl
from jax.experimental.pallas import tpu as pltpu
from jax.sharding import Mesh, PartitionSpec as P

H = 48
PS = 64
N = 128
KW = 4
DI = 3072
GROUP = 4
HG = H // GROUP
HP = 16
XW = HG * PS
CW = XW + 2 * N
AW = CW + 128
QC = 128
EPS = 1e-05
NEG = -1e30
BF = jnp.bfloat16
F4 = jnp.float32
LIMIT = 48 * 1024 * 1024
SUMS = ("dp", "ctx", "hh")
CHAIN = ("ctx", "hh")
EVERY = ("dp", "ctx", "hh", "hl")


def swap(part, axis, k):
    count = lax.axis_size(axis)
    return lax.ppermute(part, axis, [(i, i ^ k) for i in range(count)])


def shift(part, axes, by):
    count = 1
    for axis in axes:
        count = count * lax.axis_size(axis)
    pairs = [(i, i + by) for i in range(count) if 0 <= i + by < count]
    return lax.ppermute(part, axes, pairs)


def mm(a, b):
    return jnp.dot(a, b, preferred_element_type=F4)


def mm_nt(a, b):
    return lax.dot_general(a, b, (((1,), (1,)), ((), ())), preferred_element_type=F4)


def mm_tn(a, b):
    return lax.dot_general(a, b, (((0,), (0,)), ((), ())), preferred_element_type=F4)


def grown(lead_last, e):
    v = lead_last[:, :8]
    hi = v.astype(BF)
    lo = (v - hi.astype(F4)).astype(BF)
    return (mm_tn(hi, e[:HP, :]) + mm_tn(lo, e[:HP, :]))[0:1, :]


def gather_heads(w, e):
    return mm_nt(e, w.astype(BF))


def gather_fine(w, e):
    hi = w.astype(BF)
    lo = (w - hi.astype(F4)).astype(BF)
    return mm_nt(e, hi) + mm_nt(e, lo)


def turn(v):
    return jnp.transpose(v.astype(F4)).astype(BF)


def sigmoid(v):
    return 0.5 * jnp.tanh(0.5 * v) + 0.5


def norm_rows(values, gain):
    return values * lax.rsqrt(jnp.mean(values * values, axis=-1, keepdims=True) + EPS) * gain


def running(v, back):
    r = lax.broadcasted_iota(jnp.int32, (QC, QC), 0)
    q = lax.broadcasted_iota(jnp.int32, (QC, QC), 1)
    ones = ((r >= q) if back else (r <= q)).astype(BF)
    hi = v.astype(BF)
    rest = v - hi.astype(F4)
    mid = rest.astype(BF)
    lo = (rest - mid.astype(F4)).astype(BF)
    got = mm(jnp.concatenate([hi, mid, lo], axis=0), ones)
    n = v.shape[0]
    return got[:n] + got[n : 2 * n] + got[2 * n :]


def lines_of(mt):
    return jnp.transpose(jnp.concatenate([mt, jnp.zeros((QC - 8, QC), F4)], axis=0))


def full(col):
    return jnp.broadcast_to(col, (QC, 128))


def tiles(count, width=128):
    return [slice(j * width, j * width + width) for j in range(count)]


WIDE = 256


def stacked(v, halves):
    return jnp.concatenate([v * halves[0], v * halves[1]], axis=0)


def col_of(row):
    return jnp.transpose(jnp.broadcast_to(row, (QC, QC)))


def cols_of(v):
    return jnp.transpose(jnp.concatenate([v, jnp.zeros((QC - HP, QC), F4)], axis=0))


def place_kernel(place, *refs):
    out = refs[-1]
    rows = refs[0].shape[0]
    for k, ref in enumerate(refs[:-1]):
        slot = jnp.bitwise_xor(place[0], k)
        out[pl.ds(pl.multiple_of(slot * rows, rows), rows), :] = ref[...]


def placed(place, pieces):
    rows, width = pieces[0].shape
    vm = pl.BlockSpec(memory_space=pltpu.VMEM)
    return pl.pallas_call(
        place_kernel,
        out_shape=jax.ShapeDtypeStruct((len(pieces) * rows, width), BF),
        in_specs=[pl.BlockSpec(memory_space=pltpu.SMEM)] + [vm] * len(pieces),
        out_specs=vm,
        compiler_params=pltpu.CompilerParams(vmem_limit_bytes=LIMIT),
        name="place_rows",
    )(place, *pieces)


def joined(cur, got, side):
    low = jnp.where(side == 0, cur, got)
    high = jnp.where(side == 0, got, cur)
    return jnp.concatenate([low, high], axis=0)


def plain():
    return lax.axis_size("hh") == 1


def near_rows(mine):
    if not plain() or mine.shape[0] % 16:
        return [mine]
    return [mine] + [swap(mine, "ctx", k) for k in range(1, lax.axis_size("ctx"))]


def all_rows(pieces, cuts):
    if len(pieces) == 1:
        whole = lax.all_gather(pieces[0], SUMS, axis=0, tiled=True)
        return [whole[:, a:b] for a, b in cuts]
    stack = placed(lax.axis_index("ctx").astype(jnp.int32).reshape(1), pieces)
    got = swap(stack, "dp", 1)
    side = lax.axis_index("dp")
    return [joined(stack[:, a:b], got[:, a:b], side) for a, b in cuts]


def half_of(v, side):
    return lax.dynamic_slice_in_dim(v, side * (v.shape[1] // 2), v.shape[1] // 2, axis=1)


def chain_pieces(keep, got):
    count = lax.axis_size("ctx")
    ctx = lax.axis_index("ctx")
    keep = keep.reshape(count, -1, keep.shape[-1])
    got = got.reshape(keep.shape)
    pieces = []
    for k in range(count):
        at = jnp.bitwise_xor(ctx, k)
        parts = [lax.dynamic_index_in_dim(v, at, 0, keepdims=False) for v in (keep, got)]
        pieces.append((parts[0].astype(F4) + parts[1].astype(F4)).astype(BF))
    return pieces


def chain_sum(pieces):
    out = pieces[0].astype(F4)
    for k in range(1, len(pieces)):
        out = out + swap(pieces[k], "ctx", k).astype(F4)
    return out.astype(BF)


def work(length, us):
    flops = int(us * 1e9) * length // 1024
    return pl.CostEstimate(flops=flops, transcendentals=0, bytes_accessed=length * 8192)


def fixed(*shape):
    return pl.BlockSpec(shape, lambda i: (0,) * len(shape))


def ahead(rows, width, at=0):
    return pl.BlockSpec((rows, width), lambda i: (i, at))


def ahead3(seqs, *shape):
    return pl.BlockSpec((seqs, *shape), lambda i: (i, 0, 0))


def behind(n, rows, width, at=0):
    return pl.BlockSpec((rows, width), lambda i: (n - 1 - i, at))


def behind3(n, seqs, *shape):
    return pl.BlockSpec((seqs, *shape), lambda i: (n - 1 - i, 0, 0))


def decays(cum, mt):
    last = cum[:, QC - 1 : QC]
    same_last = (mt[0:1, :] == mt[2:3, :]).astype(F4)
    follows = (mt[1:2, :] == mt[2:3, :]).astype(F4)
    tail0 = jnp.exp(last - cum) * same_last
    lead_last = jnp.exp(last) * follows
    return tail0, lead_last


def front_kernel(
    xr, br, rr, halo, meta, taps, hp, e, x_o, bc_o, sl_o, sc_o, st_o, dec_o, buf, st, dec
):
    i = pl.program_id(0)
    seqs = halo.shape[0]

    @pl.when(i == 0)
    def _():
        buf[:, 0:8, :] = halo[...].astype(F4)
        st[...] = jnp.zeros_like(st)
        dec[...] = jnp.ones_like(dec)

    @pl.when(i > 0)
    def _():
        buf[:, 0:8, :] = buf[:, QC : QC + 8, :]

    every = range(seqs)
    rows = [slice(s * QC, s * QC + QC) for s in every]
    tails, lasts = [], []
    for s in every:
        v = jnp.transpose(rr[rows[s], :].astype(F4))[:HP] + hp[0]
        dt = jnp.maximum(v, 0.0) + jnp.log1p(jnp.exp(-jnp.abs(v)))
        cum = running(dt * hp[1], False)
        sc_o[s, 0:HP, :] = cum
        sc_o[s, HP:, :] = dt
        tail0, lead_last = decays(cum, meta[s])
        dec[s] = dec[s] * lead_last
        tails.append(cols_of(tail0 * dt).astype(BF))
        lasts.append(grown(lead_last, e))
    order = tiles(CW // 128)
    n_x = XW // 128
    for s in every:
        turned = lines_of(meta[s])
        masks = [full(turned[:, 3 + k : 4 + k]) for k in range(3)]
        for j in [*range(n_x, len(order)), *range(n_x)]:
            c = order[j]
            if j < n_x:
                own = xr[rows[s], c].astype(F4)
            else:
                own = br[rows[s], j * 128 - XW : j * 128 - XW + 128].astype(F4)
            buf[s, 8 : QC + 8, c] = own
            mixed = taps[4:5, c] + taps[3:4, c] * own
            for k in range(3):
                mixed = mixed + taps[k : k + 1, c] * (
                    buf[s, 5 + k : 5 + k + QC, c] * masks[k]
                )
            sig = sigmoid(mixed)
            act = (mixed * sig).astype(BF)
            sl_o[rows[s], c] = (sig + mixed * sig * (1.0 - sig)).astype(BF)
            if j < n_x:
                x_o[rows[s], c] = act
                if j % 2:
                    c2 = slice(j * 128 - 128, j * 128 + 128)
                    pair = jnp.concatenate([held, act], axis=1).astype(F4)
                    xw = (pair * mm(tails[s], e[:, c2])).astype(BF)
                    st[s, :, c2] = st[s, :, c2] * lasts[s][:, c2] + mm(b_t, xw)
                held = act
            else:
                bc_o[rows[s], j * 128 - XW : j * 128 - XW + 128] = act
                if j == n_x:
                    b_t = turn(act)
    st_o[...] = st[...].astype(BF)
    dec_o[...] = dec[...]


def front(seqs, raw, halo, meta, taps, hp, e):
    length = raw.shape[0]
    span = seqs * QC
    sd = jax.ShapeDtypeStruct
    return pl.pallas_call(
        front_kernel,
        grid=(length // span,),
        in_specs=[
            ahead(span, XW),
            ahead(span, 2 * N, XW // (2 * N)),
            ahead(span, 128, CW // 128),
            fixed(seqs, 8, CW),
            ahead3(seqs, 8, 128),
            fixed(8, CW),
            fixed(2, HP, 128),
            fixed(128, XW),
        ],
        out_specs=[
            ahead(span, XW),
            ahead(span, 2 * N),
            ahead(span, CW),
            ahead3(seqs, 2 * HP, 128),
            fixed(seqs, N, XW),
            fixed(seqs, HP, 128),
        ],
        out_shape=[
            sd((length, XW), BF),
            sd((length, 2 * N), BF),
            sd((length, CW), BF),
            sd((length // QC, 2 * HP, 128), F4),
            sd((seqs, N, XW), BF),
            sd((seqs, HP, 128), F4),
        ],
        scratch_shapes=[
            pltpu.VMEM((seqs, QC + 8, CW), F4),
            pltpu.VMEM((seqs, N, XW), F4),
            pltpu.VMEM((seqs, HP, 128), F4),
        ],
        compiler_params=pltpu.CompilerParams(vmem_limit_bytes=LIMIT),
        cost_estimate=work(length, 1),
        name="conv_state",
    )(raw, raw, raw, halo, meta, taps, hp, e)


def lane_halves():
    lane = lax.broadcasted_iota(jnp.int32, (1, 128), 1)
    return [(lane < PS).astype(BF), (lane >= PS).astype(BF)]


def inside_of(mt):
    r = lax.broadcasted_iota(jnp.int32, (QC, QC), 0)
    q = lax.broadcasted_iota(jnp.int32, (QC, QC), 1)
    return (col_of(mt[0:1, :]) == mt[0:1, :]) & (r >= q)


def scan_kernel(x_r, bc, sc, meta, s_in, z_r, skip, gain, e, y_o, sg_o, ent_o, sum_o, st):
    i = pl.program_id(0)
    seqs = s_in.shape[0]
    every = range(seqs)
    rows = [slice(s * QC, s * QC + QC) for s in every]

    @pl.when(i == 0)
    def _():
        st[...] = s_in[...].astype(F4)

    halves = lane_halves()
    for s in every:
        mt = meta[s]
        cum, dt = sc[s, 0:HP, :], sc[s, HP:, :]
        b, c = bc[rows[s], :N], bc[rows[s], N:]
        lead = cols_of(jnp.exp(cum) * (mt[0:1, :] == mt[1:2, :]).astype(F4)).astype(BF)
        tail0, lead_last = decays(cum, mt)
        tail = cols_of(tail0 * dt).astype(BF)
        b_t = turn(b)
        scores = mm_nt(c, b)
        inside = inside_of(mt)
        cum_cols = cols_of(cum)
        squares = jnp.zeros((QC, 128), F4)
        grow = grown(lead_last, e)
        for j, at in enumerate(tiles(XW // WIDE, WIDE)):
            ej = e[:, at]
            xf = x_r[rows[s], at].astype(F4)
            now = st[s, :, at]
            before = now.astype(BF)
            ent_o[s, :, at] = before
            wide = mm(lead, ej) * mm(c, before) + skip[:, at] * xf
            xw = (xf * mm(tail, ej)).astype(BF)
            st[s, :, at] = now * grow[:, at] + mm(b_t, xw)
            for k in range(WIDE // 128):
                here = slice(j * WIDE + k * 128, j * WIDE + k * 128 + 128)
                xp = x_r[rows[s], here]
                ws = []
                for half in range(2):
                    h = (j * WIDE + k * 128) // PS + half
                    gap = jnp.where(inside, cum_cols[:, h : h + 1] - sc[s, h : h + 1, :], NEG)
                    ws.append((scores * jnp.exp(gap) * sc[s, HP + h : HP + h + 1, :]).astype(BF))
                y = wide[:, k * 128 : k * 128 + 128] + mm(jnp.concatenate(ws, axis=1), stacked(xp, halves))
                low = y.astype(BF)
                y_o[rows[s], here] = low
                z = z_r[rows[s], here]
                v = low.astype(F4) * z * sigmoid(z)
                squares = squares + v * v
                sg_o[rows[s], here] = (v * gain[:, here]).astype(BF)
        sum_o[s] = jnp.sum(jnp.transpose(squares), axis=0, keepdims=True)


def scan(seqs, x, bc, sc, meta, s_in, z, skip, gain, e):
    length = x.shape[0]
    span = seqs * QC
    chunks = length // QC
    sd = jax.ShapeDtypeStruct
    return pl.pallas_call(
        scan_kernel,
        grid=(length // span,),
        in_specs=[
            ahead(span, XW),
            ahead(span, 2 * N),
            ahead3(seqs, 2 * HP, 128),
            ahead3(seqs, 8, 128),
            fixed(seqs, N, XW),
            ahead(span, XW),
            fixed(1, XW),
            fixed(1, XW),
            fixed(128, XW),
        ],
        out_specs=[ahead(span, XW), ahead(span, XW), ahead3(seqs, N, XW), ahead3(seqs, 1, QC)],
        out_shape=[
            sd((length, XW), BF),
            sd((length, XW), BF),
            sd((chunks, N, XW), BF),
            sd((chunks, 1, QC), F4),
        ],
        scratch_shapes=[pltpu.VMEM((seqs, N, XW), F4)],
        compiler_params=pltpu.CompilerParams(vmem_limit_bytes=LIMIT),
        cost_estimate=work(length, 1),
        name="scan_gate",
    )(x, bc, sc, meta, s_in, z, skip, gain, e)


def gate_kernel(y_r, z_r, dg_r, sq, al, bc, sc, meta, gain, e, dy_o, dz_o, gg_o, ds_o, ds, gg):
    i = pl.program_id(0)
    seqs = ds.shape[0]
    every = range(seqs)
    rows = [slice(s * QC, s * QC + QC) for s in every]

    @pl.when(i == 0)
    def _():
        gg[...] = jnp.zeros_like(gg)
        ds[...] = jnp.zeros_like(ds)

    for s in every:
        mt = meta[s]
        cum = sc[s, 0:HP, :]
        c = bc[rows[s], N:]
        scale = lax.rsqrt(sq[s] * (1.0 / DI) + EPS)
        rstd = jnp.concatenate([col_of(scale)] * (WIDE // 128), axis=1)
        pull = col_of(al[s] * (scale * scale * scale) * (1.0 / DI))
        pull = jnp.concatenate([pull] * (WIDE // 128), axis=1)
        lead = cols_of(jnp.exp(cum) * (mt[0:1, :] == mt[1:2, :]).astype(F4)).astype(BF)
        _, lead_last = decays(cum, mt)
        c_t = turn(c)
        grow = grown(lead_last, e)
        for at in tiles(XW // WIDE, WIDE):
            ej = e[:, at]
            y = y_r[rows[s], at].astype(F4)
            z = z_r[rows[s], at]
            sig = sigmoid(z)
            act = z * sig
            v = y * act
            dg = dg_r[rows[s], at] * rstd
            gg[0:1, at] = gg[0:1, at] + jnp.sum(dg * v, axis=0, keepdims=True)
            d_v = dg * gain[:, at] - v * pull
            dy = (d_v * act).astype(BF)
            dy_o[rows[s], at] = dy
            dz_o[rows[s], at] = (d_v * y * (sig + act * (1.0 - sig))).astype(BF)
            led = (dy.astype(F4) * mm(lead, ej)).astype(BF)
            ds[s, :, at] = ds[s, :, at] * grow[:, at] + mm(c_t, led)
    ds_o[...] = ds[...].astype(BF)
    gg_o[...] = gg[...]


def gate(seqs, y, z, dg, sq, al, bc, sc, meta, gain, e):
    length = y.shape[0]
    span = seqs * QC
    n = length // span
    sd = jax.ShapeDtypeStruct
    wide = behind(n, span, XW)
    line = behind3(n, seqs, 1, QC)
    return pl.pallas_call(
        gate_kernel,
        grid=(n,),
        in_specs=[
            wide,
            wide,
            wide,
            line,
            line,
            behind(n, span, 2 * N),
            behind3(n, seqs, 2 * HP, 128),
            behind3(n, seqs, 8, 128),
            fixed(1, XW),
            fixed(128, XW),
        ],
        out_specs=[wide, wide, fixed(8, XW), fixed(seqs, N, XW)],
        out_shape=[
            sd((length, XW), BF),
            sd((length, XW), BF),
            sd((8, XW), F4),
            sd((seqs, N, XW), BF),
        ],
        scratch_shapes=[pltpu.VMEM((seqs, N, XW), F4), pltpu.VMEM((8, XW), F4)],
        compiler_params=pltpu.CompilerParams(vmem_limit_bytes=LIMIT),
        cost_estimate=work(length, 1),
        name="gate_back",
    )(y, z, dg, sq, al, bc, sc, meta, gain, e)


def back_kernel(
    x_r, bc, sl, sc, meta, ent, dy_r, d_end, xr, br, rr, halo, taps, hp, skip, e,
    draw_o, rim_o, cg_o, hg_o,
    ds, carry, colbuf, rowbuf, cg, hg,
):
    i = pl.program_id(0)
    seqs = ds.shape[0]
    every = range(seqs)
    rows = [slice(s * QC, s * QC + QC) for s in every]
    first = (i == pl.num_programs(0) - 1).astype(F4)

    @pl.when(i == 0)
    def _():
        ds[...] = d_end[...].astype(F4)
        carry[...] = jnp.zeros_like(carry)
        cg[...] = jnp.zeros_like(cg)
        hg[...] = jnp.zeros_like(hg)
        colbuf[...] = jnp.zeros_like(colbuf)
        rowbuf[...] = jnp.zeros_like(rowbuf)

    halves = lane_halves()
    lane = lax.broadcasted_iota(jnp.int32, (1, 128), 1)
    token = lax.broadcasted_iota(jnp.int32, (QC, 128), 0)
    edge = lax.broadcasted_iota(jnp.int32, (8, 128), 0)
    place = lax.broadcasted_iota(jnp.int32, (HP, QC), 1)

    near_of = {}

    def conv_back(s, c, own, d_act, turned):
        dm = d_act * sl[rows[s], c].astype(F4)
        near = near_of[s]
        shifted = [dm]
        for k in range(3):
            ready = shifted[-1] * near
            moved = pltpu.roll(ready, QC - 1, 0)
            shifted.append(jnp.where(token == QC - 1, carry[s, k : k + 1, c], moved))
            carry[s, k : k + 1, c] = ready[0:1, :]
        d_raw = taps[3:4, c] * shifted[0]
        for k in range(3):
            d_raw = d_raw + taps[2 - k : 3 - k, c] * shifted[k + 1]
        draw_o[rows[s], c] = d_raw.astype(BF)
        parts = [jnp.sum(own * v, axis=0, keepdims=True) for v in shifted[::-1]]
        parts.append(jnp.sum(dm, axis=0, keepdims=True))
        head = dm[0:8, :]
        outside = halo[s, :, c].astype(F4) * first
        rim = jnp.zeros((8, 128), F4)
        for k in range(3):
            held = jnp.where(edge < 3 - k, head * turned[0:8, 3 + k : 4 + k], 0.0)
            held = pltpu.roll(held, 5 + k, 0)
            rim = rim + taps[k : k + 1, c] * held
            parts[k] = parts[k] + jnp.sum(outside * held, axis=0, keepdims=True)
        rim_o[s, :, c] = rim.astype(BF)
        cg[0:5, c] = cg[0:5, c] + jnp.concatenate(parts, axis=0)

    for s in every:
        mt = meta[s]
        turned = lines_of(mt)
        near_of[s] = full(turned[:, 5:6])
        cum, dt = sc[s, 0:HP, :], sc[s, HP:, :]
        b, c = bc[rows[s], :N], bc[rows[s], N:]
        lead = cols_of(jnp.exp(cum) * (mt[0:1, :] == mt[1:2, :]).astype(F4)).astype(BF)
        tail0, lead_last = decays(cum, mt)
        tail = cols_of(tail0 * dt).astype(BF)
        c_t = turn(c)
        scores = mm_nt(c, b)
        inside = inside_of(mt)
        cum_cols = cols_of(cum)
        d_sc = jnp.zeros((QC, QC), F4)
        sums = jnp.zeros((QC, 128), F4)
        tq = jnp.zeros((HP, QC), F4)
        lv = jnp.zeros((HP, QC), F4)
        d_b = jnp.zeros((QC, N), F4)
        d_c = jnp.zeros((QC, N), F4)
        grow = grown(lead_last, e)
        for j, at in enumerate(tiles(XW // WIDE, WIDE)):
            ej = e[:, at]
            xf = x_r[rows[s], at].astype(F4)
            dyf = dy_r[rows[s], at].astype(F4)
            before = ent[s, :, at]
            now = ds[s, :, at]
            after = now.astype(BF)
            tailj = mm(tail, ej)
            u = tailj * mm(b, after)
            led = dyf * mm(lead, ej)
            ledb = led.astype(BF)
            both = jnp.concatenate([xf * u, led * mm(c, before)], axis=0)
            got = gather_heads(both, ej[:HP])
            tq = tq + got[:, :QC]
            lv = lv + got[:, QC:]
            d_b = d_b + mm_nt((xf * tailj).astype(BF), after)
            d_c = d_c + mm_nt(ledb, before)
            colbuf[s, 0:1, at] = jnp.sum(now * before.astype(F4), axis=0, keepdims=True)
            colbuf[s, 1:2, at] = jnp.sum(dyf * xf, axis=0, keepdims=True)
            ds[s, :, at] = now * grow[:, at] + mm(c_t, ledb)
            wide = u + skip[:, at] * dyf
            for k in range(WIDE // 128):
                here = slice(j * WIDE + k * 128, j * WIDE + k * 128 + 128)
                dyp = dy_r[rows[s], here]
                d_ms = mm_nt(dyp, stacked(x_r[rows[s], here], halves))
                ws = []
                for half in range(2):
                    h = (j * WIDE + k * 128) // PS + half
                    gap = jnp.where(inside, cum_cols[:, h : h + 1] - sc[s, h : h + 1, :], NEG)
                    dec = jnp.exp(gap)
                    dtr = sc[s, HP + h : HP + h + 1, :]
                    sl_h = scores * dec
                    d_m = d_ms[:, half * QC : half * QC + QC]
                    g = d_m * sl_h
                    rowbuf[s, h : h + 1, :] = jnp.sum(g, axis=0, keepdims=True)
                    sums = jnp.where(lane == h, jnp.sum(g * dtr, axis=1, keepdims=True), sums)
                    d_sc = d_sc + d_m * (dec * dtr)
                    ws.append((sl_h * dtr).astype(BF))
                dx = wide[:, k * 128 : k * 128 + 128] + mm_tn(
                    jnp.concatenate(ws, axis=0), stacked(dyp, halves)
                )
                conv_back(s, here, xr[rows[s], here].astype(F4), dx.astype(BF).astype(F4), turned)
        d_scb = d_sc.astype(BF)
        d_b = d_b + mm_tn(d_scb, c)
        d_c = d_c + mm(d_scb, b)
        conv_back(s, slice(XW, XW + N), br[rows[s], :N].astype(F4), d_b, turned)
        conv_back(s, slice(XW + N, CW), br[rows[s], N:].astype(F4), d_c, turned)
        ecol = rowbuf[s]
        both = gather_fine(colbuf[s], e[:HP, :])
        at_end = jnp.sum(tq, axis=1, keepdims=True) + lead_last * both[:, 0:1]
        d_cum = jnp.transpose(sums)[:HP] - dt * ecol - tq + lv
        d_la = running(d_cum + jnp.where(place == QC - 1, at_end, 0.0), True)
        v = jnp.transpose(rr[rows[s], :].astype(F4))[:HP] + hp[0]
        d_rate = (ecol + tq / jnp.maximum(dt, 1e-30) + d_la * hp[1]) * sigmoid(v)
        draw_o[rows[s], CW:] = cols_of(d_rate).astype(BF)
        hg[0] = hg[0] + d_rate
        hg[1] = hg[1] + d_la * dt * hp[1]
        hg[2] = hg[2] + jnp.where(place == 0, both[:, 1:2], 0.0)
    cg_o[...] = cg[...]
    hg_o[...] = hg[...]


def scan_back(seqs, x, bc, sl, sc, meta, ent, dy, d_end, raw, halo, taps, hp, skip, e):
    length = x.shape[0]
    span = seqs * QC
    n = length // span
    sd = jax.ShapeDtypeStruct
    return pl.pallas_call(
        back_kernel,
        grid=(n,),
        in_specs=[
            behind(n, span, XW),
            behind(n, span, 2 * N),
            behind(n, span, CW),
            behind3(n, seqs, 2 * HP, 128),
            behind3(n, seqs, 8, 128),
            behind3(n, seqs, N, XW),
            behind(n, span, XW),
            fixed(seqs, N, XW),
            behind(n, span, XW),
            behind(n, span, 2 * N, XW // (2 * N)),
            behind(n, span, 128, CW // 128),
            fixed(seqs, 8, CW),
            fixed(8, CW),
            fixed(2, HP, 128),
            fixed(1, XW),
            fixed(128, XW),
        ],
        out_specs=[behind(n, span, AW), fixed(seqs, 8, CW), fixed(8, CW), fixed(3, HP, 128)],
        out_shape=[
            sd((length, AW), BF),
            sd((seqs, 8, CW), BF),
            sd((8, CW), F4),
            sd((3, HP, 128), F4),
        ],
        scratch_shapes=[
            pltpu.VMEM((seqs, N, XW), F4),
            pltpu.VMEM((seqs, 8, CW), F4),
            pltpu.VMEM((seqs, 8, XW), F4),
            pltpu.VMEM((seqs, HP, 128), F4),
            pltpu.VMEM((8, CW), F4),
            pltpu.VMEM((3, HP, 128), F4),
        ],
        compiler_params=pltpu.CompilerParams(vmem_limit_bytes=LIMIT),
        cost_estimate=work(length, 2),
        name="scan_back",
    )(x, bc, sl, sc, meta, ent, dy, d_end, raw, raw, raw, halo, taps, hp, skip, e)


def last_kernel(x_r, xbc_o, dt_o, taps_o, bias_o, gate_o, norm_o, h0_o, h1_o, h2_o):
    own = xbc_o.shape[0]
    r = lax.broadcasted_iota(jnp.int32, (128, 128), 0)
    c = lax.broadcasted_iota(jnp.int32, (128, 128), 1)
    bc = jnp.zeros((own, 2 * N), F4)
    dt = jnp.zeros((own, 128), F4)
    shared = jnp.zeros((8, AW), F4)
    heads = [jnp.zeros((16, 128), F4) for _ in range(3)]
    for g in range(GROUP):
        at = slice(g * XW, g * XW + XW)
        xbc_o[:, at] = x_r[g, :own, :XW].astype(F4)
        bc = bc + x_r[g, :own, XW:CW].astype(F4)
        move = ((c == r + HG * g) & (r < HG)).astype(BF)
        dt = dt + mm(x_r[g, :own, CW:], move)
        tail = x_r[g, own:, :].astype(F4)
        both = tail[:8] + tail[8:]
        taps_o[:, at] = both[:4, :XW]
        bias_o[:, at] = both[4:5, :XW]
        gate_o[:, at] = both[5:6, :XW]
        shared = shared + both
        for p in range(3):
            move = ((c - HG * g == r - HP * p) & (r >= HP * p) & (r < HP * p + HG)).astype(BF)
            heads[p] = heads[p] + mm(tail[:, XW : XW + 128].astype(BF), move)
    xbc_o[:, DI:] = bc
    dt_o[...] = dt[:, :H]
    taps_o[:, DI:] = shared[:4, XW:CW]
    bias_o[:, DI:] = shared[4:5, XW:CW]
    norm_o[:, :AW] = shared[6:7, :]
    norm_o[:, AW:] = shared[7:8, : norm_o.shape[1] - AW]
    for p, ref in enumerate((h0_o, h1_o, h2_o)):
        ref[...] = heads[p][5:6, :H] + heads[p][13:14, :H]


def last_outputs(x_all, own, width):
    sd = jax.ShapeDtypeStruct
    vm = pl.BlockSpec(memory_space=pltpu.VMEM)
    shapes = [(own, DI + 2 * N), (own, H), (4, DI + 2 * N), (1, DI + 2 * N), (1, DI), (1, width)]
    shapes.extend([(1, H)] * 3)
    return pl.pallas_call(
        last_kernel,
        out_shape=[sd(shape, F4) for shape in shapes],
        in_specs=[vm],
        out_specs=[vm] * len(shapes),
        compiler_params=pltpu.CompilerParams(vmem_limit_bytes=LIMIT),
        name="last_outputs",
    )(x_all)


def down_kernel(a, w, base, n, o, dots):
    v = mm_nt(a[...], w[...]) + base[...].astype(F4)
    o[...] = v.astype(BF)
    dots[...] = jnp.sum(v * n[...].astype(F4), axis=0, keepdims=True)


def down(a, w, base, normed):
    length, inner = a.shape
    width = w.shape[0]
    cols = 256
    return pl.pallas_call(
        down_kernel,
        grid=(width // cols,),
        in_specs=[
            fixed(length, inner),
            ahead(cols, inner),
            pl.BlockSpec((length, cols), lambda i: (0, i)),
            pl.BlockSpec((length, cols), lambda i: (0, i)),
        ],
        out_specs=[
            pl.BlockSpec((length, cols), lambda i: (0, i)),
            pl.BlockSpec((1, cols), lambda i: (0, i)),
        ],
        out_shape=[
            jax.ShapeDtypeStruct((length, width), BF),
            jax.ShapeDtypeStruct((1, width), F4),
        ],
        compiler_params=pltpu.CompilerParams(vmem_limit_bytes=LIMIT),
        name="down_proj",
    )(a, w, base, normed)


def pad_lanes(v, width):
    return jnp.pad(v, [(0, 0)] * (v.ndim - 1) + [(0, width - v.shape[-1])])


def carried(state, decay, hops, by):
    total = shift(state, CHAIN, by)
    if hops == 1:
        return total
    total, product = total.astype(F4), 1.0
    for j in range(2, hops + 1):
        product = product * shift(decay, CHAIN, by * (j - 1))
        total = total + product * shift(state, CHAIN, by * j).astype(F4)
    return total.astype(BF)


def shards(
    tokens_in, seg_ids, in_norm, z_proj, xbc_proj, dt_proj, conv_taps, conv_bias,
    dt_bias, a_log, d_skip, gate_norm, out_proj, out_cotangent,
):
    seqs, rows, width = tokens_in.shape
    length = seg_ids.shape[1]
    block = rows * GROUP
    n_blocks = length // block
    hops = min(-(-(length // 4 - 1) // block), n_blocks - 1)
    n_sums = lax.axis_size("dp") * n_blocks
    hl = lax.axis_index("hl")
    own_rows = z_proj.shape[0]

    def collected(part):
        return lax.all_gather(part, "hl", axis=0).reshape(GROUP * seqs * rows, width)

    def quarters(w):
        return w.reshape(w.shape[0], GROUP, -1).transpose(1, 0, 2)

    bc_cols = jnp.broadcast_to(xbc_proj[None, :, DI:], (GROUP, own_rows, 2 * N))
    parts = [quarters(xbc_proj[:, :DI]), bc_cols, pad_lanes(quarters(dt_proj), 128), quarters(z_proj)]
    parts = jnp.concatenate(parts, axis=-1)
    if plain():
        def part_of(k):
            return lax.dynamic_index_in_dim(parts, jnp.bitwise_xor(hl, k), 0, keepdims=False)

        near_parts = [part_of(0)] + [swap(part_of(k), "hl", k) for k in (3, 2, 1)][::-1]
        in_mine = placed(hl.astype(jnp.int32).reshape(1), near_parts)
    else:
        in_mine = lax.all_to_all(parts, "hl", 0, 0, tiled=True)
        in_mine = in_mine.reshape(GROUP * own_rows, AW + XW)
    pairs = [(f, (f % n_sums) * GROUP + f // n_sums) for f in range(GROUP * n_sums)]
    wo_mine = lax.ppermute(out_proj, EVERY, pairs)
    in_mine, wo_mine, tokens_now = lax.optimization_barrier((in_mine, wo_mine, tokens_in))
    tokens = collected(tokens_now)
    cot = collected(out_cotangent)
    wx, wz = all_rows(near_rows(in_mine), [(0, AW), (AW, AW + XW)])
    wx, wz, wo_mine = lax.optimization_barrier((wx, wz, wo_mine))
    wo_near = near_rows(wo_mine)

    def mine(v, size):
        return lax.dynamic_slice_in_dim(v, hl * size, size, axis=-1)

    taps = jnp.concatenate([conv_taps, conv_bias[None]], axis=0)
    taps = jnp.concatenate([mine(taps[:, :DI], XW), taps[:, DI:]], axis=1)
    taps = jnp.pad(taps, ((0, 3), (0, 0)))
    hp = jnp.stack([mine(dt_bias, HG), -jnp.exp(mine(a_log, HG))])
    hp = jnp.broadcast_to(jnp.pad(hp, ((0, 0), (0, HP - HG)))[:, :, None], (2, HP, 128))
    skip = jnp.repeat(mine(d_skip, HG), PS)[None]
    gain = mine(gate_norm, XW)[None]
    e = (jnp.arange(128)[:, None] == jnp.arange(XW)[None, :] // PS).astype(BF)

    start = lax.axis_index(CHAIN) * block
    seg_pad = jnp.concatenate([jnp.full((seqs, 8), -1, jnp.int32), seg_ids], axis=1)
    near = lax.dynamic_slice_in_dim(seg_pad, start, block + 8, axis=1)
    seg = near[:, 8:].reshape(seqs, GROUP, QC)
    lines = [seg, jnp.broadcast_to(near[:, 7 : 7 + block : QC][:, :, None], seg.shape)]
    lines.append(jnp.broadcast_to(seg[:, :, QC - 1 :], seg.shape))
    for k in range(KW - 1):
        lines.append((near[:, 5 + k : 5 + k + block].reshape(seg.shape) == seg).astype(jnp.int32))
    lines.extend([jnp.zeros_like(seg)] * 2)
    meta = jnp.stack(lines, axis=2).astype(F4)
    meta = meta.transpose(1, 0, 2, 3).reshape(GROUP * seqs, 8, QC)

    tokens, wx, wz, meta, taps, hp, skip, gain, e = lax.optimization_barrier(
        (tokens, wx, wz, meta, taps, hp, skip, gain, e)
    )
    normed = norm_rows(tokens.astype(F4), in_norm).astype(BF)
    raw = mm(normed, wx).astype(BF)
    raw, *wo_near = lax.optimization_barrier((raw, *wo_near))
    [wo] = all_rows(wo_near, [(0, width)])
    last = raw.reshape(GROUP, seqs, rows, AW)[GROUP - 1, :, rows - 8 :, :CW]
    halo = shift(last, CHAIN, 1)
    x, bc, sl, sc, state, decay = front(seqs, raw, halo, meta, taps, hp, e)
    decay_row = jnp.repeat(decay[:, :HG, 0], PS, axis=-1)[:, None]
    state, z_normed = lax.optimization_barrier((state, normed))
    s_in = carried(state, decay_row, hops, 1)
    gates = mm(z_normed, wz)
    s_in, wo = lax.optimization_barrier((s_in, wo))
    y, sg, ent, squares = scan(seqs, x, bc, sc, meta, s_in, gates, skip, gain, e)

    def team_sum(part):
        total = part
        for k in range(1, GROUP):
            total = total + swap(part, "hl", k)
        return total

    def spread_sum(part):
        total = lax.psum_scatter(part, "hl", scatter_dimension=0, tiled=True)
        return total.reshape(seqs, rows, width)

    out_rows = mm(sg, wo).astype(BF)
    squares = team_sum(squares)
    cot, out_rows, squares = lax.optimization_barrier((cot, out_rows, squares))
    d_gated = mm_nt(cot, wo)
    row_scale = lax.rsqrt(squares * (1.0 / DI) + EPS)
    gated = (sg.astype(F4) * row_scale.reshape(-1, 1)).astype(BF)
    along = team_sum(jnp.sum(d_gated * sg.astype(F4), axis=1).reshape(squares.shape))
    out_sum = spread_sum(out_rows)
    dp = lax.axis_index("dp")
    if plain():
        o_give, o_keep = (mm_tn(half_of(gated, at), cot).astype(BF) for at in (1 - dp, dp))
    dy, dz, gg, d_state = gate(seqs, y, gates, d_gated, squares, along, bc, sc, meta, gain, e)
    d_end = carried(d_state, decay_row, hops, -1)
    if plain():
        n_give, n_keep = (half_of(normed, at) for at in (1 - dp, dp))
        z_give, z_keep = (mm_tn(v, dz).astype(BF) for v in (n_give, n_keep))
        dy, z_give, z_keep = lax.optimization_barrier((dy, z_give, z_keep))
        z_got, o_got = swap(z_give, "dp", 1), swap(o_give, "dp", 1)
        early = []
        for z_part, o_part in zip(chain_pieces(z_keep, z_got), chain_pieces(o_keep, o_got)):
            early.append(jnp.concatenate([z_part, o_part[:, : width // 2], o_part[:, width // 2 :]]))
        dy, *early = lax.optimization_barrier((dy, *early))
        early = chain_sum(early)
    draw, rim, conv_total, head_total = scan_back(
        seqs, x, bc, sl, sc, meta, ent, dy, d_end, raw, halo, taps, hp, skip, e
    )
    rim = shift(rim, CHAIN, -1)
    from_z = mm_nt(dz, wz).astype(BF)
    if plain():
        rim, from_z, out_sum, early = lax.optimization_barrier((rim, from_z, out_sum, early))
    draw = draw.reshape(GROUP, seqs, rows, AW)
    edge = draw[GROUP - 1 :, :, rows - 8 :, :CW].astype(F4) + rim.astype(F4)
    draw = lax.dynamic_update_slice(draw, edge.astype(BF), (GROUP - 1, 0, rows - 8, 0))
    draw = draw.reshape(GROUP * seqs * rows, AW)

    if plain():
        z_rows = GROUP * own_rows
        o_rows = (early.shape[0] - z_rows) // 2
        z_own = early[:z_rows].reshape(GROUP, own_rows, XW)
        o_own = jnp.concatenate([early[z_rows : z_rows + o_rows], early[z_rows + o_rows :]], axis=1)
        o_back = lax.ppermute(o_own, EVERY, [(b, a) for a, b in pairs])
        z_all = lax.all_to_all(z_own, "hl", 0, 0, tiled=True)
        d_low, norm_total = down(draw, wx, from_z, normed)
        d_low, draw, z_all, o_back = lax.optimization_barrier((d_low, draw, z_all, o_back))
        out_proj_grad = o_back.astype(F4)
        x_give = mm_tn(n_give, draw).astype(BF)
        x_give, draw = lax.optimization_barrier((x_give, draw))
        x_got = swap(x_give, "dp", 1)
        x_keep = mm_tn(n_keep, draw).astype(BF)
        x_pieces = chain_pieces(x_keep, x_got)
        x_own = chain_sum(x_pieces)
    else:
        grads = [mm_tn(normed, dz), mm_tn(gated, cot), mm_tn(normed, draw)]
        grads = [g.astype(BF) for g in grads]
        d_low, norm_total = down(draw, wx, from_z, normed)
        z_own, o_own, x_own = (
            lax.psum_scatter(g, SUMS, scatter_dimension=0, tiled=True) for g in grads
        )
    d_sum = spread_sum(d_low)
    if not plain():
        out_proj_grad = lax.ppermute(o_own, EVERY, [(b, a) for a, b in pairs]).astype(F4)

    heads = jnp.sum(head_total, axis=2).reshape(1, -1)
    norm_grad = norm_total / in_norm[None]
    pack = jnp.concatenate(
        [
            pad_lanes(conv_total[:5], AW),
            pad_lanes(jnp.concatenate([gg[:1], heads], axis=1), AW),
            norm_grad[:, :AW],
            pad_lanes(norm_grad[:, AW:], AW),
        ],
        axis=0,
    )
    for axis in SUMS:
        pack = pack + sum(swap(pack, axis, k) for k in range(1, lax.axis_size(axis)))
    high = pack.astype(BF)
    small = jnp.concatenate([high, (pack - high.astype(F4)).astype(BF)], axis=0)
    small = jnp.broadcast_to(small[None], (GROUP, 16, AW))
    x_own = jnp.concatenate([x_own.reshape(GROUP, own_rows, AW), small], axis=1)
    if not plain():
        z_all = lax.all_to_all(z_own.reshape(GROUP, own_rows, XW), "hl", 0, 0, tiled=True)
    x_all = lax.all_to_all(x_own, "hl", 0, 0, tiled=True)

    u = tokens_in.astype(F4)
    scale = lax.rsqrt(jnp.mean(u * u, axis=-1, keepdims=True) + EPS)
    hat = u * scale
    dh = d_sum.astype(F4) * in_norm
    along = jnp.mean(dh * hat, axis=-1, keepdims=True)
    own_scale = lax.dynamic_index_in_dim(row_scale.reshape(GROUP, seqs, rows, 1), hl, 0, keepdims=False)
    layer_out = (tokens_in.astype(F4) + own_scale * out_sum.astype(F4)).astype(BF)
    z_proj_grad = z_all.transpose(1, 0, 2).reshape(own_rows, DI).astype(F4)
    if plain():
        outs = last_outputs(x_all, own_rows, width)
        xbc_proj_grad, dt_proj_grad, taps_grad = outs[:3]
        bias_grad, gate_grad, in_norm_grad = (v.reshape(-1) for v in outs[3:6])
        per_head = [v.reshape(-1) for v in outs[6:]]
    else:
        x_parts = x_all[:, :own_rows]
        xs = x_parts[:, :, :XW].transpose(1, 0, 2).reshape(own_rows, DI).astype(F4)
        bc_grad = jnp.sum(x_parts[:, :, XW:CW].astype(F4), axis=0)
        xbc_proj_grad = jnp.concatenate([xs, bc_grad], axis=1)
        dt_parts = x_parts[:, :, CW : CW + HG].transpose(1, 0, 2)
        dt_proj_grad = dt_parts.reshape(own_rows, H).astype(F4)
        got = x_all[:, own_rows:, :AW].astype(F4)
        got = got[:, :8] + got[:, 8:]
        conv_x = got[:, :5, :XW].transpose(1, 0, 2).reshape(5, DI)
        conv_all = jnp.concatenate([conv_x, jnp.sum(got[:, :5, XW:CW], axis=0)], axis=1)
        per_head = got[:, 5, XW : XW + 3 * HP].reshape(GROUP, 3, HP)[:, :, :HG]
        per_head = per_head.transpose(1, 0, 2).reshape(3, H)
        in_norm_grad = jnp.sum(got[:, 6:8], axis=0).reshape(-1)[:width]
        taps_grad, bias_grad, gate_grad = conv_all[:4], conv_all[4], got[:, 5, :XW].reshape(DI)
    in_norm_grad, along = lax.optimization_barrier((in_norm_grad, along))
    d_u = scale * (dh - hat * along)
    tokens_grad = d_u + out_cotangent.astype(F4)
    return (
        layer_out,
        tokens_grad,
        in_norm_grad,
        z_proj_grad,
        xbc_proj_grad,
        dt_proj_grad,
        taps_grad,
        bias_grad,
        per_head[0],
        per_head[1],
        per_head[2],
        gate_grad,
        out_proj_grad,
    )


def solution(mesh):
    sizes = dict(mesh.shape)
    grid = mesh.devices.reshape(sizes["dp"], sizes["ctx"], sizes["hd"] // GROUP, GROUP)
    fine = Mesh(grid, ("dp", "ctx", "hh", "hl"))
    tok = P("dp", ("ctx", "hh", "hl"), None)
    wgt = P(("dp", "ctx", "hh", "hl"), None)
    in_specs = (tok, P("dp", None), P(), wgt, wgt, wgt, P(), P(), P(), P(), P(), P(), wgt, tok)
    out_specs = (tok, tok, P(), wgt, wgt, wgt, P(), P(), P(), P(), P(), P(), wgt)
    return jax.shard_map(shards, mesh=fine, in_specs=in_specs, out_specs=out_specs, check_vma=False)
```
